32 devices in a mesh: img: 4 (over y, core), pix: 8 (over z, x).
Axes of the slice: x: 2, y: 2, z: 4, core: 2. Of those that a mesh axis runs over, the one named last changes fastest.
Arguments:
- pixels: float32 [2, 4, 82944, 261], P(None, 'img', 'pix'), may hold values from -6 to 6
- sides: int32 [2], replicated, may hold values from 160 to 288, as said below
- owner: int32 [256], replicated, may hold values from 0 to 255, each once
- master: float32 [256, 128, 128], P(('img', 'pix')), may hold values from -0.375 to 0.375
- left_stat: float32 [256, 128, 128], P(('img', 'pix'))
- right_stat: float32 [256, 128, 128], P(('img', 'pix'))
- left_root: float32 [256, 128, 128], P(('img', 'pix'))
- right_root: float32 [256, 128, 128], P(('img', 'pix'))
- kv_weight: float32 [2, 261, 1024], replicated, may hold values from -0.375 to 0.375
- latent_array: float32 [512, 1024], replicated, may hold values from -6 to 6
- in_gain: float32 [261], replicated, may hold values from 0.5 to 1.5
- lat_gains: float32 [2, 1024], replicated, may hold values from 0.5 to 1.5
- cotangent: float32 [2, 4, 512, 1024], P(None, 'img', 'pix'), may hold values from -6 to 6
Outputs:
- latents_out: float32 [2, 4, 512, 1024], P(None, 'img', 'pix')
- pixel_grad: float32 [2, 4, 82944, 261], P(None, 'img', 'pix')
- new_left: float32 [256, 128, 128], P(('img', 'pix'))
- new_right: float32 [256, 128, 128], P(('img', 'pix'))
- new_master: float32 [256, 128, 128], P(('img', 'pix'))
- new_copy: bfloat16 [256, 128, 128], P(('img', 'pix'))
- kv_grad: float32 [2, 261, 1024], replicated
- new_kv: float32 [2, 261, 1024], replicated
- latent_grad: float32 [512, 1024], replicated
- new_latent: float32 [512, 1024], replicated
- in_gain_grad: float32 [261], replicated
- new_in_gain: float32 [261], replicated
- lat_gain_grad: float32 [2, 1024], replicated
- new_lat_gains: float32 [2, 1024], replicated
The draws below stay inside these ranges and needn't reach their ends.
Inputs may be any that keep to these rules, and one draw needn't show every extreme that they name: Every image of micro-batch m is sides[m] pixels a side, one of 160, 224 or 288; some micro-batch has 288 and some has a smaller side. Slot p of an image (row by row) is a real pixel when p < sides[m]^2; the rest of the 82944 slots are padding. A permutation: block b lives in slot owner[b]; the slots run in order over the devices of img+pix, an equal number to each.
All inputs are finite; a program needn't handle non-finite values.
Results may differ from the reference program's by a relative error of at most 0.015.
The reference program's roundings to bfloat16 on the way count: a program that leaves them out, or rounds other values in their place, can miss the bound.
Values may be sent and summed in bfloat16 or wider, within the bound.
No kernel may reach another device: no remote copies, remote signals or barrier semaphores. Data moves between devices by JAX's collectives and lax.ppermute only.
A program may use at most 448 MiB of HBM per device.

```python
import math
import jax
import jax.numpy as jnp
from jax import lax

CIN = 261
DL = 1024
LAT = 512
SIDE = 288
BLK = 128
MB = 2
IMAGES = 4
PIXELS = 82944
NBLK = 256
N_PIX = 8


def draw_sides(key, part):
    picked = jax.random.randint(jax.random.fold_in(key, 11), (MB,), 0, 3)
    ninths = jnp.array([5, 7, 9], jnp.int32)[picked]
    place = jax.random.randint(jax.random.fold_in(key, 12), (), 0, MB)
    lesser = jax.random.randint(jax.random.fold_in(key, 13), (), 0, 2)
    ninths = ninths.at[place].set(9)
    ninths = ninths.at[(place + 1) % MB].set(jnp.array([5, 7], jnp.int32)[lesser])
    return (SIDE * ninths // 9).astype(jnp.int32)


def block_matrices(key, level, spread_log):
    noise_key = jax.random.fold_in(key, 21)
    factor_key = jax.random.fold_in(key, 22)
    noise = jax.random.normal(noise_key, (NBLK, BLK, BLK), jnp.float32)
    factor = jnp.exp(jax.random.uniform(factor_key, (NBLK, 1, 1), jnp.float32, 0.0, spread_log))
    identity = jnp.eye(BLK, dtype=jnp.float32)
    return level * factor * (identity + 0.5 / BLK * (noise + jnp.swapaxes(noise, 1, 2)))


def stat_level():
    return float(BLK) * float(MB) * float(IMAGES) * float(LAT)


def draw_left_stat(key, part):
    return block_matrices(jax.random.fold_in(key, 1), stat_level(), math.log(4.0))


def draw_right_stat(key, part):
    return block_matrices(jax.random.fold_in(key, 2), stat_level(), math.log(4.0))


def draw_left_root(key, part):
    return block_matrices(jax.random.fold_in(key, 3), stat_level() ** (-0.25), math.log(2.0))


def draw_right_root(key, part):
    return block_matrices(jax.random.fold_in(key, 4), stat_level() ** (-0.25), math.log(2.0))


def level_of(rng, extent, split, smallest, high):
    level = 1.0
    for axis_at, shards_of in split:
        draws = jax.random.uniform(jax.random.fold_in(jax.random.fold_in(rng, 6), axis_at), (shards_of,), jnp.float32, smallest / len(split), high / len(split))
        level = level * jnp.repeat(jnp.exp(draws), extent[axis_at] // shards_of).reshape((-1,) + (1,) * (len(extent) - 1 - axis_at))
    return level


def bell_draw(key, dims, scale, bound, split=(), kind=jnp.bfloat16):
    values = scale * jax.random.normal(key, dims, jnp.float32)
    if split:
        values = values * level_of(key, dims, split, -0.22, 0.18)
    return jnp.clip(values, -bound, bound).astype(kind)


def setup_inputs(seed: int = 0) -> dict:
    streams_of = jax.random.split(jax.random.key(seed), 14)
    pixels = bell_draw(streams_of[0], (MB, IMAGES, PIXELS, CIN), 1.0, 6.0, ((1, 4), (2, 8)), jnp.float32)
    sides = draw_sides(jax.random.fold_in(streams_of[13], 71), 0)
    owner = jax.random.permutation(streams_of[2], NBLK).astype(jnp.int32)
    master = bell_draw(streams_of[3], (NBLK, BLK, BLK), (DL // 4) ** -0.5, 0.375, ((0, 32),), jnp.float32)
    left_stat = draw_left_stat(jax.random.fold_in(streams_of[13], 71), 0)
    right_stat = draw_right_stat(jax.random.fold_in(streams_of[13], 71), 0)
    left_root = draw_left_root(jax.random.fold_in(streams_of[13], 71), 0)
    right_root = draw_right_root(jax.random.fold_in(streams_of[13], 71), 0)
    kv_weight = bell_draw(streams_of[8], (2, CIN, DL), CIN ** -0.5, 0.375, (), jnp.float32)
    latent_array = bell_draw(streams_of[9], (LAT, DL), 1.0, 6.0, (), jnp.float32)
    in_gain = jnp.clip(1.0 + 0.1 * jax.random.normal(streams_of[10], (CIN,), jnp.float32), 0.5, 1.5)
    lat_gains = jnp.clip(1.0 + 0.1 * jax.random.normal(streams_of[11], (2, DL), jnp.float32), 0.5, 1.5)
    cotangent = bell_draw(streams_of[12], (MB, IMAGES, LAT, DL), 1.0, 6.0, ((1, 4), (2, 8)), jnp.float32)
    return {"pixels": pixels, "sides": sides, "owner": owner, "master": master, "left_stat": left_stat, "right_stat": right_stat, "left_root": left_root, "right_root": right_root, "kv_weight": kv_weight, "latent_array": latent_array, "in_gain": in_gain, "lat_gains": lat_gains, "cotangent": cotangent}


@jax.custom_vjp
def low(v):
    return lax.optimization_barrier(v.astype(jnp.bfloat16)).astype(jnp.float32)

@jax.custom_vjp
def low_back(v):
    return v

def low_keep(v):
    return (low(v), None)

def low_pass(kept, grad):
    return (grad,)

def back_keep(v):
    return (v, None)

def back_low(kept, grad):
    return (low(grad),)
low.defvjp(low_keep, low_pass)
low_back.defvjp(back_keep, back_low)
HIGHEST_PRECISION = lax.Precision.HIGHEST

def matmul(left_side, right_side):
    return jnp.dot(left_side, right_side, precision=HIGHEST_PRECISION)

def standardize(values_in):
    average = lax.optimization_barrier(jnp.mean(values_in, axis=-1, keepdims=True))
    centred = values_in - average
    variance = lax.optimization_barrier(jnp.mean(centred * centred, axis=-1, keepdims=True))
    return centred * lax.rsqrt(variance + 1e-05)

def layer_norm(values_in, gain_row):
    return standardize(values_in) * gain_row

def unblock(blocks):
    per_side = DL // BLK
    return blocks.reshape(4, per_side, per_side, BLK, BLK).transpose(0, 1, 3, 2, 4).reshape(4, DL, DL)

def to_blocks(matrices):
    per_side = DL // BLK
    return matrices.reshape(4, per_side, BLK, per_side, BLK).transpose(0, 1, 3, 2, 4).reshape(NBLK, BLK, BLK)

def normalized(gradient, reduce_axes):
    return gradient / jnp.sqrt(lax.optimization_barrier(jnp.mean(gradient * gradient, axis=reduce_axes, keepdims=True)) + 1e-06)

def forward(pixels, latent_array, in_gain, lat_gains, square, kv_weight, counts):
    w_query = low(square[0])
    w_out = low(square[1])
    w_up = low(square[2])
    w_down = low(square[3])
    w_key = low(kv_weight[0])
    w_value = low(kv_weight[1])
    inv_root = 1.0 / math.sqrt(DL)
    lat_norm = layer_norm(latent_array, lat_gains[0])
    query = low(low_back(matmul(low(lat_norm), w_query)))
    rows_blk = PIXELS // N_PIX

    def one_image(image_pixels, count):
        blocks = image_pixels.reshape(N_PIX, rows_blk, CIN)
        starts = jnp.arange(N_PIX, dtype=jnp.int32) * rows_blk

        def block_fn(carry, inputs):
            x_blk, start = inputs
            numerator, denominator = carry
            normed = low(layer_norm(x_blk, in_gain))
            keys = low(low_back(matmul(normed, w_key)))
            values = low(low_back(matmul(normed, w_value)))
            scores = low_back(matmul(query, keys.T) * inv_root)
            valid = start + jnp.arange(rows_blk, dtype=jnp.int32) < count
            weights_exp = jnp.where(valid[None, :], jnp.exp(scores), 0.0)
            return ((numerator + matmul(low(weights_exp), values), denominator + lax.optimization_barrier(jnp.sum(weights_exp, axis=1))), None)
        init = (jnp.zeros((LAT, DL), jnp.float32), jnp.zeros((LAT,), jnp.float32))
        (numerator, denominator), _ = lax.scan(jax.checkpoint(block_fn), init, (blocks, starts))
        numerator = low_back(numerator)
        attended = numerator / denominator[:, None]
        resid = latent_array + low_back(matmul(low(attended), w_out))
        hidden = low_back(matmul(low(layer_norm(resid, lat_gains[1])), w_up))
        mlp_out = low_back(matmul(low(jax.nn.gelu(hidden, approximate=False)), w_down))
        return resid + mlp_out
    flat = pixels.reshape(MB * IMAGES, PIXELS, CIN)
    checked = jax.checkpoint(lambda item: one_image(item[0], item[1]))
    outputs = lax.map(checked, (flat, counts))
    return outputs.reshape(MB, IMAGES, LAT, DL)

def reference(pixels, sides, owner, master, left_stat, right_stat, left_root, right_root, kv_weight, latent_array, in_gain, lat_gains, cotangent):
    square = unblock(master[owner])
    counts = jnp.repeat(sides * sides, IMAGES).astype(jnp.int32)

    def wrapped(pix_in, lat_in, gain_in, gains_lat, square_in, kv_in):
        return forward(pix_in, lat_in, gain_in, gains_lat, square_in, kv_in, counts)
    latents_out, pullback = jax.vjp(wrapped, pixels, latent_array, in_gain, lat_gains, square, kv_weight)
    pixel_grad, latent_grad, in_gain_grad, lat_gain_grad, square_grad, kv_grad = pullback(cotangent)
    grads = jnp.zeros((NBLK, BLK, BLK), jnp.float32).at[owner].set(to_blocks(square_grad))
    new_left = 0.5 * left_stat + 0.5 * jnp.einsum('bij,bkj->bik', grads, grads, precision=HIGHEST_PRECISION)
    new_right = 0.5 * right_stat + 0.5 * jnp.einsum('bji,bjk->bik', grads, grads, precision=HIGHEST_PRECISION)
    half_step = jnp.einsum('bij,bjk->bik', left_root, grads, precision=HIGHEST_PRECISION)
    shampoo = jnp.einsum('bij,bjk->bik', half_step, right_root, precision=HIGHEST_PRECISION)
    new_master = master - 0.5 / math.sqrt(DL) * normalized(shampoo, (1, 2))
    new_copy = new_master.astype(jnp.bfloat16)
    new_kv = kv_weight - 0.3 / math.sqrt(CIN) * normalized(kv_grad, (1, 2))
    new_latent = latent_array - 0.3 * normalized(latent_grad, (0, 1))
    new_in_gain = in_gain - 0.2 * normalized(in_gain_grad, (0,))
    new_lat_gains = lat_gains - 0.2 * normalized(lat_gain_grad, (1,))
    return (latents_out, pixel_grad, new_left, new_right, new_master, new_copy, kv_grad, new_kv, latent_grad, new_latent, in_gain_grad, new_in_gain, lat_gain_grad, new_lat_gains)
```

```python
import math

import jax
import jax.numpy as jnp
from jax import lax
from jax.sharding import PartitionSpec as P

CIN = 261
DL = 1024
LAT = 512
BLK = 128
NBLK = 256


HIGHEST_PRECISION = lax.Precision.HIGHEST


def standardize(values_in):
    average = jnp.mean(values_in, axis=-1, keepdims=True)
    centred = values_in - average
    variance = jnp.mean(centred * centred, axis=-1, keepdims=True)
    return centred * lax.rsqrt(variance + 1e-05)


def gelu_exact(values_in):
    return jax.nn.gelu(values_in, approximate=False)


def unblock(blocks, full_width, block_size):
    per_side = full_width // block_size
    return (
        blocks.reshape(4, per_side, per_side, block_size, block_size)
        .transpose(0, 1, 3, 2, 4)
        .reshape(4, full_width, full_width)
    )


def to_blocks(matrices, full_width, block_size):
    per_side = full_width // block_size
    return (
        matrices.reshape(4, per_side, block_size, per_side, block_size)
        .transpose(0, 1, 3, 2, 4)
        .reshape(4 * per_side * per_side, block_size, block_size)
    )


def normalized(gradient, reduce_axes):
    return gradient / jnp.sqrt(
        jnp.mean(gradient * gradient, axis=reduce_axes, keepdims=True) + 1e-06
    )


def product(pattern, left_side, right_side):
    return jnp.einsum(pattern, left_side, right_side, preferred_element_type=jnp.float32)


def latent_pass(numerator, denominator, lat_part, cot_rows, lat_gain, w_out, w_up, w_down):
    attended = numerator / denominator[..., None]
    att_low = attended.astype(jnp.bfloat16)
    resid = lat_part[None] + product("mrd,de->mre", att_low, w_out)
    normed, normed_back = jax.vjp(standardize, resid)
    hn_low = (normed * lat_gain).astype(jnp.bfloat16)
    hidden = product("mrd,de->mre", hn_low, w_up)
    active, active_back = jax.vjp(gelu_exact, hidden)
    act_low = active.astype(jnp.bfloat16)
    latents_out = resid + product("mrd,de->mre", act_low, w_down)
    g_mlp = cot_rows.astype(jnp.bfloat16)
    d_active = product("mre,de->mrd", g_mlp, w_down)
    d_hidden = active_back(d_active)[0].astype(jnp.bfloat16)
    d_normed = product("mre,de->mrd", d_hidden, w_up)
    d_resid = cot_rows + normed_back(d_normed * lat_gain)[0]
    d_branch = d_resid.astype(jnp.bfloat16)
    d_attended = product("mre,de->mrd", d_branch, w_out)
    d_numer = d_attended / denominator[..., None]
    d_denom = -jnp.sum(d_attended * numerator / (denominator * denominator)[..., None], axis=-1)
    row_pairs = (att_low, d_branch, hn_low, d_hidden, act_low, g_mlp)
    gain_mlp = jnp.sum(d_normed * normed, axis=(0, 1))
    lat_resid = jnp.sum(d_resid, axis=0)
    return (latents_out, d_numer.astype(jnp.bfloat16), d_denom, (row_pairs, gain_mlp, lat_resid))


def fine(pattern, left_side, right_side):
    return jnp.einsum(
        pattern,
        left_side.astype(jnp.float32),
        right_side.astype(jnp.float32),
        precision=HIGHEST_PRECISION,
    )


def shards(
    pixels,
    sides,
    owner,
    master,
    left_stat,
    right_stat,
    left_root,
    right_root,
    kv_weight,
    latent_array,
    in_gain,
    lat_gains,
    cotangent,
):
    micro = pixels.shape[0]
    rows_dev = pixels.shape[2]
    lat_rows = LAT // lax.axis_size("pix")
    pix_start = lax.axis_index("pix") * rows_dev
    row_start = lax.axis_index("pix") * lat_rows
    inv_root = 1.0 / math.sqrt(DL)
    gathered = lax.all_gather(master.astype(jnp.bfloat16), ("img", "pix"), axis=0, tiled=True)
    square = unblock(jnp.take(gathered, owner, axis=0), DL, BLK)
    w_query, w_out, w_up, w_down = (square[0], square[1], square[2], square[3])
    kv_low = kv_weight.astype(jnp.bfloat16)
    w_key, w_value = (kv_low[0], kv_low[1])
    lat_norm, lat_norm_back = jax.vjp(standardize, latent_array)
    lat_low = (lat_norm * lat_gains[0]).astype(jnp.bfloat16)
    query = jnp.dot(lat_low, w_query, preferred_element_type=jnp.float32).astype(jnp.bfloat16)
    query_in = (product("ld,cd->lc", query, w_key) * inv_root).astype(jnp.bfloat16)
    positions = pix_start + jnp.arange(rows_dev, dtype=jnp.int32)
    stored = []
    numer_list = []
    denom_list = []
    for micro_index in range(micro):
        pix_std, pix_back = jax.vjp(standardize, pixels[micro_index, 0])
        pix_low = (pix_std * in_gain).astype(jnp.bfloat16)
        valid = positions < sides[micro_index] * sides[micro_index]
        scores = product("lc,pc->lp", query_in, pix_low)
        weights_exp = jnp.where(valid[None, :], jnp.exp(scores), 0.0)
        numer_list.append(product("lp,pc->lc", weights_exp.astype(jnp.bfloat16), pix_low))
        denom_list.append(jnp.sum(weights_exp, axis=1))
        stored.append((pix_std, pix_back, pix_low, valid))
    numer_in = lax.psum_scatter(jnp.stack(numer_list), "pix", scatter_dimension=1, tiled=True)
    denominator = lax.psum_scatter(jnp.stack(denom_list), "pix", scatter_dimension=1, tiled=True)
    numerator = fine("mlc,cd->mld", numer_in, w_value)
    latents_out, d_numer, d_denom, latent_grads = latent_pass(
        numerator,
        denominator,
        lax.dynamic_slice_in_dim(latent_array, row_start, lat_rows, 0),
        cotangent[:, 0],
        lat_gains[1],
        w_out,
        w_up,
        w_down,
    )
    row_pairs, gain_mlp, lat_resid = latent_grads
    value_grad = fine("mlc,mld->cd", numer_in, d_numer)
    d_numer_in = product("mld,cd->mlc", d_numer, w_value).astype(jnp.bfloat16)
    d_numer_all = lax.all_gather(d_numer_in, "pix", axis=1, tiled=True)
    d_denom_all = lax.all_gather(d_denom, "pix", axis=1, tiled=True)
    score_sum = jnp.zeros((LAT, CIN), jnp.float32)
    gain_input = jnp.zeros((CIN,), jnp.float32)
    pixel_list = []
    for micro_index in range(micro):
        pix_std, pix_back, pix_low, valid = stored[micro_index]
        scores = product("lc,pc->lp", query_in, pix_low)
        weights_exp = jnp.where(valid[None, :], jnp.exp(scores), 0.0)
        d_exp = product("lc,pc->lp", d_numer_all[micro_index], pix_low) + d_denom_all[micro_index][:, None]
        d_scores = (weights_exp * d_exp).astype(jnp.bfloat16)
        score_sum = score_sum + product("lp,pc->lc", d_scores, pix_low)
        d_pix_norm = product("lp,lc->pc", d_scores, query_in) + product(
            "lp,lc->pc", weights_exp.astype(jnp.bfloat16), d_numer_all[micro_index]
        )
        pixel_list.append(pix_back(d_pix_norm * in_gain)[0])
        gain_input = gain_input + jnp.sum(d_pix_norm * pix_std, axis=0)
    pixel_grad = jnp.stack(pixel_list)[:, None]
    lat_resid_full = lax.dynamic_update_slice_in_dim(
        jnp.zeros((LAT, DL), jnp.float32), lat_resid, row_start, 0
    )
    score_total, resid_total, value_total, in_gain_grad, gain_mlp_total = lax.psum(
        (score_sum, lat_resid_full, value_grad, gain_input, gain_mlp),
        ("img", "pix"),
    )
    d_query = (fine("lc,cd->ld", score_total, w_key) * inv_root).astype(jnp.bfloat16)
    key_total = fine("lc,ld->cd", score_total, query) * inv_root
    kv_grad = jnp.stack([key_total, value_total])
    d_lat_norm = product("le,de->ld", d_query, w_query)
    latent_grad = resid_total + lat_norm_back(d_lat_norm * lat_gains[0])[0]
    lat_gain_grad = jnp.stack([jnp.sum(d_lat_norm * lat_norm, axis=0), gain_mlp_total])
    att_rows, branch_rows, hn_rows, hid_rows, act_rows, mlp_rows = row_pairs

    def own_product(left_rows, right_rows):
        return product("mrd,mre->de", left_rows, right_rows)

    grad_query = product("ld,le->de", lat_low, d_query)
    leader = (lax.axis_index(("img", "pix")) == 0).astype(jnp.float32)
    matrices = jnp.stack(
        [
            grad_query * leader,
            own_product(att_rows, branch_rows),
            own_product(hn_rows, hid_rows),
            own_product(act_rows, mlp_rows),
        ]
    )
    buffer = jnp.zeros((NBLK, BLK, BLK), jnp.float32).at[owner].set(to_blocks(matrices, DL, BLK))
    reduced = lax.psum_scatter(buffer, ("img", "pix"), scatter_dimension=0, tiled=True)
    new_left = 0.5 * left_stat + 0.5 * jnp.einsum(
        "bij,bkj->bik", reduced, reduced, precision=HIGHEST_PRECISION
    )
    new_right = 0.5 * right_stat + 0.5 * jnp.einsum(
        "bji,bjk->bik", reduced, reduced, precision=HIGHEST_PRECISION
    )
    half_step = jnp.einsum("bij,bjk->bik", left_root, reduced, precision=HIGHEST_PRECISION)
    shampoo = jnp.einsum("bij,bjk->bik", half_step, right_root, precision=HIGHEST_PRECISION)
    new_master = master - 0.5 / math.sqrt(DL) * normalized(shampoo, (1, 2))
    new_copy = new_master.astype(jnp.bfloat16)
    new_kv = kv_weight - 0.3 / math.sqrt(CIN) * normalized(kv_grad, (1, 2))
    new_latent = latent_array - 0.3 * normalized(latent_grad, (0, 1))
    new_in_gain = in_gain - 0.2 * normalized(in_gain_grad, (0,))
    new_lat_gains = lat_gains - 0.2 * normalized(lat_gain_grad, (1,))
    return (
        latents_out[:, None],
        pixel_grad,
        new_left,
        new_right,
        new_master,
        new_copy,
        kv_grad,
        new_kv,
        latent_grad,
        new_latent,
        in_gain_grad,
        new_in_gain,
        lat_gain_grad,
        new_lat_gains,
    )


def solution(mesh):
    in_specs = (
        P(None, "img", "pix", None),
        P(),
        P(),
        P(("img", "pix"), None, None),
        P(("img", "pix"), None, None),
        P(("img", "pix"), None, None),
        P(("img", "pix"), None, None),
        P(("img", "pix"), None, None),
        P(),
        P(),
        P(),
        P(),
        P(None, "img", "pix", None),
    )
    out_specs = (
        P(None, "img", "pix", None),
        P(None, "img", "pix", None),
        P(("img", "pix"), None, None),
        P(("img", "pix"), None, None),
        P(("img", "pix"), None, None),
        P(("img", "pix"), None, None),
        P(),
        P(),
        P(),
        P(),
        P(),
        P(),
        P(),
        P(),
    )
    return jax.shard_map(shards, mesh=mesh, in_specs=in_specs, out_specs=out_specs, check_vma=False)
```

```python
import math

import jax
import jax.numpy as jnp
from jax import lax
from jax.experimental import pallas as pl
from jax.experimental.pallas import tpu as pltpu
from jax.sharding import PartitionSpec as P

CIN = 261
DL = 1024
LAT = 512
BLK = 128
NBLK = 256
PER_MATRIX = NBLK // 4
CEXT = 264
ONES_ROW = 261
MASK_ROW = 263
MASKED = -1e30

HIGHEST_PRECISION = lax.Precision.HIGHEST


def standardize(values_in):
    average = jnp.mean(values_in, axis=-1, keepdims=True)
    centred = values_in - average
    variance = jnp.mean(centred * centred, axis=-1, keepdims=True)
    return centred * lax.rsqrt(variance + 1e-05)


def gelu_exact(values_in):
    return jax.nn.gelu(values_in, approximate=False)


def unblock(blocks, full_width, block_size):
    per_side = full_width // block_size
    return (
        blocks.reshape(4, per_side, per_side, block_size, block_size)
        .transpose(0, 1, 3, 2, 4)
        .reshape(4, full_width, full_width)
    )


def normalized(gradient, reduce_axes):
    return gradient / jnp.sqrt(
        jnp.mean(gradient * gradient, axis=reduce_axes, keepdims=True) + 1e-06
    )


def product(pattern, left_side, right_side):
    return jnp.einsum(pattern, left_side, right_side, preferred_element_type=jnp.float32)


def fine(pattern, left_side, right_side):
    return jnp.einsum(
        pattern,
        left_side.astype(jnp.float32),
        right_side.astype(jnp.float32),
        precision=HIGHEST_PRECISION,
    )


def two_terms(values_in):
    head = lax.reduce_precision(values_in, 8, 7)
    return (head.astype(jnp.bfloat16), (values_in - head).astype(jnp.bfloat16))


def contract_rows(left_side, right_side, precision=None):
    return lax.dot_general(
        left_side,
        right_side,
        (((0,), (0,)), ((), ())),
        precision=precision,
        preferred_element_type=jnp.float32,
    )


def dot(left_side, right_side):
    return jnp.dot(left_side, right_side, preferred_element_type=jnp.float32)


def tile_of(rows, most):
    return max(size for size in range(16, most + 1, 16) if rows % size == 0)


def prepare_body(place_ref, pix_ref, gain_ref, out_ref):
    micro_index = pl.program_id(0)
    rows = pix_ref.shape[2]
    normed = standardize(pix_ref[0, 0])
    out_ref[0, :, :CIN] = (normed * gain_ref[...]).astype(jnp.bfloat16)
    extra = (rows, CEXT - CIN)
    slot = place_ref[0] + pl.program_id(1) * rows + lax.broadcasted_iota(jnp.int32, extra, 0)
    column = lax.broadcasted_iota(jnp.int32, extra, 1) + CIN
    mask = jnp.where(slot < place_ref[1 + micro_index], 0.0, MASKED)
    out_ref[0, :, CIN:] = jnp.where(column == MASK_ROW, mask, 1.0).astype(jnp.bfloat16)


def prepare_pixels(place, pixels, in_gain):
    micro, _, rows_dev, _ = pixels.shape
    rows = tile_of(rows_dev, 1152)
    return pl.pallas_call(
        prepare_body,
        grid=(micro, rows_dev // rows),
        in_specs=[
            pl.BlockSpec(memory_space=pltpu.SMEM),
            pl.BlockSpec((1, 1, rows, CIN), lambda m, t: (m, 0, t, 0)),
            pl.BlockSpec((1, CIN), lambda m, t: (0, 0)),
        ],
        out_specs=pl.BlockSpec((1, rows, CEXT), lambda m, t: (m, t, 0)),
        out_shape=jax.ShapeDtypeStruct((micro, rows_dev, CEXT), jnp.bfloat16),
        name="prepare_pixels",
    )(place, pixels, in_gain[None])


def attend_body(feat_ref, query_ref, out_ref, sum_ref):
    tile = pl.program_id(1)
    feats = feat_ref[0]
    weights = jnp.exp(dot(feats, query_ref[...])).astype(jnp.bfloat16)

    @pl.when(tile == 0)
    def _():
        sum_ref[...] = jnp.zeros_like(sum_ref)

    sum_ref[...] += contract_rows(feats, weights)

    @pl.when(tile == pl.num_programs(1) - 1)
    def _():
        sums = sum_ref[...]
        low = sums.astype(jnp.bfloat16)
        rest = (sums - low.astype(jnp.float32))[ONES_ROW : ONES_ROW + 1]
        row = lax.broadcasted_iota(jnp.int32, sums.shape, 0)
        out_ref[0] = jnp.where(row == ONES_ROW + 1, rest, sums).astype(jnp.bfloat16)


def attend(feats, query_cols):
    micro, rows_dev, _ = feats.shape
    rows = tile_of(rows_dev, 1152)
    return pl.pallas_call(
        attend_body,
        grid=(micro, rows_dev // rows),
        in_specs=[
            pl.BlockSpec((1, rows, CEXT), lambda m, t: (m, t, 0)),
            pl.BlockSpec((CEXT, LAT), lambda m, t: (0, 0)),
        ],
        out_specs=pl.BlockSpec((1, CEXT, LAT), lambda m, t: (m, 0, 0)),
        out_shape=jax.ShapeDtypeStruct((micro, CEXT, LAT), jnp.bfloat16),
        scratch_shapes=[pltpu.VMEM((CEXT, LAT), jnp.float32)],
        name="attend",
    )(feats, query_cols)


def attend_back_body(pix_ref, feat_ref, gain_ref, qc_ref, dc_ref, qr_ref, dr_ref, *rest):
    grad_ref, score_ref, gain_sum_ref = rest[-3:]
    feats = feat_ref[0]
    weights = jnp.exp(dot(feats, qc_ref[...]))
    d_exp = dot(feats, dc_ref[0])
    d_scores = (weights * d_exp).astype(jnp.bfloat16)
    d_pix = (dot(d_scores, qr_ref[...]) + dot(weights.astype(jnp.bfloat16), dr_ref[0]))[:, :CIN]

    @pl.when(pl.program_id(0) == 0)
    def _():
        score_ref[...] = jnp.zeros_like(score_ref)
        gain_sum_ref[...] = jnp.zeros_like(gain_sum_ref)

    score_ref[...] += contract_rows(feats, d_scores)
    pix = pix_ref[0, 0]
    centred = pix - jnp.mean(pix, axis=-1, keepdims=True)
    scale = lax.rsqrt(jnp.mean(centred * centred, axis=-1, keepdims=True) + 1e-05)
    normed = centred * scale
    gain_sum_ref[...] += jnp.sum(d_pix * normed, axis=0, keepdims=True)
    d_normed = d_pix * gain_ref[...]
    along = jnp.mean(d_normed * normed, axis=-1, keepdims=True)
    grad_ref[0, 0] = (d_normed - jnp.mean(d_normed, axis=-1, keepdims=True) - normed * along) * scale


def attend_back(micro_index, earlier, pixels, feats, in_gain, query_cols, d_cols, query_rows, d_rows):
    rows_dev = feats.shape[1]
    rows = tile_of(rows_dev, 1152)
    m = micro_index
    in_specs = [
        pl.BlockSpec((1, 1, rows, CIN), lambda t: (m, 0, t, 0)),
        pl.BlockSpec((1, rows, CEXT), lambda t: (m, t, 0)),
        pl.BlockSpec((1, CIN), lambda t: (0, 0)),
        pl.BlockSpec((CEXT, LAT), lambda t: (0, 0)),
        pl.BlockSpec((1, CEXT, LAT), lambda t: (m, 0, 0)),
        pl.BlockSpec((LAT, CEXT), lambda t: (0, 0)),
        pl.BlockSpec((1, LAT, CEXT), lambda t: (m, 0, 0)),
    ]
    operands = [pixels, feats, in_gain[None], query_cols, d_cols, query_rows, d_rows]
    aliases = {}
    if earlier is not None:
        in_specs.append(pl.BlockSpec(memory_space=pl.ANY))
        aliases = {len(operands): 0}
        operands.append(earlier)
    return pl.pallas_call(
        attend_back_body,
        grid=(rows_dev // rows,),
        in_specs=in_specs,
        out_specs=[
            pl.BlockSpec((1, 1, rows, CIN), lambda t: (m, 0, t, 0)),
            pl.BlockSpec((CEXT, LAT), lambda t: (0, 0)),
            pl.BlockSpec((1, CIN), lambda t: (0, 0)),
        ],
        out_shape=[
            jax.ShapeDtypeStruct(pixels.shape, jnp.float32),
            jax.ShapeDtypeStruct((CEXT, LAT), jnp.float32),
            jax.ShapeDtypeStruct((1, CIN), jnp.float32),
        ],
        input_output_aliases=aliases,
        name="attend_back",
    )(*operands)


def slot_grads_body(where_ref, left_ref, right_ref, keep_ref, send_ref, full_ref, zero_ref, sems):
    half = NBLK // 2
    side = DL // BLK

    def put(source, block):
        place = where_ref[block]

        @pl.when(place < half)
        def _():
            pltpu.make_async_copy(source, keep_ref.at[place], sems.at[0]).start()

        @pl.when(place >= half)
        def _():
            pltpu.make_async_copy(source, send_ref.at[place - half], sems.at[1]).start()

    zero_ref[...] = jnp.zeros_like(zero_ref)

    @pl.loop(0, PER_MATRIX)
    def _(block):
        put(zero_ref, block)

    for matrix in range(3):
        full_ref[matrix] = contract_rows(left_ref[matrix], right_ref[matrix]).astype(jnp.bfloat16)

        @pl.loop(0, PER_MATRIX)
        def _(block, matrix=matrix):
            row = pl.multiple_of((block // side) * BLK, BLK)
            column = pl.multiple_of((block % side) * BLK, BLK)
            put(
                full_ref.at[matrix, pl.ds(row, BLK), pl.ds(column, BLK)],
                (matrix + 1) * PER_MATRIX + block,
            )

    pltpu.make_async_copy(keep_ref, keep_ref, sems.at[0]).wait()
    pltpu.make_async_copy(send_ref, send_ref, sems.at[1]).wait()


def slot_grads(where, left_rows, right_rows):
    half = jax.ShapeDtypeStruct((NBLK // 2, BLK, BLK), jnp.bfloat16)
    return pl.pallas_call(
        slot_grads_body,
        in_specs=[
            pl.BlockSpec(memory_space=pltpu.SMEM),
            pl.BlockSpec(memory_space=pltpu.VMEM),
            pl.BlockSpec(memory_space=pltpu.VMEM),
        ],
        out_specs=[pl.BlockSpec(memory_space=pl.ANY)] * 2,
        out_shape=[half, half],
        scratch_shapes=[
            pltpu.VMEM((3, DL, DL), jnp.bfloat16),
            pltpu.VMEM((BLK, BLK), jnp.bfloat16),
            pltpu.SemaphoreType.DMA((2,)),
        ],
        name="slot_grads",
    )(where, left_rows, right_rows)


def update_body(block_ref, lat_ref, dq_ref, sum_ref, ls_ref, rs_ref, lr_ref, rr_ref, ma_ref, *outs):
    new_left, new_right, new_master, new_copy = outs

    def exact(left_side, right_side, dims):
        return lax.dot_general(
            left_side,
            right_side,
            (dims, ((), ())),
            precision=HIGHEST_PRECISION,
            preferred_element_type=jnp.float32,
        )

    is_query = block_ref[pl.program_id(0)] < PER_MATRIX
    grad = jnp.where(is_query, contract_rows(lat_ref[...], dq_ref[...]), sum_ref[0])
    new_left[0] = 0.5 * ls_ref[0] + 0.5 * exact(grad, grad, ((1,), (1,)))
    new_right[0] = 0.5 * rs_ref[0] + 0.5 * exact(grad, grad, ((0,), (0,)))
    half_step = exact(lr_ref[0], grad, ((1,), (0,)))
    shampoo = exact(half_step, rr_ref[0], ((1,), (0,)))
    mean_square = jnp.mean(shampoo * shampoo)
    updated = ma_ref[0] - 0.5 / math.sqrt(DL) * (shampoo / jnp.sqrt(mean_square + 1e-06))
    new_master[0] = updated
    new_copy[0] = updated.astype(jnp.bfloat16)


def update_slots(blocks, lat_low, d_query, sums, left_stat, right_stat, left_root, right_root, master):
    slots = master.shape[0]
    side = DL // BLK
    spec = pl.BlockSpec((1, BLK, BLK), lambda s, block: (s, 0, 0))

    def query_block(s, block):
        return jnp.where(block[s] < PER_MATRIX, block[s], 0)

    shape = jax.ShapeDtypeStruct(master.shape, jnp.float32)
    return pl.pallas_call(
        update_body,
        grid_spec=pltpu.PrefetchScalarGridSpec(
            num_scalar_prefetch=1,
            grid=(slots,),
            in_specs=[
                pl.BlockSpec((LAT, BLK), lambda s, block: (0, query_block(s, block) // side)),
                pl.BlockSpec((LAT, BLK), lambda s, block: (0, query_block(s, block) % side)),
            ]
            + [spec] * 6,
            out_specs=[spec] * 4,
        ),
        out_shape=[shape, shape, shape, jax.ShapeDtypeStruct(master.shape, jnp.bfloat16)],
        name="update_slots",
    )(blocks, lat_low, d_query, sums, left_stat, right_stat, left_root, right_root, master)


def swap(array, axis):
    return lax.all_to_all(array, axis, 0, 0, tiled=True)


def everyone(array, axis):
    return swap(jnp.broadcast_to(array[None], (lax.axis_size(axis), *array.shape)), axis)


def total_of(partial):
    rows, width = partial.shape
    n_pix = lax.axis_size("pix")
    each = -(-rows // n_pix)
    padded = jnp.pad(partial.astype(jnp.bfloat16), ((0, each * n_pix - rows), (0, 0)))
    part = jnp.sum(swap(padded.reshape(n_pix, each, width), "pix").astype(jnp.float32), axis=0)
    part = jnp.sum(everyone(part, "img"), axis=0).astype(jnp.bfloat16)
    return everyone(part, "pix").reshape(n_pix * each, width)[:rows]


def add_low(left_side, right_side):
    return (left_side.astype(jnp.float32) + right_side.astype(jnp.float32)).astype(jnp.bfloat16)


def latent_pass(numerator, denominator, lat_part, cot_rows, lat_gain, w_out, w_up, w_down):
    attended = numerator / denominator[..., None]
    att_low = attended.astype(jnp.bfloat16)
    resid = lat_part[None] + product("mrd,de->mre", att_low, w_out)
    normed, normed_back = jax.vjp(standardize, resid)
    hn_low = (normed * lat_gain).astype(jnp.bfloat16)
    hidden = product("mrd,de->mre", hn_low, w_up)
    active, active_back = jax.vjp(gelu_exact, hidden)
    act_low = active.astype(jnp.bfloat16)
    latents_out = resid + product("mrd,de->mre", act_low, w_down)
    g_mlp = cot_rows.astype(jnp.bfloat16)
    d_active = product("mre,de->mrd", g_mlp, w_down)
    d_hidden = active_back(d_active)[0].astype(jnp.bfloat16)
    d_normed = product("mre,de->mrd", d_hidden, w_up)
    d_resid = cot_rows + normed_back(d_normed * lat_gain)[0]
    d_branch = d_resid.astype(jnp.bfloat16)
    d_attended = product("mre,de->mrd", d_branch, w_out)
    d_numer = d_attended / denominator[..., None]
    d_denom = -jnp.sum(d_attended * numerator / (denominator * denominator)[..., None], axis=-1)
    left_rows = jnp.stack([att_low, hn_low, act_low]).reshape(3, -1, DL)
    right_rows = jnp.stack([d_branch, d_hidden, g_mlp]).reshape(3, -1, DL)
    gain_mlp = jnp.sum(d_normed * normed, axis=(0, 1))
    lat_resid = jnp.sum(d_resid, axis=0)
    return (
        latents_out,
        d_numer.astype(jnp.bfloat16),
        d_denom,
        (left_rows, right_rows, gain_mlp, lat_resid),
    )


def shards(
    pixels,
    sides,
    owner,
    master,
    left_stat,
    right_stat,
    left_root,
    right_root,
    kv_weight,
    latent_array,
    in_gain,
    lat_gains,
    cotangent,
):
    micro = pixels.shape[0]
    rows_dev = pixels.shape[2]
    n_pix = lax.axis_size("pix")
    n_img = lax.axis_size("img")
    img = lax.axis_index("img")
    pix = lax.axis_index("pix")
    slots_dev = master.shape[0]
    lat_rows = LAT // n_pix
    row_start = pix * lat_rows
    inv_root = 1.0 / math.sqrt(DL)

    place = jnp.concatenate([(pix * rows_dev)[None], sides * sides]).astype(jnp.int32)
    gathered = lax.all_gather(master.astype(jnp.bfloat16), ("img", "pix"), axis=0, tiled=True)
    feats = prepare_pixels(place, pixels, in_gain)
    square = unblock(jnp.take(gathered, owner, axis=0), DL, BLK)
    w_query, w_out, w_up, w_down = (square[0], square[1], square[2], square[3])
    kv_low = kv_weight.astype(jnp.bfloat16)
    w_key, w_value = (kv_low[0], kv_low[1])
    lat_norm, lat_norm_back = jax.vjp(standardize, latent_array)
    lat_low = (lat_norm * lat_gains[0]).astype(jnp.bfloat16)
    query = dot(lat_low, w_query).astype(jnp.bfloat16)
    query_in = (product("ld,cd->lc", query, w_key) * inv_root).astype(jnp.bfloat16)
    query_rows = jnp.concatenate(
        [
            query_in,
            jnp.zeros((LAT, MASK_ROW - CIN), jnp.bfloat16),
            jnp.ones((LAT, CEXT - MASK_ROW), jnp.bfloat16),
        ],
        axis=1,
    )
    query_cols = query_rows.T

    sums = attend(feats, query_cols)
    sums = sums.reshape(micro, CEXT, n_pix, lat_rows).transpose(2, 1, 0, 3)
    sums = swap(sums.reshape(n_pix, CEXT, micro * lat_rows), "pix")
    sums = jnp.sum(sums.astype(jnp.float32), axis=0)
    numer_in = sums[:CIN]
    denominator = (sums[ONES_ROW] + sums[ONES_ROW + 1]).reshape(micro, lat_rows)
    numerator = fine("cr,cd->rd", numer_in, w_value).reshape(micro, lat_rows, DL)
    latents_out, d_numer, d_denom, latent_grads = latent_pass(
        numerator,
        denominator,
        lax.dynamic_slice_in_dim(latent_array, row_start, lat_rows, 0),
        cotangent[:, 0],
        lat_gains[1],
        w_out,
        w_up,
        w_down,
    )
    left_rows, right_rows, gain_mlp, lat_resid = latent_grads
    d_numer = d_numer.reshape(micro * lat_rows, DL)
    head, rest = two_terms(d_denom.reshape(1, micro * lat_rows))
    d_cols = product("rd,cd->cr", d_numer, w_value).astype(jnp.bfloat16)
    d_cols = jnp.concatenate([d_cols, head, rest, jnp.zeros_like(head)], axis=0)
    d_cols = everyone(d_cols, "pix").reshape(n_pix, CEXT, micro, lat_rows)
    d_cols = d_cols.transpose(2, 1, 0, 3).reshape(micro, CEXT, LAT)
    d_rows = d_cols.transpose(0, 2, 1)

    device_of = owner // slots_dev
    img_of = device_of // n_pix
    n_far = n_img // 2
    far_step = (img_of // 2 - img // 2) % n_far
    where = (far_step * n_pix + device_of % n_pix) * slots_dev + owner % slots_dev
    where = where + jnp.where(img_of % 2 == img % 2, 0, NBLK // 2)
    keep, send = slot_grads(where.astype(jnp.int32), left_rows, right_rows)
    got = lax.ppermute(send, "img", [(i, i ^ 1) for i in range(n_img)])
    count = NBLK // 2 // n_far
    pieces = [
        add_low(keep[k * count : (k + 1) * count], got[k * count : (k + 1) * count])
        for k in range(n_far)
    ]
    grads = pieces[0].astype(jnp.float32)
    for k in range(1, n_far):
        hop = [(i, (i + 2 * k) % n_img) for i in range(n_img)]
        grads = grads + lax.ppermute(pieces[k], "img", hop).astype(jnp.float32)

    value_grad = fine("cr,rd->cd", numer_in, d_numer)
    early = jnp.concatenate([value_grad, gain_mlp[None]], axis=0)

    results = (None,)
    score_sum = jnp.zeros((CEXT, LAT), jnp.float32)
    gain_sum = jnp.zeros((1, CIN), jnp.float32)
    for micro_index in range(micro):
        results = attend_back(
            micro_index,
            results[0],
            pixels,
            feats,
            in_gain,
            query_cols,
            d_cols,
            query_rows,
            d_rows,
        )
        score_sum = score_sum + results[1]
        gain_sum = gain_sum + results[2]
    pixel_grad = results[0]

    early_total = total_of(early).astype(jnp.float32)
    value_total = early_total[:CIN]
    gain_mlp_total = early_total[CIN]
    lat_part = jnp.sum(everyone(lat_resid.astype(jnp.bfloat16), "img").astype(jnp.float32), axis=0)
    resid_total = everyone(lat_part.astype(jnp.bfloat16), "pix").reshape(LAT, DL)

    late = jnp.concatenate([score_sum[:CIN], jnp.pad(gain_sum, ((0, 0), (0, LAT - CIN)))], axis=0)
    late_total = total_of(late)
    score_total = late_total[:CIN]
    in_gain_grad = late_total[CIN, :CIN].astype(jnp.float32)

    grads = grads.astype(jnp.bfloat16).reshape(n_pix * slots_dev, BLK, BLK)
    grads = swap(grads, "pix").reshape(n_pix, slots_dev, BLK, BLK)
    grads = jnp.sum(grads.astype(jnp.float32), axis=0)

    d_query = (contract_rows(score_total, w_key) * inv_root).astype(jnp.bfloat16)
    key_total = dot(score_total, query) * inv_root
    kv_grad = jnp.stack([key_total, value_total])
    d_lat_norm = product("le,de->ld", d_query, w_query)
    latent_grad = resid_total.astype(jnp.float32) + lat_norm_back(d_lat_norm * lat_gains[0])[0]
    lat_gain_grad = jnp.stack([jnp.sum(d_lat_norm * lat_norm, axis=0), gain_mlp_total])

    mine = (img * n_pix + pix) * slots_dev + jnp.arange(slots_dev, dtype=jnp.int32)
    blocks = jnp.sum(
        jnp.where(owner[None] == mine[:, None], jnp.arange(NBLK, dtype=jnp.int32)[None], 0), axis=1
    )
    new_left, new_right, new_master, new_copy = update_slots(
        blocks.astype(jnp.int32),
        lat_low,
        d_query,
        grads,
        left_stat,
        right_stat,
        left_root,
        right_root,
        master,
    )
    new_kv = kv_weight - 0.3 / math.sqrt(CIN) * normalized(kv_grad, (1, 2))
    new_latent = latent_array - 0.3 * normalized(latent_grad, (0, 1))
    new_in_gain = in_gain - 0.2 * normalized(in_gain_grad, (0,))
    new_lat_gains = lat_gains - 0.2 * normalized(lat_gain_grad, (1,))
    return (
        latents_out[:, None],
        pixel_grad,
        new_left,
        new_right,
        new_master,
        new_copy,
        kv_grad,
        new_kv,
        latent_grad,
        new_latent,
        in_gain_grad,
        new_in_gain,
        lat_gain_grad,
        new_lat_gains,
    )


def solution(mesh):
    pixel_spec = P(None, "img", "pix", None)
    slot_spec = P(("img", "pix"), None, None)
    in_specs = (
        (pixel_spec, P(), P()) + (slot_spec,) * 5 + (P(),) * 4 + (pixel_spec,)
    )
    out_specs = (pixel_spec, pixel_spec) + (slot_spec,) * 4 + (P(),) * 8
    return jax.shard_map(shards, mesh=mesh, in_specs=in_specs, out_specs=out_specs, check_vma=False)
```

```python
import math

import jax
import jax.numpy as jnp
from jax import lax
from jax.experimental import pallas as pl
from jax.experimental.pallas import tpu as pltpu
from jax.sharding import PartitionSpec as P

CIN = 261
DL = 1024
LAT = 512
BLK = 128
NBLK = 256
PER_MATRIX = NBLK // 4
CEXT = 264
ONES_ROW = 261
MASK_ROW = 263
MASKED = -1e30

HIGHEST_PRECISION = lax.Precision.HIGHEST


def standardize(values_in):
    average = jnp.mean(values_in, axis=-1, keepdims=True)
    centred = values_in - average
    variance = jnp.mean(centred * centred, axis=-1, keepdims=True)
    return centred * lax.rsqrt(variance + 1e-05)


def gelu_exact(values_in):
    return jax.nn.gelu(values_in, approximate=False)


def normalized(gradient, reduce_axes):
    return gradient / jnp.sqrt(
        jnp.mean(gradient * gradient, axis=reduce_axes, keepdims=True) + 1e-06
    )


def product(pattern, left_side, right_side):
    return jnp.einsum(pattern, left_side, right_side, preferred_element_type=jnp.float32)


def fine(pattern, left_side, right_side):
    return jnp.einsum(
        pattern,
        left_side.astype(jnp.float32),
        right_side.astype(jnp.float32),
        precision=HIGHEST_PRECISION,
    )


def two_terms(values_in):
    head = lax.reduce_precision(values_in, 8, 7)
    return (head.astype(jnp.bfloat16), (values_in - head).astype(jnp.bfloat16))


def contract_rows(left_side, right_side, precision=None):
    return lax.dot_general(
        left_side,
        right_side,
        (((0,), (0,)), ((), ())),
        precision=precision,
        preferred_element_type=jnp.float32,
    )


def dot(left_side, right_side):
    return jnp.dot(left_side, right_side, preferred_element_type=jnp.float32)


def dot_last(left_side, right_side):
    return lax.dot_general(
        left_side, right_side, (((1,), (1,)), ((), ())), preferred_element_type=jnp.float32
    )


def tile_of(rows, most):
    return max((size for size in range(128, most + 1, 128) if rows % size == 0), default=rows)


def lies_across(pixels):
    micro, _, rows_dev, _ = pixels.shape
    return jnp.swapaxes(pixels, 2, 3).reshape(micro, CIN, 1, rows_dev)


def centre(pix):
    centred = pix - jnp.mean(pix, axis=0, keepdims=True)
    scale = lax.rsqrt(jnp.mean(centred * centred, axis=0, keepdims=True) + 1e-05)
    return (centred * scale, scale)


def cost(flops, count):
    return pl.CostEstimate(flops=int(flops), bytes_accessed=int(count), transcendentals=0)


def prepare_body(place_ref, pix_ref, gain_ref, out_ref):
    micro_index = pl.program_id(0)
    normed, _ = centre(pix_ref[0, :, 0, :])
    columns = normed.shape[1]
    extra = (CEXT - CIN, columns)
    slot = place_ref[0] + pl.program_id(1) * columns + lax.broadcasted_iota(jnp.int32, extra, 1)
    row = lax.broadcasted_iota(jnp.int32, extra, 0) + CIN
    mask = jnp.where(slot < place_ref[1 + micro_index], 0.0, MASKED)
    tail = jnp.where(row == MASK_ROW, mask, 1.0)
    out_ref[0] = jnp.concatenate([normed * gain_ref[...], tail], axis=0).astype(jnp.bfloat16)


def prepare_pixels(place, across, gain_column):
    micro, _, _, rows_dev = across.shape
    rows = tile_of(rows_dev, 1152)
    return pl.pallas_call(
        prepare_body,
        grid=(micro, rows_dev // rows),
        in_specs=[
            pl.BlockSpec(memory_space=pltpu.SMEM),
            pl.BlockSpec((1, CIN, 1, rows), lambda m, t: (m, 0, 0, t)),
            pl.BlockSpec((CIN, 1), lambda m, t: (0, 0)),
        ],
        out_specs=pl.BlockSpec((1, CEXT, rows), lambda m, t: (m, 0, t)),
        out_shape=jax.ShapeDtypeStruct((micro, CEXT, rows_dev), jnp.bfloat16),
        cost_estimate=cost(0, 6 * micro * rows_dev * CEXT),
        name="prepare_pixels",
    )(place, across, gain_column)


def attend_body(feat_ref, query_ref, exp_ref, out_ref, sum_ref):
    tile = pl.program_id(1)
    feats = feat_ref[0]
    weights = jnp.exp(contract_rows(feats, query_ref[...])).astype(jnp.bfloat16)
    exp_ref[0] = weights

    @pl.when(tile == 0)
    def _():
        sum_ref[...] = jnp.zeros_like(sum_ref)

    sum_ref[...] += dot(feats, weights)

    @pl.when(tile == pl.num_programs(1) - 1)
    def _():
        sums = sum_ref[...]
        low = sums.astype(jnp.bfloat16)
        rest = (sums - low.astype(jnp.float32))[ONES_ROW : ONES_ROW + 1]
        row = lax.broadcasted_iota(jnp.int32, sums.shape, 0)
        out_ref[0] = jnp.where(row == ONES_ROW + 1, rest, sums).astype(jnp.bfloat16)


def attend(feats, query_cols):
    micro, _, rows_dev = feats.shape
    rows = tile_of(rows_dev, 1152)
    return pl.pallas_call(
        attend_body,
        grid=(micro, rows_dev // rows),
        in_specs=[
            pl.BlockSpec((1, CEXT, rows), lambda m, t: (m, 0, t)),
            pl.BlockSpec((CEXT, LAT), lambda m, t: (0, 0)),
        ],
        out_specs=[
            pl.BlockSpec((1, rows, LAT), lambda m, t: (m, t, 0)),
            pl.BlockSpec((1, CEXT, LAT), lambda m, t: (m, 0, 0)),
        ],
        out_shape=[
            jax.ShapeDtypeStruct((micro, rows_dev, LAT), jnp.bfloat16),
            jax.ShapeDtypeStruct((micro, CEXT, LAT), jnp.bfloat16),
        ],
        scratch_shapes=[pltpu.VMEM((CEXT, LAT), jnp.float32)],
        cost_estimate=cost(8 * micro * rows_dev * LAT * CEXT, 4 * micro * rows_dev * LAT),
        name="attend",
    )(feats, query_cols)


def attend_back_body(pix_ref, feat_ref, exp_ref, gain_ref, dc_ref, qc_ref, *rest):
    grad_ref, score_ref, gain_sum_ref = rest[-3:]
    feats = feat_ref[0]
    weights = exp_ref[0]
    d_exp = contract_rows(feats, dc_ref[0])
    d_scores = (weights.astype(jnp.float32) * d_exp).astype(jnp.bfloat16)

    @pl.when(pl.program_id(0) == 0)
    def _():
        score_ref[...] = jnp.zeros_like(score_ref)
        gain_sum_ref[...] = jnp.zeros_like(gain_sum_ref)

    score_ref[...] += dot(feats, d_scores)
    d_pix = (dot_last(qc_ref[...], d_scores) + dot_last(dc_ref[0], weights))[:CIN]
    normed, scale = centre(pix_ref[0, :, 0, :])
    gain_sum_ref[...] += jnp.sum(d_pix * normed, axis=1, keepdims=True)
    d_normed = d_pix * gain_ref[...]
    along = jnp.mean(d_normed * normed, axis=0, keepdims=True)
    level = jnp.mean(d_normed, axis=0, keepdims=True)
    grad_ref[0, :, 0, :] = (d_normed - level - normed * along) * scale


def attend_back(micro_index, earlier, across, feats, weights, gain_column, d_cols, query_cols):
    rows_dev = feats.shape[2]
    rows = tile_of(rows_dev, 1152)
    m = micro_index
    in_specs = [
        pl.BlockSpec((1, CIN, 1, rows), lambda t: (m, 0, 0, t)),
        pl.BlockSpec((1, CEXT, rows), lambda t: (m, 0, t)),
        pl.BlockSpec((1, rows, LAT), lambda t: (m, t, 0)),
        pl.BlockSpec((CIN, 1), lambda t: (0, 0)),
        pl.BlockSpec((1, CEXT, LAT), lambda t: (m, 0, 0)),
        pl.BlockSpec((CEXT, LAT), lambda t: (0, 0)),
    ]
    operands = [across, feats, weights, gain_column, d_cols, query_cols]
    aliases = {}
    if earlier is not None:
        in_specs.append(pl.BlockSpec(memory_space=pl.ANY))
        aliases = {len(operands): 0}
        operands.append(earlier)
    return pl.pallas_call(
        attend_back_body,
        grid=(rows_dev // rows,),
        in_specs=in_specs,
        out_specs=[
            pl.BlockSpec((1, CIN, 1, rows), lambda t: (m, 0, 0, t)),
            pl.BlockSpec((CEXT, LAT), lambda t: (0, 0)),
            pl.BlockSpec((CIN, 1), lambda t: (0, 0)),
        ],
        out_shape=[
            jax.ShapeDtypeStruct(across.shape, jnp.float32),
            jax.ShapeDtypeStruct((CEXT, LAT), jnp.float32),
            jax.ShapeDtypeStruct((CIN, 1), jnp.float32),
        ],
        input_output_aliases=aliases,
        cost_estimate=cost(16 * rows_dev * LAT * CEXT, rows_dev * 4000),
        name="attend_back",
    )(*operands)


def query_body(owner_ref, blocks_ref, lat_ref, gain_ref, key_ref, *rest):
    low_ref, query_ref, cols_ref, wq_ref, wo_ref, w1_ref, w2_ref, square_ref, sems = rest
    side = DL // BLK

    def fetch(matrix, target_ref):
        @pl.loop(0, PER_MATRIX)
        def _(block):
            row = pl.multiple_of((block // side) * BLK, BLK)
            column = pl.multiple_of((block % side) * BLK, BLK)
            pltpu.make_async_copy(
                blocks_ref.at[owner_ref[matrix * PER_MATRIX + block]],
                target_ref.at[pl.ds(row, BLK), pl.ds(column, BLK)],
                sems.at[matrix],
            ).start()

    def settle(matrix, target_ref):
        pltpu.make_async_copy(target_ref, target_ref, sems.at[matrix]).wait()

    fetch(0, square_ref)
    for matrix, target_ref in ((1, wo_ref), (2, w1_ref), (3, w2_ref)):
        fetch(matrix, target_ref)
    lat_low = (standardize(lat_ref[...]) * gain_ref[...]).astype(jnp.bfloat16)
    low_ref[...] = lat_low
    settle(0, square_ref)
    keep = pltpu.make_async_copy(square_ref, wq_ref, sems.at[0])
    keep.start()
    query = dot(lat_low, square_ref[...]).astype(jnp.bfloat16)
    query_ref[...] = query
    scores = dot_last(key_ref[...], query) * (1.0 / math.sqrt(DL))
    row = lax.broadcasted_iota(jnp.int32, (CEXT - CIN, LAT), 0) + CIN
    tail = jnp.where(row == MASK_ROW, 1.0, 0.0)
    cols_ref[...] = jnp.concatenate([scores, tail], axis=0).astype(jnp.bfloat16)
    keep.wait()
    for matrix, target_ref in ((1, wo_ref), (2, w1_ref), (3, w2_ref)):
        settle(matrix, target_ref)


def make_query(owner, gathered, latent_array, gain, w_key):
    vmem = pl.BlockSpec(memory_space=pltpu.VMEM)
    hbm = pl.BlockSpec(memory_space=pl.ANY)
    rows = jax.ShapeDtypeStruct((LAT, DL), jnp.bfloat16)
    square = jax.ShapeDtypeStruct((DL, DL), jnp.bfloat16)
    return pl.pallas_call(
        query_body,
        in_specs=[pl.BlockSpec(memory_space=pltpu.SMEM), hbm, vmem, vmem, vmem],
        out_specs=[vmem] * 3 + [hbm] * 4,
        out_shape=[rows, rows, jax.ShapeDtypeStruct((CEXT, LAT), jnp.bfloat16)] + [square] * 4,
        scratch_shapes=[pltpu.VMEM((DL, DL), jnp.bfloat16), pltpu.SemaphoreType.DMA((4,))],
        cost_estimate=cost(3 * LAT * DL * DL, 4 * NBLK * BLK * BLK),
        name="make_query",
    )(owner, gathered, latent_array, gain[None], w_key)


def slot_grads_body(where_ref, left_ref, right_ref, keep_ref, send_ref, full_ref, zero_ref, sems):
    half = NBLK // 2
    side = DL // BLK

    def put(source, block):
        place = where_ref[block]

        @pl.when(place < half)
        def _():
            pltpu.make_async_copy(source, keep_ref.at[place], sems.at[0]).start()

        @pl.when(place >= half)
        def _():
            pltpu.make_async_copy(source, send_ref.at[place - half], sems.at[1]).start()

    zero_ref[...] = jnp.zeros_like(zero_ref)

    @pl.loop(0, PER_MATRIX)
    def _(block):
        put(zero_ref, block)

    for matrix in range(3):
        full_ref[matrix] = contract_rows(left_ref[matrix], right_ref[matrix]).astype(jnp.bfloat16)

        @pl.loop(0, PER_MATRIX)
        def _(block, matrix=matrix):
            row = pl.multiple_of((block // side) * BLK, BLK)
            column = pl.multiple_of((block % side) * BLK, BLK)
            put(
                full_ref.at[matrix, pl.ds(row, BLK), pl.ds(column, BLK)],
                (matrix + 1) * PER_MATRIX + block,
            )

    pltpu.make_async_copy(keep_ref, keep_ref, sems.at[0]).wait()
    pltpu.make_async_copy(send_ref, send_ref, sems.at[1]).wait()


def slot_grads(where, left_rows, right_rows):
    half = jax.ShapeDtypeStruct((NBLK // 2, BLK, BLK), jnp.bfloat16)
    return pl.pallas_call(
        slot_grads_body,
        in_specs=[
            pl.BlockSpec(memory_space=pltpu.SMEM),
            pl.BlockSpec(memory_space=pltpu.VMEM),
            pl.BlockSpec(memory_space=pltpu.VMEM),
        ],
        out_specs=[pl.BlockSpec(memory_space=pl.ANY)] * 2,
        out_shape=[half, half],
        scratch_shapes=[
            pltpu.VMEM((3, DL, DL), jnp.bfloat16),
            pltpu.VMEM((BLK, BLK), jnp.bfloat16),
            pltpu.SemaphoreType.DMA((2,)),
        ],
        name="slot_grads",
    )(where, left_rows, right_rows)


def update_body(block_ref, lat_ref, dq_ref, sum_ref, ls_ref, rs_ref, lr_ref, rr_ref, ma_ref, *outs):
    new_left, new_right, new_master, new_copy = outs

    def exact(left_side, right_side, dims):
        return lax.dot_general(
            left_side,
            right_side,
            (dims, ((), ())),
            precision=HIGHEST_PRECISION,
            preferred_element_type=jnp.float32,
        )

    is_query = block_ref[pl.program_id(0)] < PER_MATRIX
    grad = jnp.where(is_query, contract_rows(lat_ref[...], dq_ref[...]), sum_ref[0])
    new_left[0] = 0.5 * ls_ref[0] + 0.5 * exact(grad, grad, ((1,), (1,)))
    new_right[0] = 0.5 * rs_ref[0] + 0.5 * exact(grad, grad, ((0,), (0,)))
    half_step = exact(lr_ref[0], grad, ((1,), (0,)))
    shampoo = exact(half_step, rr_ref[0], ((1,), (0,)))
    mean_square = jnp.mean(shampoo * shampoo)
    updated = ma_ref[0] - 0.5 / math.sqrt(DL) * (shampoo / jnp.sqrt(mean_square + 1e-06))
    new_master[0] = updated
    new_copy[0] = updated.astype(jnp.bfloat16)


def update_slots(blocks, lat_low, d_query, sums, left_stat, right_stat, left_root, right_root, master):
    slots = master.shape[0]
    side = DL // BLK
    spec = pl.BlockSpec((1, BLK, BLK), lambda s, block: (s, 0, 0))

    def query_block(s, block):
        return jnp.where(block[s] < PER_MATRIX, block[s], 0)

    shape = jax.ShapeDtypeStruct(master.shape, jnp.float32)
    return pl.pallas_call(
        update_body,
        grid_spec=pltpu.PrefetchScalarGridSpec(
            num_scalar_prefetch=1,
            grid=(slots,),
            in_specs=[
                pl.BlockSpec((LAT, BLK), lambda s, block: (0, query_block(s, block) // side)),
                pl.BlockSpec((LAT, BLK), lambda s, block: (0, query_block(s, block) % side)),
            ]
            + [spec] * 6,
            out_specs=[spec] * 4,
        ),
        out_shape=[shape, shape, shape, jax.ShapeDtypeStruct(master.shape, jnp.bfloat16)],
        name="update_slots",
    )(blocks, lat_low, d_query, sums, left_stat, right_stat, left_root, right_root, master)


def swap(array, axis):
    return lax.all_to_all(array, axis, 0, 0, tiled=True)


def everyone(array, axis):
    return swap(jnp.broadcast_to(array[None], (lax.axis_size(axis), *array.shape)), axis)


def total_of(partial):
    rows, width = partial.shape
    n_pix = lax.axis_size("pix")
    each = -(-rows // n_pix)
    padded = jnp.pad(partial.astype(jnp.bfloat16), ((0, each * n_pix - rows), (0, 0)))
    part = jnp.sum(swap(padded.reshape(n_pix, each, width), "pix").astype(jnp.float32), axis=0)
    part = jnp.sum(everyone(part, "img"), axis=0).astype(jnp.bfloat16)
    return everyone(part, "pix").reshape(n_pix * each, width)[:rows]


def add_low(left_side, right_side):
    return (left_side.astype(jnp.float32) + right_side.astype(jnp.float32)).astype(jnp.bfloat16)


def latent_pass(numerator, denominator, lat_part, cot_rows, lat_gain, w_out, w_up, w_down):
    attended = numerator / denominator[..., None]
    att_low = attended.astype(jnp.bfloat16)
    resid = lat_part[None] + product("mrd,de->mre", att_low, w_out)
    normed, normed_back = jax.vjp(standardize, resid)
    hn_low = (normed * lat_gain).astype(jnp.bfloat16)
    hidden = product("mrd,de->mre", hn_low, w_up)
    active, active_back = jax.vjp(gelu_exact, hidden)
    act_low = active.astype(jnp.bfloat16)
    latents_out = resid + product("mrd,de->mre", act_low, w_down)
    g_mlp = cot_rows.astype(jnp.bfloat16)
    d_active = product("mre,de->mrd", g_mlp, w_down)
    d_hidden = active_back(d_active)[0].astype(jnp.bfloat16)
    d_normed = product("mre,de->mrd", d_hidden, w_up)
    d_resid = cot_rows + normed_back(d_normed * lat_gain)[0]
    d_branch = d_resid.astype(jnp.bfloat16)
    d_attended = product("mre,de->mrd", d_branch, w_out)
    d_numer = d_attended / denominator[..., None]
    d_denom = -jnp.sum(d_attended * numerator / (denominator * denominator)[..., None], axis=-1)
    left_rows = jnp.stack([att_low, hn_low, act_low]).reshape(3, -1, DL)
    right_rows = jnp.stack([d_branch, d_hidden, g_mlp]).reshape(3, -1, DL)
    gain_mlp = jnp.sum(d_normed * normed, axis=(0, 1))
    lat_resid = jnp.sum(d_resid, axis=0)
    return (
        latents_out,
        d_numer.astype(jnp.bfloat16),
        d_denom,
        (left_rows, right_rows, gain_mlp, lat_resid),
    )


def shards(
    pixels,
    sides,
    owner,
    master,
    left_stat,
    right_stat,
    left_root,
    right_root,
    kv_weight,
    latent_array,
    in_gain,
    lat_gains,
    cotangent,
):
    micro = pixels.shape[0]
    rows_dev = pixels.shape[2]
    n_pix = lax.axis_size("pix")
    n_img = lax.axis_size("img")
    img = lax.axis_index("img")
    pix = lax.axis_index("pix")
    slots_dev = master.shape[0]
    lat_rows = LAT // n_pix
    row_start = pix * lat_rows
    inv_root = 1.0 / math.sqrt(DL)

    place = jnp.concatenate([(pix * rows_dev)[None], sides * sides]).astype(jnp.int32)
    gathered = lax.all_gather(master.astype(jnp.bfloat16), ("img", "pix"), axis=0, tiled=True)
    across = lies_across(pixels)
    gain_column = in_gain[:, None]
    feats = prepare_pixels(place, across, gain_column)
    kv_low = kv_weight.astype(jnp.bfloat16)
    w_key, w_value = (kv_low[0], kv_low[1])
    lat_norm, lat_norm_back = jax.vjp(standardize, latent_array)
    lat_low, query, query_cols, w_query, w_out, w_up, w_down = make_query(
        owner, gathered, latent_array, lat_gains[0], w_key
    )

    weights, sums = attend(feats, query_cols)
    sums = sums.reshape(micro, CEXT, n_pix, lat_rows).transpose(2, 1, 0, 3)
    sums = swap(sums.reshape(n_pix, CEXT, micro * lat_rows), "pix")
    sums = jnp.sum(sums.astype(jnp.float32), axis=0)
    numer_in = sums[:CIN]
    denominator = (sums[ONES_ROW] + sums[ONES_ROW + 1]).reshape(micro, lat_rows)
    numerator = fine("cr,cd->rd", numer_in, w_value).reshape(micro, lat_rows, DL)
    latents_out, d_numer, d_denom, latent_grads = latent_pass(
        numerator,
        denominator,
        lax.dynamic_slice_in_dim(latent_array, row_start, lat_rows, 0),
        cotangent[:, 0],
        lat_gains[1],
        w_out,
        w_up,
        w_down,
    )
    left_rows, right_rows, gain_mlp, lat_resid = latent_grads
    d_numer = d_numer.reshape(micro * lat_rows, DL)
    head, rest = two_terms(d_denom.reshape(1, micro * lat_rows))
    d_cols = product("rd,cd->cr", d_numer, w_value).astype(jnp.bfloat16)
    d_cols = jnp.concatenate([d_cols, head, rest, jnp.zeros_like(head)], axis=0)
    d_cols = everyone(d_cols, "pix").reshape(n_pix, CEXT, micro, lat_rows)
    d_cols = d_cols.transpose(2, 1, 0, 3).reshape(micro, CEXT, LAT)

    device_of = owner // slots_dev
    img_of = device_of // n_pix
    n_far = n_img // 2
    far_step = (img_of // 2 - img // 2) % n_far
    where = (far_step * n_pix + device_of % n_pix) * slots_dev + owner % slots_dev
    where = where + jnp.where(img_of % 2 == img % 2, 0, NBLK // 2)
    keep, send = slot_grads(where.astype(jnp.int32), left_rows, right_rows)
    got = lax.ppermute(send, "img", [(i, i ^ 1) for i in range(n_img)])
    count = NBLK // 2 // n_far
    pieces = [
        add_low(keep[k * count : (k + 1) * count], got[k * count : (k + 1) * count])
        for k in range(n_far)
    ]
    grads = pieces[0].astype(jnp.float32)
    for k in range(1, n_far):
        hop = [(i, (i + 2 * k) % n_img) for i in range(n_img)]
        grads = grads + lax.ppermute(pieces[k], "img", hop).astype(jnp.float32)

    value_grad = fine("cr,rd->cd", numer_in, d_numer)
    early = jnp.concatenate([value_grad, gain_mlp[None]], axis=0)

    results = (None,)
    score_sum = jnp.zeros((CEXT, LAT), jnp.float32)
    gain_sum = jnp.zeros((CIN, 1), jnp.float32)
    for micro_index in range(micro):
        results = attend_back(
            micro_index, results[0], across, feats, weights, gain_column, d_cols, query_cols
        )
        score_sum = score_sum + results[1]
        gain_sum = gain_sum + results[2]
    pixel_grad = jnp.swapaxes(results[0].reshape(micro, 1, CIN, rows_dev), 2, 3)

    early_total = total_of(early).astype(jnp.float32)
    value_total = early_total[:CIN]
    gain_mlp_total = early_total[CIN]
    lat_part = jnp.sum(everyone(lat_resid.astype(jnp.bfloat16), "img").astype(jnp.float32), axis=0)
    resid_total = everyone(lat_part.astype(jnp.bfloat16), "pix").reshape(LAT, DL)

    late = jnp.concatenate([score_sum[:CIN], jnp.pad(gain_sum.T, ((0, 0), (0, LAT - CIN)))], axis=0)
    late_total = total_of(late)
    score_total = late_total[:CIN]
    in_gain_grad = late_total[CIN, :CIN].astype(jnp.float32)

    grads = grads.astype(jnp.bfloat16).reshape(n_pix * slots_dev, BLK, BLK)
    grads = swap(grads, "pix").reshape(n_pix, slots_dev, BLK, BLK)
    grads = jnp.sum(grads.astype(jnp.float32), axis=0)

    d_query = (contract_rows(score_total, w_key) * inv_root).astype(jnp.bfloat16)
    key_total = dot(score_total, query) * inv_root
    kv_grad = jnp.stack([key_total, value_total])
    d_lat_norm = product("le,de->ld", d_query, w_query)
    latent_grad = resid_total.astype(jnp.float32) + lat_norm_back(d_lat_norm * lat_gains[0])[0]
    lat_gain_grad = jnp.stack([jnp.sum(d_lat_norm * lat_norm, axis=0), gain_mlp_total])

    mine = (img * n_pix + pix) * slots_dev + jnp.arange(slots_dev, dtype=jnp.int32)
    blocks = jnp.sum(
        jnp.where(owner[None] == mine[:, None], jnp.arange(NBLK, dtype=jnp.int32)[None], 0), axis=1
    )
    new_left, new_right, new_master, new_copy = update_slots(
        blocks.astype(jnp.int32),
        lat_low,
        d_query,
        grads,
        left_stat,
        right_stat,
        left_root,
        right_root,
        master,
    )
    new_kv = kv_weight - 0.3 / math.sqrt(CIN) * normalized(kv_grad, (1, 2))
    new_latent = latent_array - 0.3 * normalized(latent_grad, (0, 1))
    new_in_gain = in_gain - 0.2 * normalized(in_gain_grad, (0,))
    new_lat_gains = lat_gains - 0.2 * normalized(lat_gain_grad, (1,))
    return (
        latents_out[:, None],
        pixel_grad,
        new_left,
        new_right,
        new_master,
        new_copy,
        kv_grad,
        new_kv,
        latent_grad,
        new_latent,
        in_gain_grad,
        new_in_gain,
        lat_gain_grad,
        new_lat_gains,
    )


def solution(mesh):
    pixel_spec = P(None, "img", "pix", None)
    slot_spec = P(("img", "pix"), None, None)
    in_specs = (
        (pixel_spec, P(), P()) + (slot_spec,) * 5 + (P(),) * 4 + (pixel_spec,)
    )
    out_specs = (pixel_spec, pixel_spec) + (slot_spec,) * 4 + (P(),) * 8
    return jax.shard_map(shards, mesh=mesh, in_specs=in_specs, out_specs=out_specs, check_vma=False)
```

```python
import math

import jax
import jax.numpy as jnp
from jax import lax
from jax.experimental import pallas as pl
from jax.experimental.pallas import tpu as pltpu
from jax.sharding import PartitionSpec as P

CIN = 261
DL = 1024
LAT = 512
BLK = 128
NBLK = 256
PER_MATRIX = NBLK // 4
CEXT = 264
ONES_ROW = 261
MASK_ROW = 263
MASKED = -1e30

HIGHEST_PRECISION = lax.Precision.HIGHEST


def standardize(values_in):
    average = jnp.mean(values_in, axis=-1, keepdims=True)
    centred = values_in - average
    variance = jnp.mean(centred * centred, axis=-1, keepdims=True)
    return centred * lax.rsqrt(variance + 1e-05)


def gelu_exact(values_in):
    return jax.nn.gelu(values_in, approximate=False)


def normalized(gradient, reduce_axes):
    return gradient / jnp.sqrt(
        jnp.mean(gradient * gradient, axis=reduce_axes, keepdims=True) + 1e-06
    )


def product(pattern, left_side, right_side):
    return jnp.einsum(pattern, left_side, right_side, preferred_element_type=jnp.float32)


def fine(pattern, left_side, right_side):
    return jnp.einsum(
        pattern,
        left_side.astype(jnp.float32),
        right_side.astype(jnp.float32),
        precision=HIGHEST_PRECISION,
    )


def two_terms(values_in):
    head = lax.reduce_precision(values_in, 8, 7)
    return (head.astype(jnp.bfloat16), (values_in - head).astype(jnp.bfloat16))


def contract_rows(left_side, right_side, precision=None):
    return lax.dot_general(
        left_side,
        right_side,
        (((0,), (0,)), ((), ())),
        precision=precision,
        preferred_element_type=jnp.float32,
    )


def dot(left_side, right_side):
    return jnp.dot(left_side, right_side, preferred_element_type=jnp.float32)


def dot_last(left_side, right_side):
    return lax.dot_general(
        left_side, right_side, (((1,), (1,)), ((), ())), preferred_element_type=jnp.float32
    )


def tile_of(rows, most):
    return max((size for size in range(128, most + 1, 128) if rows % size == 0), default=rows)


def lies_across(pixels):
    micro, _, rows_dev, _ = pixels.shape
    return jnp.swapaxes(pixels, 2, 3).reshape(micro, CIN, 1, rows_dev)


def centre(pix):
    centred = pix - jnp.mean(pix, axis=0, keepdims=True)
    scale = lax.rsqrt(jnp.mean(centred * centred, axis=0, keepdims=True) + 1e-05)
    return (centred * scale, scale)


def cost(flops, count):
    return pl.CostEstimate(flops=int(flops), bytes_accessed=int(count), transcendentals=0)


def prepare_body(place_ref, pix_ref, gain_ref, out_ref):
    micro_index = pl.program_id(0)
    normed, _ = centre(pix_ref[0, :, 0, :])
    columns = normed.shape[1]
    extra = (CEXT - CIN, columns)
    slot = place_ref[0] + pl.program_id(1) * columns + lax.broadcasted_iota(jnp.int32, extra, 1)
    row = lax.broadcasted_iota(jnp.int32, extra, 0) + CIN
    mask = jnp.where(slot < place_ref[1 + micro_index], 0.0, MASKED)
    tail = jnp.where(row == MASK_ROW, mask, 1.0)
    out_ref[0] = jnp.concatenate([normed * gain_ref[...], tail], axis=0).astype(jnp.bfloat16)


def prepare_pixels(place, across, gain_column):
    micro, _, _, rows_dev = across.shape
    rows = tile_of(rows_dev, 1152)
    return pl.pallas_call(
        prepare_body,
        grid=(micro, rows_dev // rows),
        in_specs=[
            pl.BlockSpec(memory_space=pltpu.SMEM),
            pl.BlockSpec((1, CIN, 1, rows), lambda m, t: (m, 0, 0, t)),
            pl.BlockSpec((CIN, 1), lambda m, t: (0, 0)),
        ],
        out_specs=pl.BlockSpec((1, CEXT, rows), lambda m, t: (m, 0, t)),
        out_shape=jax.ShapeDtypeStruct((micro, CEXT, rows_dev), jnp.bfloat16),
        cost_estimate=cost(0, 6 * micro * rows_dev * CEXT),
        name="prepare_pixels",
    )(place, across, gain_column)


def attend_body(feat_ref, query_ref, exp_ref, out_ref, sum_ref):
    tile = pl.program_id(1)
    feats = feat_ref[0]
    weights = jnp.exp(contract_rows(feats, query_ref[...])).astype(jnp.bfloat16)
    exp_ref[0] = weights

    @pl.when(tile == 0)
    def _():
        sum_ref[...] = jnp.zeros_like(sum_ref)

    sum_ref[...] += dot(feats, weights)

    @pl.when(tile == pl.num_programs(1) - 1)
    def _():
        sums = sum_ref[...]
        low = sums.astype(jnp.bfloat16)
        rest = (sums - low.astype(jnp.float32))[ONES_ROW : ONES_ROW + 1]
        row = lax.broadcasted_iota(jnp.int32, sums.shape, 0)
        out_ref[0] = jnp.where(row == ONES_ROW + 1, rest, sums).astype(jnp.bfloat16)


def attend(feats, query_cols):
    micro, _, rows_dev = feats.shape
    rows = tile_of(rows_dev, 1152)
    return pl.pallas_call(
        attend_body,
        grid=(micro, rows_dev // rows),
        in_specs=[
            pl.BlockSpec((1, CEXT, rows), lambda m, t: (m, 0, t)),
            pl.BlockSpec((CEXT, LAT), lambda m, t: (0, 0)),
        ],
        out_specs=[
            pl.BlockSpec((1, rows, LAT), lambda m, t: (m, t, 0)),
            pl.BlockSpec((1, CEXT, LAT), lambda m, t: (m, 0, 0)),
        ],
        out_shape=[
            jax.ShapeDtypeStruct((micro, rows_dev, LAT), jnp.bfloat16),
            jax.ShapeDtypeStruct((micro, CEXT, LAT), jnp.bfloat16),
        ],
        scratch_shapes=[pltpu.VMEM((CEXT, LAT), jnp.float32)],
        cost_estimate=cost(8 * micro * rows_dev * LAT * CEXT, 4 * micro * rows_dev * LAT),
        name="attend",
    )(feats, query_cols)


def tiles_of(feats):
    rows_dev = feats.shape[2]
    return rows_dev // tile_of(rows_dev, 1152)


def parts_of(feats):
    micro = feats.shape[0]
    tiles = tiles_of(feats)
    head = tiles - tiles // 2
    parts = []
    for m in range(micro):
        parts.append((m, 0, head))
        if head < tiles:
            parts.append((m, head, tiles - head))
    return parts


def attend_back_body(pix_ref, feat_ref, exp_ref, gain_ref, dc_ref, qc_ref, *rest):
    grad_ref, score_ref, gain_sum_ref = rest[-3:]
    feats = feat_ref[0]
    weights = exp_ref[0]
    d_exp = contract_rows(feats, dc_ref[0])
    d_scores = (weights.astype(jnp.float32) * d_exp).astype(jnp.bfloat16)

    @pl.when(pl.program_id(0) == 0)
    def _():
        score_ref[...] = jnp.zeros_like(score_ref)
        gain_sum_ref[...] = jnp.zeros_like(gain_sum_ref)

    score_ref[...] += dot(feats, d_scores)
    d_pix = (dot_last(qc_ref[...], d_scores) + dot_last(dc_ref[0], weights))[:CIN]
    normed, scale = centre(pix_ref[0, :, 0, :])
    gain_sum_ref[...] += jnp.sum(d_pix * normed, axis=1, keepdims=True)
    d_normed = d_pix * gain_ref[...]
    along = jnp.mean(d_normed * normed, axis=0, keepdims=True)
    level = jnp.mean(d_normed, axis=0, keepdims=True)
    grad_ref[0, :, 0, :] = (d_normed - level - normed * along) * scale


def attend_back(part, earlier, across, feats, weights, gain_column, d_cols, query_cols):
    m, first, tiles = part
    rows = feats.shape[2] // tiles_of(feats)
    in_specs = [
        pl.BlockSpec((1, CIN, 1, rows), lambda t: (m, 0, 0, first + t)),
        pl.BlockSpec((1, CEXT, rows), lambda t: (m, 0, first + t)),
        pl.BlockSpec((1, rows, LAT), lambda t: (m, first + t, 0)),
        pl.BlockSpec((CIN, 1), lambda t: (0, 0)),
        pl.BlockSpec((1, CEXT, LAT), lambda t: (m, 0, 0)),
        pl.BlockSpec((CEXT, LAT), lambda t: (0, 0)),
    ]
    operands = [across, feats, weights, gain_column, d_cols, query_cols]
    aliases = {}
    if earlier is not None:
        in_specs.append(pl.BlockSpec(memory_space=pl.ANY))
        aliases = {len(operands): 0}
        operands.append(earlier)
    return pl.pallas_call(
        attend_back_body,
        grid=(tiles,),
        in_specs=in_specs,
        out_specs=[
            pl.BlockSpec((1, CIN, 1, rows), lambda t: (m, 0, 0, first + t)),
            pl.BlockSpec((CEXT, LAT), lambda t: (0, 0)),
            pl.BlockSpec((CIN, 1), lambda t: (0, 0)),
        ],
        out_shape=[
            jax.ShapeDtypeStruct(across.shape, jnp.float32),
            jax.ShapeDtypeStruct((CEXT, LAT), jnp.float32),
            jax.ShapeDtypeStruct((CIN, 1), jnp.float32),
        ],
        input_output_aliases=aliases,
        cost_estimate=cost(16 * tiles * rows * LAT * CEXT, tiles * rows * 4000),
        name="attend_back",
    )(*operands)


def query_body(owner_ref, blocks_ref, lat_ref, gain_ref, key_ref, *rest):
    low_ref, query_ref, cols_ref, wq_ref, wo_ref, w1_ref, w2_ref, sems = rest
    squares = (wq_ref, wo_ref, w1_ref, w2_ref)
    side = DL // BLK

    def fetch(matrix):
        @pl.loop(0, PER_MATRIX)
        def _(block):
            row = pl.multiple_of((block // side) * BLK, BLK)
            column = pl.multiple_of((block % side) * BLK, BLK)
            pltpu.make_async_copy(
                blocks_ref.at[owner_ref[matrix * PER_MATRIX + block]],
                squares[matrix].at[pl.ds(row, BLK), pl.ds(column, BLK)],
                sems.at[matrix],
            ).start()

    def settle(matrix):
        pltpu.make_async_copy(squares[matrix], squares[matrix], sems.at[matrix]).wait()

    for matrix in range(4):
        fetch(matrix)
    lat_low = (standardize(lat_ref[...]) * gain_ref[...]).astype(jnp.bfloat16)
    low_ref[...] = lat_low
    settle(0)
    query = dot(lat_low, wq_ref[...]).astype(jnp.bfloat16)
    query_ref[...] = query
    scores = dot_last(key_ref[...], query) * (1.0 / math.sqrt(DL))
    row = lax.broadcasted_iota(jnp.int32, (CEXT - CIN, LAT), 0) + CIN
    tail = jnp.where(row == MASK_ROW, 1.0, 0.0)
    cols_ref[...] = jnp.concatenate([scores, tail], axis=0).astype(jnp.bfloat16)
    for matrix in range(1, 4):
        settle(matrix)


def make_query(owner, gathered, latent_array, gain, w_key):
    vmem = pl.BlockSpec(memory_space=pltpu.VMEM)
    hbm = pl.BlockSpec(memory_space=pl.ANY)
    rows = jax.ShapeDtypeStruct((LAT, DL), jnp.bfloat16)
    square = jax.ShapeDtypeStruct((DL, DL), jnp.bfloat16)
    return pl.pallas_call(
        query_body,
        in_specs=[pl.BlockSpec(memory_space=pltpu.SMEM), hbm, vmem, vmem, vmem],
        out_specs=[vmem] * 7,
        out_shape=[rows, rows, jax.ShapeDtypeStruct((CEXT, LAT), jnp.bfloat16)] + [square] * 4,
        scratch_shapes=[pltpu.SemaphoreType.DMA((4,))],
        cost_estimate=cost(3 * LAT * DL * DL, 4 * NBLK * BLK * BLK),
        name="make_query",
    )(owner, gathered, latent_array, gain[None], w_key)


def image_sums_body(where_ref, *rest):
    n_img = len(rest) - 7
    pieces, (grads_ref, value_ref, resid_ref, rows_ref, full_ref, zero_ref, sems) = (
        rest[:n_img],
        rest[n_img:],
    )
    side = DL // BLK
    count = pieces[0].shape[1]

    def put(source, block):
        place = where_ref[n_img + block]

        @pl.when(place >= 0)
        def _():
            pltpu.make_async_copy(source, grads_ref.at[place], sems.at[1]).start()

    for piece in range(n_img):
        first = pl.multiple_of(where_ref[piece] * count, count)
        pltpu.make_async_copy(
            pieces[piece], rows_ref.at[:, pl.ds(first, count), :], sems.at[0]
        ).start()
    zero_ref[...] = jnp.zeros_like(zero_ref)

    @pl.loop(0, PER_MATRIX)
    def _(block):
        put(zero_ref, block)

    pltpu.make_async_copy(rows_ref, rows_ref, sems.at[0]).wait()
    for matrix in range(3):
        full_ref[matrix] = contract_rows(rows_ref[matrix], rows_ref[3 + matrix]).astype(jnp.bfloat16)

        @pl.loop(0, PER_MATRIX)
        def _(block, matrix=matrix):
            row = pl.multiple_of((block // side) * BLK, BLK)
            column = pl.multiple_of((block % side) * BLK, BLK)
            put(
                full_ref.at[matrix, pl.ds(row, BLK), pl.ds(column, BLK)],
                (matrix + 1) * PER_MATRIX + block,
            )

    value_ref[...] = contract_rows(rows_ref[7, :, :CEXT], rows_ref[6]).astype(jnp.bfloat16)
    each = resid_ref.shape[0]
    total = rows_ref[3, :each, :].astype(jnp.float32)
    for first in range(each, rows_ref.shape[1], each):
        total = total + rows_ref[3, first : first + each, :].astype(jnp.float32)
    resid_ref[...] = total.astype(jnp.bfloat16)
    pltpu.make_async_copy(grads_ref, grads_ref, sems.at[1]).wait()


def image_sums(where, pieces, lat_rows):
    n_img = len(pieces)
    slabs, count, _ = pieces[0].shape
    hbm = pl.BlockSpec(memory_space=pl.ANY)
    vmem = pl.BlockSpec(memory_space=pltpu.VMEM)
    return pl.pallas_call(
        image_sums_body,
        in_specs=[pl.BlockSpec(memory_space=pltpu.SMEM)] + [hbm] * n_img,
        out_specs=[hbm, vmem, vmem],
        out_shape=[
            jax.ShapeDtypeStruct((NBLK // n_img, BLK, BLK), jnp.bfloat16),
            jax.ShapeDtypeStruct((CEXT, DL), jnp.bfloat16),
            jax.ShapeDtypeStruct((lat_rows, DL), jnp.bfloat16),
        ],
        scratch_shapes=[
            pltpu.VMEM((slabs, n_img * count, DL), jnp.bfloat16),
            pltpu.VMEM((3, DL, DL), jnp.bfloat16),
            pltpu.VMEM((BLK, BLK), jnp.bfloat16),
            pltpu.SemaphoreType.DMA((2,)),
        ],
        cost_estimate=cost(8 * n_img * count * DL * DL, 16 * DL * DL),
        name="image_sums",
    )(where, *pieces)


def update_body(block_ref, lat_ref, dq_ref, sum_ref, ls_ref, rs_ref, lr_ref, rr_ref, ma_ref, *outs):
    new_left, new_right, new_master, new_copy = outs

    def exact(left_side, right_side, dims):
        return lax.dot_general(
            left_side,
            right_side,
            (dims, ((), ())),
            precision=HIGHEST_PRECISION,
            preferred_element_type=jnp.float32,
        )

    is_query = block_ref[pl.program_id(0)] < PER_MATRIX
    grad = jnp.where(is_query, contract_rows(lat_ref[...], dq_ref[...]), sum_ref[0])
    new_left[0] = 0.5 * ls_ref[0] + 0.5 * exact(grad, grad, ((1,), (1,)))
    new_right[0] = 0.5 * rs_ref[0] + 0.5 * exact(grad, grad, ((0,), (0,)))
    half_step = exact(lr_ref[0], grad, ((1,), (0,)))
    shampoo = exact(half_step, rr_ref[0], ((1,), (0,)))
    mean_square = jnp.mean(shampoo * shampoo)
    updated = ma_ref[0] - 0.5 / math.sqrt(DL) * (shampoo / jnp.sqrt(mean_square + 1e-06))
    new_master[0] = updated
    new_copy[0] = updated.astype(jnp.bfloat16)


def update_slots(blocks, lat_low, d_query, sums, left_stat, right_stat, left_root, right_root, master):
    slots = master.shape[0]
    side = DL // BLK
    spec = pl.BlockSpec((1, BLK, BLK), lambda s, block: (s, 0, 0))

    def query_block(s, block):
        return jnp.where(block[s] < PER_MATRIX, block[s], 0)

    shape = jax.ShapeDtypeStruct(master.shape, jnp.float32)
    return pl.pallas_call(
        update_body,
        grid_spec=pltpu.PrefetchScalarGridSpec(
            num_scalar_prefetch=1,
            grid=(slots,),
            in_specs=[
                pl.BlockSpec((LAT, BLK), lambda s, block: (0, query_block(s, block) // side)),
                pl.BlockSpec((LAT, BLK), lambda s, block: (0, query_block(s, block) % side)),
            ]
            + [spec] * 6,
            out_specs=[spec] * 4,
        ),
        out_shape=[shape, shape, shape, jax.ShapeDtypeStruct(master.shape, jnp.bfloat16)],
        name="update_slots",
    )(blocks, lat_low, d_query, sums, left_stat, right_stat, left_root, right_root, master)


def swap(array, axis):
    return lax.all_to_all(array, axis, 0, 0, tiled=True)


def everyone(array, axis):
    return swap(jnp.broadcast_to(array[None], (lax.axis_size(axis), *array.shape)), axis)


def near_hop(array, axis):
    size = lax.axis_size(axis)
    return lax.ppermute(array, axis, [(i, i ^ 1) for i in range(size)])


def far_hop(array, axis, step):
    size = lax.axis_size(axis)
    return lax.ppermute(array, axis, [(i, (i + 2 * step) % size) for i in range(size)])


def split_near(array, axis):
    size = lax.axis_size(axis)
    near = lax.axis_index(axis) % 2
    pairs = array.reshape(size // 2, 2, *array.shape[1:])
    return (
        lax.dynamic_index_in_dim(pairs, near, 1, False),
        lax.dynamic_index_in_dim(pairs, 1 - near, 1, False),
    )


def sum_parts(kept, sent, axis):
    size = lax.axis_size(axis)
    far = lax.axis_index(axis) // 2
    got = near_hop(sent, axis)
    kept = (kept.astype(jnp.float32) + got.astype(jnp.float32)).astype(jnp.bfloat16)
    total = lax.dynamic_index_in_dim(kept, far, 0, False).astype(jnp.float32)
    for step in range(1, size // 2):
        part = lax.dynamic_index_in_dim(kept, (far + step) % (size // 2), 0, False)
        total = total + far_hop(part, axis, step).astype(jnp.float32)
    return total


def gather_parts(array, axis):
    size = lax.axis_size(axis)
    near = lax.axis_index(axis) % 2
    far = lax.axis_index(axis) // 2
    got = [array] + [far_hop(array, axis, step) for step in range(1, size // 2)]
    got = lax.dynamic_slice_in_dim(jnp.stack(got[::-1] * 2), size // 2 - 1 - far, size // 2, 0)
    other = near_hop(got, axis)
    both = jnp.where(near == 0, jnp.stack([got, other], axis=1), jnp.stack([other, got], axis=1))
    return both.reshape(size, *array.shape)


def total_of(partial):
    rows, width = partial.shape
    n_pix = lax.axis_size("pix")
    each = -(-rows // n_pix)
    padded = jnp.pad(partial.astype(jnp.bfloat16), ((0, each * n_pix - rows), (0, 0)))
    part = jnp.sum(swap(padded.reshape(n_pix, each, width), "pix").astype(jnp.float32), axis=0)
    part = jnp.sum(everyone(part, "img"), axis=0).astype(jnp.bfloat16)
    return everyone(part, "pix").reshape(n_pix * each, width)[:rows]


def latent_pass(numerator, denominator, lat_part, cot_rows, lat_gain, w_out, w_up, w_down):
    attended = numerator / denominator[..., None]
    att_low = attended.astype(jnp.bfloat16)
    resid = lat_part[None] + product("mrd,de->mre", att_low, w_out)
    normed, normed_back = jax.vjp(standardize, resid)
    hn_low = (normed * lat_gain).astype(jnp.bfloat16)
    hidden = product("mrd,de->mre", hn_low, w_up)
    active, active_back = jax.vjp(gelu_exact, hidden)
    act_low = active.astype(jnp.bfloat16)
    latents_out = resid + product("mrd,de->mre", act_low, w_down)
    g_mlp = cot_rows.astype(jnp.bfloat16)
    d_active = product("mre,de->mrd", g_mlp, w_down)
    d_hidden = active_back(d_active)[0].astype(jnp.bfloat16)
    d_normed = product("mre,de->mrd", d_hidden, w_up)
    d_resid = cot_rows + normed_back(d_normed * lat_gain)[0]
    d_branch = d_resid.astype(jnp.bfloat16)
    d_attended = product("mre,de->mrd", d_branch, w_out)
    d_numer = d_attended / denominator[..., None]
    d_denom = -jnp.sum(d_attended * numerator / (denominator * denominator)[..., None], axis=-1)
    gain_mlp = jnp.sum(d_normed * normed, axis=(0, 1))
    row_arrays = (att_low, hn_low, act_low, d_branch, d_hidden, g_mlp)
    return (latents_out, d_numer.astype(jnp.bfloat16), d_denom, (row_arrays, gain_mlp))


def shards(
    pixels,
    sides,
    owner,
    master,
    left_stat,
    right_stat,
    left_root,
    right_root,
    kv_weight,
    latent_array,
    in_gain,
    lat_gains,
    cotangent,
):
    micro = pixels.shape[0]
    rows_dev = pixels.shape[2]
    n_pix = lax.axis_size("pix")
    n_img = lax.axis_size("img")
    img = lax.axis_index("img")
    pix = lax.axis_index("pix")
    slots_dev = master.shape[0]
    lat_rows = LAT // n_pix
    row_start = pix * lat_rows
    inv_root = 1.0 / math.sqrt(DL)

    place = jnp.concatenate([(pix * rows_dev)[None], sides * sides]).astype(jnp.int32)
    gathered = lax.all_gather(master.astype(jnp.bfloat16), ("img", "pix"), axis=0, tiled=True)
    across = lies_across(pixels)
    gain_column = in_gain[:, None]
    feats = prepare_pixels(place, across, gain_column)
    kv_low = kv_weight.astype(jnp.bfloat16)
    w_key, w_value = (kv_low[0], kv_low[1])
    lat_norm, lat_norm_back = jax.vjp(standardize, latent_array)
    lat_low, query, query_cols, w_query, w_out, w_up, w_down = make_query(
        owner, gathered, latent_array, lat_gains[0], w_key
    )

    weights, sums = attend(feats, query_cols)
    sums = sums.reshape(micro, CEXT, n_pix, lat_rows).transpose(2, 1, 0, 3)
    sums = swap(sums.reshape(n_pix, CEXT, micro * lat_rows), "pix")
    sums = jnp.sum(sums.astype(jnp.float32), axis=0)
    numer_in = sums[:CIN]
    denominator = (sums[ONES_ROW] + sums[ONES_ROW + 1]).reshape(micro, lat_rows)
    numerator = fine("cr,cd->rd", numer_in, w_value).reshape(micro, lat_rows, DL)
    latents_out, d_numer, d_denom, latent_grads = latent_pass(
        numerator,
        denominator,
        lax.dynamic_slice_in_dim(latent_array, row_start, lat_rows, 0),
        cotangent[:, 0],
        lat_gains[1],
        w_out,
        w_up,
        w_down,
    )
    row_arrays, gain_mlp = latent_grads
    d_numer = d_numer.reshape(micro * lat_rows, DL)
    head, rest = two_terms(d_denom.reshape(1, micro * lat_rows))
    d_cols = product("rd,cd->cr", d_numer, w_value).astype(jnp.bfloat16)
    d_cols = jnp.concatenate([d_cols, head, rest, jnp.zeros_like(head)], axis=0)
    d_cols = everyone(d_cols, "pix").reshape(n_pix, CEXT, micro, lat_rows)
    d_cols = d_cols.transpose(2, 1, 0, 3).reshape(micro, CEXT, LAT)

    numer_rows = jnp.pad(numer_in.astype(jnp.bfloat16).T, ((0, 0), (0, DL - CIN)))
    own = jnp.stack(
        [array.reshape(micro * lat_rows, DL) for array in row_arrays] + [d_numer, numer_rows]
    )
    mate = [(i, i ^ 1) for i in range(n_img)]
    pieces = [own, lax.ppermute(own, "img", mate)]
    images = [img, img ^ 1]
    far = []
    for step in range(1, n_img // 2):
        hop = [(i, (i + 2 * step) % n_img) for i in range(n_img)]
        far.append(lax.ppermute(own, "img", hop))
        images += [(img - 2 * step) % n_img, (img - 2 * step) % n_img ^ 1]
    device_of = owner // slots_dev
    place_of = device_of % n_pix * slots_dev + owner % slots_dev
    where = jnp.where(device_of // n_pix == img, place_of, -1)

    results = (None,)
    score_sum = jnp.zeros((CEXT, LAT), jnp.float32)
    gain_sum = jnp.zeros((CIN, 1), jnp.float32)
    width = DL // n_img
    each = -(-CEXT // n_pix)
    parts = parts_of(feats)
    for at, part in enumerate(parts):
        if at == len(parts) - 2:
            far, gain_sum = lax.optimization_barrier((far, gain_sum))
            for piece in far:
                pieces += [piece, lax.ppermute(piece, "img", mate)]
        if at == len(parts) - 1:
            pieces, gain_sum = lax.optimization_barrier((pieces, gain_sum))
            where = jnp.concatenate([jnp.stack(images), where]).astype(jnp.int32)
            grads, value_part, resid_part = image_sums(where, pieces, lat_rows)
            value_part = jnp.pad(value_part, ((0, each * n_pix - CEXT), (0, 0)))
            value_part = lax.dynamic_slice_in_dim(value_part, img * width, width, 1)
            value_sides = split_near(value_part.reshape(n_pix, each, width), "pix")
            grad_sides = split_near(grads.reshape(n_pix, slots_dev, BLK, BLK), "pix")
            gain_column, value_sides, grad_sides = lax.optimization_barrier(
                (gain_column, value_sides, grad_sides)
            )
        results = attend_back(
            part, results[0], across, feats, weights, gain_column, d_cols, query_cols
        )
        score_sum = score_sum + results[1]
        gain_sum = gain_sum + results[2]
    pixel_grad = jnp.swapaxes(results[0].reshape(micro, 1, CIN, rows_dev), 2, 3)

    value_part = sum_parts(*value_sides, "pix").astype(jnp.bfloat16)
    resid_part = lax.dynamic_slice_in_dim(resid_part, img * width, width, 1)
    early = gather_parts(jnp.concatenate([value_part, resid_part], axis=0), "pix")
    early = gather_parts(early, "img").transpose(1, 2, 0, 3).reshape(n_pix, each + lat_rows, DL)
    value_total = early[:, :each].reshape(n_pix * each, DL)[:CIN].astype(jnp.float32)
    resid_total = early[:, each:].reshape(LAT, DL)

    late = jnp.concatenate(
        [
            score_sum[:CIN],
            jnp.pad(gain_sum.T, ((0, 0), (0, LAT - CIN))),
            gain_mlp.reshape(DL // LAT, LAT),
        ],
        axis=0,
    )
    late_total = total_of(late)
    score_total = late_total[:CIN]
    in_gain_grad = late_total[CIN, :CIN].astype(jnp.float32)
    gain_mlp_total = late_total[CIN + 1 :].reshape(DL).astype(jnp.float32)

    grads = sum_parts(*grad_sides, "pix")

    d_query = (contract_rows(score_total, w_key) * inv_root).astype(jnp.bfloat16)
    key_total = dot(score_total, query) * inv_root
    kv_grad = jnp.stack([key_total, value_total])
    d_lat_norm = product("le,de->ld", d_query, w_query)
    latent_grad = resid_total.astype(jnp.float32) + lat_norm_back(d_lat_norm * lat_gains[0])[0]
    lat_gain_grad = jnp.stack([jnp.sum(d_lat_norm * lat_norm, axis=0), gain_mlp_total])

    mine = (img * n_pix + pix) * slots_dev + jnp.arange(slots_dev, dtype=jnp.int32)
    blocks = jnp.sum(
        jnp.where(owner[None] == mine[:, None], jnp.arange(NBLK, dtype=jnp.int32)[None], 0), axis=1
    )
    new_left, new_right, new_master, new_copy = update_slots(
        blocks.astype(jnp.int32),
        lat_low,
        d_query,
        grads,
        left_stat,
        right_stat,
        left_root,
        right_root,
        master,
    )
    new_kv = kv_weight - 0.3 / math.sqrt(CIN) * normalized(kv_grad, (1, 2))
    new_latent = latent_array - 0.3 * normalized(latent_grad, (0, 1))
    new_in_gain = in_gain - 0.2 * normalized(in_gain_grad, (0,))
    new_lat_gains = lat_gains - 0.2 * normalized(lat_gain_grad, (1,))
    return (
        latents_out[:, None],
        pixel_grad,
        new_left,
        new_right,
        new_master,
        new_copy,
        kv_grad,
        new_kv,
        latent_grad,
        new_latent,
        in_gain_grad,
        new_in_gain,
        lat_gain_grad,
        new_lat_gains,
    )


def solution(mesh):
    pixel_spec = P(None, "img", "pix", None)
    slot_spec = P(("img", "pix"), None, None)
    in_specs = (
        (pixel_spec, P(), P()) + (slot_spec,) * 5 + (P(),) * 4 + (pixel_spec,)
    )
    out_specs = (pixel_spec, pixel_spec) + (slot_spec,) * 4 + (P(),) * 8
    return jax.shard_map(shards, mesh=mesh, in_specs=in_specs, out_specs=out_specs, check_vma=False)
```

```python
import functools
import math

import jax
import jax.numpy as jnp
from jax import lax
from jax.experimental import pallas as pl
from jax.experimental.pallas import tpu as pltpu
from jax.sharding import PartitionSpec as P

CIN = 261
DL = 1024
LAT = 512
BLK = 128
NBLK = 256
PER_MATRIX = NBLK // 4
CEXT = 264
ONES_ROW = 261
MASK_ROW = 263
MASKED = -1e30

HIGHEST_PRECISION = lax.Precision.HIGHEST


def standardize(values_in):
    average = jnp.mean(values_in, axis=-1, keepdims=True)
    centred = values_in - average
    variance = jnp.mean(centred * centred, axis=-1, keepdims=True)
    return centred * lax.rsqrt(variance + 1e-05)


def gelu_exact(values_in):
    return jax.nn.gelu(values_in, approximate=False)


def normalized(gradient, reduce_axes):
    return gradient / jnp.sqrt(
        jnp.mean(gradient * gradient, axis=reduce_axes, keepdims=True) + 1e-06
    )


def product(pattern, left_side, right_side):
    return jnp.einsum(pattern, left_side, right_side, preferred_element_type=jnp.float32)


def fine(pattern, left_side, right_side):
    return jnp.einsum(
        pattern,
        left_side.astype(jnp.float32),
        right_side.astype(jnp.float32),
        precision=HIGHEST_PRECISION,
    )


def two_terms(values_in):
    head = lax.reduce_precision(values_in, 8, 7)
    return (head.astype(jnp.bfloat16), (values_in - head).astype(jnp.bfloat16))


def contract_rows(left_side, right_side, precision=None):
    return lax.dot_general(
        left_side,
        right_side,
        (((0,), (0,)), ((), ())),
        precision=precision,
        preferred_element_type=jnp.float32,
    )


def dot(left_side, right_side):
    return jnp.dot(left_side, right_side, preferred_element_type=jnp.float32)


def dot_last(left_side, right_side):
    return lax.dot_general(
        left_side, right_side, (((1,), (1,)), ((), ())), preferred_element_type=jnp.float32
    )


def tile_of(rows, most):
    return max((size for size in range(128, most + 1, 128) if rows % size == 0), default=rows)


def lies_across(pixels):
    micro, _, rows_dev, _ = pixels.shape
    return jnp.swapaxes(pixels, 2, 3).reshape(micro, CIN, 1, rows_dev)


def centre(pix):
    centred = pix - jnp.mean(pix, axis=0, keepdims=True)
    scale = lax.rsqrt(jnp.mean(centred * centred, axis=0, keepdims=True) + 1e-05)
    return (centred * scale, scale)


def cost(flops, count):
    return pl.CostEstimate(flops=int(flops), bytes_accessed=int(count), transcendentals=0)


def prepare_body(place_ref, pix_ref, gain_ref, *rest, micro_index):
    out_ref = rest[-1]
    normed, _ = centre(pix_ref[0, :, 0, :])
    columns = normed.shape[1]
    extra = (CEXT - CIN, columns)
    slot = place_ref[0] + pl.program_id(0) * columns + lax.broadcasted_iota(jnp.int32, extra, 1)
    row = lax.broadcasted_iota(jnp.int32, extra, 0) + CIN
    mask = jnp.where(slot < place_ref[1 + micro_index], 0.0, MASKED)
    tail = jnp.where(row == MASK_ROW, mask, 1.0)
    out_ref[0] = jnp.concatenate([normed * gain_ref[...], tail], axis=0).astype(jnp.bfloat16)


def prepare_pixels(micro_index, earlier, place, across, gain_column):
    micro, _, _, rows_dev = across.shape
    rows = tile_of(rows_dev, 1152)
    m = micro_index
    in_specs = [
        pl.BlockSpec(memory_space=pltpu.SMEM),
        pl.BlockSpec((1, CIN, 1, rows), lambda t: (m, 0, 0, t)),
        pl.BlockSpec((CIN, 1), lambda t: (0, 0)),
    ]
    operands = [place, across, gain_column]
    aliases = {}
    if earlier is not None:
        in_specs.append(pl.BlockSpec(memory_space=pl.ANY))
        aliases = {len(operands): 0}
        operands.append(earlier)
    return pl.pallas_call(
        functools.partial(prepare_body, micro_index=m),
        grid=(rows_dev // rows,),
        in_specs=in_specs,
        out_specs=pl.BlockSpec((1, CEXT, rows), lambda t: (m, 0, t)),
        out_shape=jax.ShapeDtypeStruct((micro, CEXT, rows_dev), jnp.bfloat16),
        input_output_aliases=aliases,
        cost_estimate=cost(0, 12 * rows_dev * CEXT),
        name="prepare_pixels",
    )(*operands)


def attend_body(feat_ref, query_ref, exp_ref, out_ref, sum_ref):
    tile = pl.program_id(1)
    feats = feat_ref[0]
    weights = jnp.exp(contract_rows(feats, query_ref[...])).astype(jnp.bfloat16)
    exp_ref[0] = weights

    @pl.when(tile == 0)
    def _():
        sum_ref[...] = jnp.zeros_like(sum_ref)

    sum_ref[...] += dot(feats, weights)

    @pl.when(tile == pl.num_programs(1) - 1)
    def _():
        sums = sum_ref[...]
        low = sums.astype(jnp.bfloat16)
        rest = (sums - low.astype(jnp.float32))[ONES_ROW : ONES_ROW + 1]
        row = lax.broadcasted_iota(jnp.int32, sums.shape, 0)
        out_ref[0] = jnp.where(row == ONES_ROW + 1, rest, sums).astype(jnp.bfloat16)


def attend(feats, query_cols):
    micro, _, rows_dev = feats.shape
    rows = tile_of(rows_dev, 1152)
    return pl.pallas_call(
        attend_body,
        grid=(micro, rows_dev // rows),
        in_specs=[
            pl.BlockSpec((1, CEXT, rows), lambda m, t: (m, 0, t)),
            pl.BlockSpec((CEXT, LAT), lambda m, t: (0, 0)),
        ],
        out_specs=[
            pl.BlockSpec((1, rows, LAT), lambda m, t: (m, t, 0)),
            pl.BlockSpec((1, CEXT, LAT), lambda m, t: (m, 0, 0)),
        ],
        out_shape=[
            jax.ShapeDtypeStruct((micro, rows_dev, LAT), jnp.bfloat16),
            jax.ShapeDtypeStruct((micro, CEXT, LAT), jnp.bfloat16),
        ],
        scratch_shapes=[pltpu.VMEM((CEXT, LAT), jnp.float32)],
        cost_estimate=cost(8 * micro * rows_dev * LAT * CEXT, 4 * micro * rows_dev * LAT),
        name="attend",
    )(feats, query_cols)


def tiles_of(feats):
    rows_dev = feats.shape[2]
    return rows_dev // tile_of(rows_dev, 1152)


def parts_of(feats):
    micro = feats.shape[0]
    tiles = tiles_of(feats)
    parts = []
    for m in range(micro):
        head = max(tiles // 3 if m == micro - 1 else tiles - tiles // 2, 1)
        parts.append((m, 0, head))
        if head < tiles:
            parts.append((m, head, tiles - head))
    return parts


def attend_back_body(pix_ref, feat_ref, exp_ref, gain_ref, dc_ref, qc_ref, *rest):
    grad_ref, score_ref, gain_sum_ref = rest[-3:]
    feats = feat_ref[0]
    weights = exp_ref[0]
    d_exp = contract_rows(feats, dc_ref[0])
    d_scores = (weights.astype(jnp.float32) * d_exp).astype(jnp.bfloat16)

    @pl.when(pl.program_id(0) == 0)
    def _():
        score_ref[...] = jnp.zeros_like(score_ref)
        gain_sum_ref[...] = jnp.zeros_like(gain_sum_ref)

    score_ref[...] += dot(feats, d_scores)
    d_pix = (dot_last(qc_ref[...], d_scores) + dot_last(dc_ref[0], weights))[:CIN]
    normed, scale = centre(pix_ref[0, :, 0, :])
    gain_sum_ref[...] += jnp.sum(d_pix * normed, axis=1, keepdims=True)
    d_normed = d_pix * gain_ref[...]
    along = jnp.mean(d_normed * normed, axis=0, keepdims=True)
    level = jnp.mean(d_normed, axis=0, keepdims=True)
    grad_ref[0, :, 0, :] = (d_normed - level - normed * along) * scale


def attend_back(part, earlier, across, feats, weights, gain_column, d_cols, query_cols):
    m, first, tiles = part
    rows = feats.shape[2] // tiles_of(feats)
    in_specs = [
        pl.BlockSpec((1, CIN, 1, rows), lambda t: (m, 0, 0, first + t)),
        pl.BlockSpec((1, CEXT, rows), lambda t: (m, 0, first + t)),
        pl.BlockSpec((1, rows, LAT), lambda t: (m, first + t, 0)),
        pl.BlockSpec((CIN, 1), lambda t: (0, 0)),
        pl.BlockSpec((1, CEXT, LAT), lambda t: (m, 0, 0)),
        pl.BlockSpec((CEXT, LAT), lambda t: (0, 0)),
    ]
    operands = [across, feats, weights, gain_column, d_cols, query_cols]
    aliases = {}
    if earlier is not None:
        in_specs.append(pl.BlockSpec(memory_space=pl.ANY))
        aliases = {len(operands): 0}
        operands.append(earlier)
    return pl.pallas_call(
        attend_back_body,
        grid=(tiles,),
        in_specs=in_specs,
        out_specs=[
            pl.BlockSpec((1, CIN, 1, rows), lambda t: (m, 0, 0, first + t)),
            pl.BlockSpec((CEXT, LAT), lambda t: (0, 0)),
            pl.BlockSpec((CIN, 1), lambda t: (0, 0)),
        ],
        out_shape=[
            jax.ShapeDtypeStruct(across.shape, jnp.float32),
            jax.ShapeDtypeStruct((CEXT, LAT), jnp.float32),
            jax.ShapeDtypeStruct((CIN, 1), jnp.float32),
        ],
        input_output_aliases=aliases,
        cost_estimate=cost(16 * tiles * rows * LAT * CEXT, tiles * rows * 4000),
        name="attend_back",
    )(*operands)


def query_body(block_ref, lat_ref, gain_ref, key_ref, *rest):
    sources, (low_ref, query_ref, cols_ref, wq_ref, wo_ref, w1_ref, w2_ref, sems) = (
        rest[:-8],
        rest[-8:],
    )
    squares = (wq_ref, wo_ref, w1_ref, w2_ref)
    side = DL // BLK
    first = 0
    for source in sources:

        @pl.loop(0, source.shape[0])
        def _(at, source=source, first=first):
            block = block_ref[first + at]
            row = pl.multiple_of((block % PER_MATRIX // side) * BLK, BLK)
            column = pl.multiple_of((block % side) * BLK, BLK)
            for matrix in range(4):

                @pl.when(block // PER_MATRIX == matrix)
                def _(matrix=matrix):
                    pltpu.make_async_copy(
                        source.at[at],
                        squares[matrix].at[pl.ds(row, BLK), pl.ds(column, BLK)],
                        sems.at[matrix],
                    ).start()

        first += source.shape[0]

    def settle(matrix):
        pltpu.make_async_copy(squares[matrix], squares[matrix], sems.at[matrix]).wait()

    lat_low = (standardize(lat_ref[...]) * gain_ref[...]).astype(jnp.bfloat16)
    low_ref[...] = lat_low
    settle(0)
    query = dot(lat_low, wq_ref[...]).astype(jnp.bfloat16)
    query_ref[...] = query
    scores = dot_last(key_ref[...], query) * (1.0 / math.sqrt(DL))
    row = lax.broadcasted_iota(jnp.int32, (CEXT - CIN, LAT), 0) + CIN
    tail = jnp.where(row == MASK_ROW, 1.0, 0.0)
    cols_ref[...] = jnp.concatenate([scores, tail], axis=0).astype(jnp.bfloat16)
    for matrix in range(1, 4):
        settle(matrix)


def make_query(blocks, sources, latent_array, gain, w_key):
    vmem = pl.BlockSpec(memory_space=pltpu.VMEM)
    hbm = pl.BlockSpec(memory_space=pl.ANY)
    rows = jax.ShapeDtypeStruct((LAT, DL), jnp.bfloat16)
    square = jax.ShapeDtypeStruct((DL, DL), jnp.bfloat16)
    return pl.pallas_call(
        query_body,
        in_specs=[pl.BlockSpec(memory_space=pltpu.SMEM), vmem, vmem, vmem] + [hbm] * len(sources),
        out_specs=[vmem] * 7,
        out_shape=[rows, rows, jax.ShapeDtypeStruct((CEXT, LAT), jnp.bfloat16)] + [square] * 4,
        scratch_shapes=[pltpu.SemaphoreType.DMA((4,))],
        cost_estimate=cost(3 * LAT * DL * DL, 4 * NBLK * BLK * BLK),
        name="make_query",
    )(blocks, latent_array, gain[None], w_key, *sources)


def image_sums_body(where_ref, *rest):
    n_img = len(rest) - 7
    pieces, (grads_ref, value_ref, resid_ref, rows_ref, full_ref, zero_ref, sems) = (
        rest[:n_img],
        rest[n_img:],
    )
    side = DL // BLK
    count = pieces[0].shape[1]

    def put(source, block):
        place = where_ref[n_img + block]

        @pl.when(place >= 0)
        def _():
            pltpu.make_async_copy(source, grads_ref.at[place], sems.at[1]).start()

    for piece in range(n_img):
        first = pl.multiple_of(where_ref[piece] * count, count)
        pltpu.make_async_copy(
            pieces[piece], rows_ref.at[:, pl.ds(first, count), :], sems.at[0]
        ).start()
    zero_ref[...] = jnp.zeros_like(zero_ref)

    @pl.loop(0, PER_MATRIX)
    def _(block):
        put(zero_ref, block)

    pltpu.make_async_copy(rows_ref, rows_ref, sems.at[0]).wait()
    for matrix in range(3):
        full_ref[matrix] = contract_rows(rows_ref[matrix], rows_ref[3 + matrix]).astype(jnp.bfloat16)

        @pl.loop(0, PER_MATRIX)
        def _(block, matrix=matrix):
            row = pl.multiple_of((block // side) * BLK, BLK)
            column = pl.multiple_of((block % side) * BLK, BLK)
            put(
                full_ref.at[matrix, pl.ds(row, BLK), pl.ds(column, BLK)],
                (matrix + 1) * PER_MATRIX + block,
            )

    value_ref[...] = contract_rows(rows_ref[7, :, :CEXT], rows_ref[6]).astype(jnp.bfloat16)
    each = resid_ref.shape[0]
    total = rows_ref[3, :each, :].astype(jnp.float32)
    for first in range(each, rows_ref.shape[1], each):
        total = total + rows_ref[3, first : first + each, :].astype(jnp.float32)
    resid_ref[...] = total.astype(jnp.bfloat16)
    pltpu.make_async_copy(grads_ref, grads_ref, sems.at[1]).wait()


def image_sums(where, pieces, lat_rows):
    n_img = len(pieces)
    slabs, count, _ = pieces[0].shape
    hbm = pl.BlockSpec(memory_space=pl.ANY)
    vmem = pl.BlockSpec(memory_space=pltpu.VMEM)
    return pl.pallas_call(
        image_sums_body,
        in_specs=[pl.BlockSpec(memory_space=pltpu.SMEM)] + [hbm] * n_img,
        out_specs=[hbm, vmem, vmem],
        out_shape=[
            jax.ShapeDtypeStruct((NBLK // n_img, BLK, BLK), jnp.bfloat16),
            jax.ShapeDtypeStruct((CEXT, DL), jnp.bfloat16),
            jax.ShapeDtypeStruct((lat_rows, DL), jnp.bfloat16),
        ],
        scratch_shapes=[
            pltpu.VMEM((slabs, n_img * count, DL), jnp.bfloat16),
            pltpu.VMEM((3, DL, DL), jnp.bfloat16),
            pltpu.VMEM((BLK, BLK), jnp.bfloat16),
            pltpu.SemaphoreType.DMA((2,)),
        ],
        cost_estimate=cost(8 * n_img * count * DL * DL, 16 * DL * DL),
        name="image_sums",
    )(where, *pieces)


def update_body(block_ref, lat_ref, dq_ref, sum_ref, ls_ref, rs_ref, lr_ref, rr_ref, ma_ref, *outs):
    new_left, new_right, new_master, new_copy = outs

    def exact(left_side, right_side, dims):
        return lax.dot_general(
            left_side,
            right_side,
            (dims, ((), ())),
            precision=HIGHEST_PRECISION,
            preferred_element_type=jnp.float32,
        )

    is_query = block_ref[pl.program_id(0)] < PER_MATRIX
    grad = jnp.where(is_query, contract_rows(lat_ref[...], dq_ref[...]), sum_ref[0])
    new_left[0] = 0.5 * ls_ref[0] + 0.5 * exact(grad, grad, ((1,), (1,)))
    new_right[0] = 0.5 * rs_ref[0] + 0.5 * exact(grad, grad, ((0,), (0,)))
    half_step = exact(lr_ref[0], grad, ((1,), (0,)))
    shampoo = exact(half_step, rr_ref[0], ((1,), (0,)))
    mean_square = jnp.mean(shampoo * shampoo)
    updated = ma_ref[0] - 0.5 / math.sqrt(DL) * (shampoo / jnp.sqrt(mean_square + 1e-06))
    new_master[0] = updated
    new_copy[0] = updated.astype(jnp.bfloat16)


def update_slots(blocks, lat_low, d_query, sums, left_stat, right_stat, left_root, right_root, master):
    slots = master.shape[0]
    side = DL // BLK
    spec = pl.BlockSpec((1, BLK, BLK), lambda s, block: (s, 0, 0))

    def query_block(s, block):
        return jnp.where(block[s] < PER_MATRIX, block[s], 0)

    shape = jax.ShapeDtypeStruct(master.shape, jnp.float32)
    return pl.pallas_call(
        update_body,
        grid_spec=pltpu.PrefetchScalarGridSpec(
            num_scalar_prefetch=1,
            grid=(slots,),
            in_specs=[
                pl.BlockSpec((LAT, BLK), lambda s, block: (0, query_block(s, block) // side)),
                pl.BlockSpec((LAT, BLK), lambda s, block: (0, query_block(s, block) % side)),
            ]
            + [spec] * 6,
            out_specs=[spec] * 4,
        ),
        out_shape=[shape, shape, shape, jax.ShapeDtypeStruct(master.shape, jnp.bfloat16)],
        name="update_slots",
    )(blocks, lat_low, d_query, sums, left_stat, right_stat, left_root, right_root, master)


def swap(array, axis):
    return lax.all_to_all(array, axis, 0, 0, tiled=True)


def everyone(array, axis):
    return swap(jnp.broadcast_to(array[None], (lax.axis_size(axis), *array.shape)), axis)


def near_hop(array, axis):
    size = lax.axis_size(axis)
    return lax.ppermute(array, axis, [(i, i ^ 1) for i in range(size)])


def far_hop(array, axis, step):
    size = lax.axis_size(axis)
    return lax.ppermute(array, axis, [(i, (i + 2 * step) % size) for i in range(size)])


def spread(array, slots, axis, hops):
    size = lax.axis_size(axis)
    got = [array]
    moves = [lambda i: i]
    if hops == "near":
        got.append(near_hop(array, axis))
        moves.append(lambda i: i ^ 1)
    else:
        for step in range(1, size // 2):
            got.append(far_hop(array, axis, step))
            moves.append(lambda i, step=step: (i - 2 * step) % size)

    def slots_after(img, pix):
        return jnp.concatenate(
            [slots(move(img), pix) if axis == "img" else slots(img, move(pix)) for move in moves]
        )

    return (jnp.concatenate(got), slots_after)


ROUTES = (
    (("pix", "near"), ("img", "far"), ("pix", "far")),
    (("img", "far"), ("pix", "far"), ("pix", "near")),
    (("pix", "far"), ("pix", "near"), ("img", "far")),
)


def gather_blocks(low, feats):
    slots_dev = low.shape[0]
    n_pix = lax.axis_size("pix")
    if slots_dev < 4 or n_pix > 8:
        low = lax.all_gather(low, ("img", "pix"), axis=0, tiled=True)
        return ([low], jnp.arange(NBLK), feats)
    quarter = slots_dev // 4
    states = []
    bounds = (0, quarter, 2 * quarter, slots_dev)
    for part in range(3):
        start, stop = bounds[part], bounds[part + 1]

        def slots(img, pix, start=start, stop=stop):
            return (img * n_pix + pix) * slots_dev + jnp.arange(start, stop)

        states.append((low[start:stop], slots))
    for phase in range(3):
        states = [spread(*state, *ROUTES[part][phase]) for part, state in enumerate(states)]
    img = lax.axis_index("img")
    pix = lax.axis_index("pix")
    arrays = []
    order = []
    held, feats = lax.optimization_barrier(([array for array, _ in states], feats))
    for array, (_, slots) in zip(held, states):
        arrays += [array, near_hop(array, "img")]
        order += [slots(img, pix), slots(img ^ 1, pix)]
    return (arrays, jnp.concatenate(order), feats)


def split_near(array, axis):
    size = lax.axis_size(axis)
    near = lax.axis_index(axis) % 2
    pairs = array.reshape(size // 2, 2, *array.shape[1:])
    return (
        lax.dynamic_index_in_dim(pairs, near, 1, False),
        lax.dynamic_index_in_dim(pairs, 1 - near, 1, False),
    )


def join_near(kept, sent, axis):
    got = near_hop(sent, axis)
    return (kept.astype(jnp.float32) + got.astype(jnp.float32)).astype(jnp.bfloat16)


def sum_far(kept, axis):
    size = lax.axis_size(axis)
    far = lax.axis_index(axis) // 2
    total = lax.dynamic_index_in_dim(kept, far, 0, False).astype(jnp.float32)
    for step in range(1, size // 2):
        part = lax.dynamic_index_in_dim(kept, (far + step) % (size // 2), 0, False)
        total = total + far_hop(part, axis, step).astype(jnp.float32)
    return total


def gather_far(array, axis):
    size = lax.axis_size(axis)
    far = lax.axis_index(axis) // 2
    got = [array] + [far_hop(array, axis, step) for step in range(1, size // 2)]
    return lax.dynamic_slice_in_dim(jnp.stack(got[::-1] * 2), size // 2 - 1 - far, size // 2, 0)


def gather_near(array, axis):
    near = lax.axis_index(axis) % 2
    other = near_hop(array, axis)
    both = jnp.where(
        near == 0, jnp.stack([array, other], axis=1), jnp.stack([other, array], axis=1)
    )
    return both.reshape(lax.axis_size(axis), *array.shape[1:])


def latent_pass(numerator, denominator, lat_part, cot_rows, lat_gain, w_out, w_up, w_down):
    attended = numerator / denominator[..., None]
    att_low = attended.astype(jnp.bfloat16)
    resid = lat_part[None] + product("mrd,de->mre", att_low, w_out)
    normed, normed_back = jax.vjp(standardize, resid)
    hn_low = (normed * lat_gain).astype(jnp.bfloat16)
    hidden = product("mrd,de->mre", hn_low, w_up)
    active, active_back = jax.vjp(gelu_exact, hidden)
    act_low = active.astype(jnp.bfloat16)
    latents_out = resid + product("mrd,de->mre", act_low, w_down)
    g_mlp = cot_rows.astype(jnp.bfloat16)
    d_active = product("mre,de->mrd", g_mlp, w_down)
    d_hidden = active_back(d_active)[0].astype(jnp.bfloat16)
    d_normed = product("mre,de->mrd", d_hidden, w_up)
    d_resid = cot_rows + normed_back(d_normed * lat_gain)[0]
    d_branch = d_resid.astype(jnp.bfloat16)
    d_attended = product("mre,de->mrd", d_branch, w_out)
    d_numer = d_attended / denominator[..., None]
    d_denom = -jnp.sum(d_attended * numerator / (denominator * denominator)[..., None], axis=-1)
    gain_mlp = jnp.sum(d_normed * normed, axis=(0, 1))
    row_arrays = (att_low, hn_low, act_low, d_branch, d_hidden, g_mlp)
    return (latents_out, d_numer.astype(jnp.bfloat16), d_denom, (row_arrays, gain_mlp))


def shards(
    pixels,
    sides,
    owner,
    master,
    left_stat,
    right_stat,
    left_root,
    right_root,
    kv_weight,
    latent_array,
    in_gain,
    lat_gains,
    cotangent,
):
    micro = pixels.shape[0]
    rows_dev = pixels.shape[2]
    n_pix = lax.axis_size("pix")
    n_img = lax.axis_size("img")
    img = lax.axis_index("img")
    pix = lax.axis_index("pix")
    slots_dev = master.shape[0]
    lat_rows = LAT // n_pix
    row_start = pix * lat_rows
    inv_root = 1.0 / math.sqrt(DL)

    place = jnp.concatenate([(pix * rows_dev)[None], sides * sides]).astype(jnp.int32)
    across = lies_across(pixels)
    gain_column = in_gain[:, None]
    feats = None
    for micro_index in range(micro - 1):
        feats = prepare_pixels(micro_index, feats, place, across, gain_column)
    sources, source_slots, feats = gather_blocks(master.astype(jnp.bfloat16), feats)
    feats = prepare_pixels(micro - 1, feats, place, across, gain_column)
    all_blocks = jnp.arange(NBLK, dtype=jnp.int32)
    source_blocks = jnp.sum(
        jnp.where(source_slots[:, None] == owner[None], all_blocks[None], 0), axis=1
    )
    kv_low = kv_weight.astype(jnp.bfloat16)
    w_key, w_value = (kv_low[0], kv_low[1])
    lat_norm, lat_norm_back = jax.vjp(standardize, latent_array)
    lat_low, query, query_cols, w_query, w_out, w_up, w_down = make_query(
        source_blocks.astype(jnp.int32), sources, latent_array, lat_gains[0], w_key
    )

    weights, sums = attend(feats, query_cols)
    sums = sums.reshape(micro, CEXT, n_pix, lat_rows).transpose(2, 1, 0, 3)
    sums = swap(sums.reshape(n_pix, CEXT, micro * lat_rows), "pix")
    sums = jnp.sum(sums.astype(jnp.float32), axis=0)
    numer_in = sums[:CIN]
    denominator = (sums[ONES_ROW] + sums[ONES_ROW + 1]).reshape(micro, lat_rows)
    numerator = fine("cr,cd->rd", numer_in, w_value).reshape(micro, lat_rows, DL)
    latents_out, d_numer, d_denom, latent_grads = latent_pass(
        numerator,
        denominator,
        lax.dynamic_slice_in_dim(latent_array, row_start, lat_rows, 0),
        cotangent[:, 0],
        lat_gains[1],
        w_out,
        w_up,
        w_down,
    )
    row_arrays, gain_mlp = latent_grads
    d_numer = d_numer.reshape(micro * lat_rows, DL)
    head, rest = two_terms(d_denom.reshape(1, micro * lat_rows))
    d_cols = product("rd,cd->cr", d_numer, w_value).astype(jnp.bfloat16)
    d_cols = jnp.concatenate([d_cols, head, rest, jnp.zeros_like(head)], axis=0)
    d_cols = everyone(d_cols, "pix").reshape(n_pix, CEXT, micro, lat_rows)
    d_cols = d_cols.transpose(2, 1, 0, 3).reshape(micro, CEXT, LAT)

    numer_rows = jnp.pad(numer_in.astype(jnp.bfloat16).T, ((0, 0), (0, DL - CIN)))
    own = jnp.stack(
        [array.reshape(micro * lat_rows, DL) for array in row_arrays] + [d_numer, numer_rows]
    )
    mate = [(i, i ^ 1) for i in range(n_img)]
    pieces = [own, lax.ppermute(own, "img", mate)]
    images = [img, img ^ 1]
    far = []
    for step in range(1, n_img // 2):
        hop = [(i, (i + 2 * step) % n_img) for i in range(n_img)]
        far.append(lax.ppermute(own, "img", hop))
        images += [(img - 2 * step) % n_img, (img - 2 * step) % n_img ^ 1]
    device_of = owner // slots_dev
    place_of = device_of % n_pix * slots_dev + owner % slots_dev
    where = jnp.where(device_of // n_pix == img, place_of, -1)

    results = (None,)
    score_sum = jnp.zeros((CEXT, LAT), jnp.float32)
    gain_sum = jnp.zeros((CIN, 1), jnp.float32)
    width = DL // n_img
    each = -(-CEXT // n_pix)
    parts = parts_of(feats)
    for at, part in enumerate(parts):
        if at == len(parts) - 2:
            far, gain_sum = lax.optimization_barrier((far, gain_sum))
            for piece in far:
                pieces += [piece, lax.ppermute(piece, "img", mate)]
        if at == len(parts) - 1:
            pieces, gain_sum = lax.optimization_barrier((pieces, gain_sum))
            where = jnp.concatenate([jnp.stack(images), where]).astype(jnp.int32)
            grads, value_part, resid_part = image_sums(where, pieces, lat_rows)
            value_part = jnp.pad(value_part, ((0, each * n_pix - CEXT), (0, 0)))
            value_part = lax.dynamic_slice_in_dim(value_part, img * width, width, 1)
            value_sides = split_near(value_part.reshape(n_pix, each, width), "pix")
            grad_sides = split_near(grads.reshape(n_pix, slots_dev, BLK, BLK), "pix")
            gain_column, value_sides, grad_sides = lax.optimization_barrier(
                (gain_column, value_sides, grad_sides)
            )
        results = attend_back(
            part, results[0], across, feats, weights, gain_column, d_cols, query_cols
        )
        score_sum = score_sum + results[1]
        gain_sum = gain_sum + results[2]
    pixel_grad = jnp.swapaxes(results[0].reshape(micro, 1, CIN, rows_dev), 2, 3)

    late = jnp.concatenate(
        [
            score_sum[:CIN],
            jnp.pad(gain_sum.T, ((0, 0), (0, LAT - CIN))),
            gain_mlp.reshape(DL // LAT, LAT),
        ],
        axis=0,
    ).astype(jnp.bfloat16)
    late = jnp.pad(late, ((0, each * n_pix - CEXT), (0, 0))).reshape(n_pix, each, LAT)
    late = jnp.sum(swap(late, "pix").astype(jnp.float32), axis=0)
    value_part = join_near(*value_sides, "pix")
    grads = join_near(*grad_sides, "pix")
    late, value_part, grads = lax.optimization_barrier((late, value_part, grads))
    late = jnp.sum(everyone(late, "img"), axis=0).astype(jnp.bfloat16)
    value_part = sum_far(value_part, "pix").astype(jnp.bfloat16)
    late, value_part = lax.optimization_barrier((late, value_part))
    late_total = everyone(late, "pix").reshape(n_pix * each, LAT)
    grads = sum_far(grads, "pix")
    resid_part = lax.dynamic_slice_in_dim(resid_part, img * width, width, 1)
    early = gather_far(jnp.concatenate([value_part, resid_part], axis=0), "pix")
    score_total, early, grads = lax.optimization_barrier((late_total[:CIN], early, grads))
    in_gain_grad = late_total[CIN, :CIN].astype(jnp.float32)
    gain_mlp_total = late_total[CIN + 1 : CEXT].reshape(DL).astype(jnp.float32)
    early = gather_near(early, "pix")
    early = gather_near(gather_far(early, "img"), "img")
    early = early.transpose(1, 2, 0, 3).reshape(n_pix, each + lat_rows, DL)
    value_total = early[:, :each].reshape(n_pix * each, DL)[:CIN].astype(jnp.float32)
    resid_total = early[:, each:].reshape(LAT, DL)

    d_query = (contract_rows(score_total, w_key) * inv_root).astype(jnp.bfloat16)
    key_total = dot(score_total, query) * inv_root
    kv_grad = jnp.stack([key_total, value_total])
    d_lat_norm = product("le,de->ld", d_query, w_query)
    latent_grad = resid_total.astype(jnp.float32) + lat_norm_back(d_lat_norm * lat_gains[0])[0]
    lat_gain_grad = jnp.stack([jnp.sum(d_lat_norm * lat_norm, axis=0), gain_mlp_total])

    mine = (img * n_pix + pix) * slots_dev + jnp.arange(slots_dev, dtype=jnp.int32)
    blocks = jnp.sum(
        jnp.where(owner[None] == mine[:, None], all_blocks[None], 0), axis=1
    )
    new_left, new_right, new_master, new_copy = update_slots(
        blocks.astype(jnp.int32),
        lat_low,
        d_query,
        grads,
        left_stat,
        right_stat,
        left_root,
        right_root,
        master,
    )
    new_kv = kv_weight - 0.3 / math.sqrt(CIN) * normalized(kv_grad, (1, 2))
    new_latent = latent_array - 0.3 * normalized(latent_grad, (0, 1))
    new_in_gain = in_gain - 0.2 * normalized(in_gain_grad, (0,))
    new_lat_gains = lat_gains - 0.2 * normalized(lat_gain_grad, (1,))
    return (
        latents_out[:, None],
        pixel_grad,
        new_left,
        new_right,
        new_master,
        new_copy,
        kv_grad,
        new_kv,
        latent_grad,
        new_latent,
        in_gain_grad,
        new_in_gain,
        lat_gain_grad,
        new_lat_gains,
    )


def solution(mesh):
    pixel_spec = P(None, "img", "pix", None)
    slot_spec = P(("img", "pix"), None, None)
    in_specs = (
        (pixel_spec, P(), P()) + (slot_spec,) * 5 + (P(),) * 4 + (pixel_spec,)
    )
    out_specs = (pixel_spec, pixel_spec) + (slot_spec,) * 4 + (P(),) * 8
    return jax.shard_map(shards, mesh=mesh, in_specs=in_specs, out_specs=out_specs, check_vma=False)
```

```python
import functools
import math

import jax
import jax.numpy as jnp
from jax import lax
import numpy as np
from jax.experimental import pallas as pl
from jax.experimental.pallas import tpu as pltpu
from jax.sharding import PartitionSpec as P

CIN = 261
DL = 1024
LAT = 512
BLK = 128
NBLK = 256
PER_MATRIX = NBLK // 4
CEXT = 264
ONES_ROW = 261
MASK_ROW = 263
MASKED = -1e30

HIGHEST_PRECISION = lax.Precision.HIGHEST


def standardize(values_in):
    average = jnp.mean(values_in, axis=-1, keepdims=True)
    centred = values_in - average
    variance = jnp.mean(centred * centred, axis=-1, keepdims=True)
    return centred * lax.rsqrt(variance + 1e-05)


def gelu_exact(values_in):
    return jax.nn.gelu(values_in, approximate=False)


def normalized(gradient, reduce_axes):
    return gradient / jnp.sqrt(
        jnp.mean(gradient * gradient, axis=reduce_axes, keepdims=True) + 1e-06
    )


def product(pattern, left_side, right_side):
    return jnp.einsum(pattern, left_side, right_side, preferred_element_type=jnp.float32)


def fine(pattern, left_side, right_side):
    return jnp.einsum(
        pattern,
        left_side.astype(jnp.float32),
        right_side.astype(jnp.float32),
        precision=HIGHEST_PRECISION,
    )


def two_terms(values_in):
    head = lax.reduce_precision(values_in, 8, 7)
    return (head.astype(jnp.bfloat16), (values_in - head).astype(jnp.bfloat16))


def contract_rows(left_side, right_side, precision=None):
    return lax.dot_general(
        left_side,
        right_side,
        (((0,), (0,)), ((), ())),
        precision=precision,
        preferred_element_type=jnp.float32,
    )


def dot(left_side, right_side):
    return jnp.dot(left_side, right_side, preferred_element_type=jnp.float32)


def dot_last(left_side, right_side):
    return lax.dot_general(
        left_side, right_side, (((1,), (1,)), ((), ())), preferred_element_type=jnp.float32
    )


def tile_of(rows, most):
    return max((size for size in range(128, most + 1, 128) if rows % size == 0), default=rows)


def lies_across(pixels):
    micro, _, rows_dev, _ = pixels.shape
    return jnp.swapaxes(pixels, 2, 3).reshape(micro, CIN, 1, rows_dev)


def centre(pix):
    centred = pix - jnp.mean(pix, axis=0, keepdims=True)
    scale = lax.rsqrt(jnp.mean(centred * centred, axis=0, keepdims=True) + 1e-05)
    return (centred * scale, scale)


def cost(flops, count):
    return pl.CostEstimate(flops=int(flops), bytes_accessed=int(count), transcendentals=0)


def prepare_body(place_ref, pix_ref, gain_ref, *rest, micro_index):
    out_ref = rest[-1]
    normed, _ = centre(pix_ref[0, :, 0, :])
    columns = normed.shape[1]
    extra = (CEXT - CIN, columns)
    slot = place_ref[0] + pl.program_id(0) * columns + lax.broadcasted_iota(jnp.int32, extra, 1)
    row = lax.broadcasted_iota(jnp.int32, extra, 0) + CIN
    mask = jnp.where(slot < place_ref[1 + micro_index], 0.0, MASKED)
    tail = jnp.where(row == MASK_ROW, mask, 1.0)
    out_ref[0] = jnp.concatenate([normed * gain_ref[...], tail], axis=0).astype(jnp.bfloat16)


def prepare_pixels(micro_index, earlier, place, across, gain_column):
    micro, _, _, rows_dev = across.shape
    rows = tile_of(rows_dev, 1152)
    m = micro_index
    in_specs = [
        pl.BlockSpec(memory_space=pltpu.SMEM),
        pl.BlockSpec((1, CIN, 1, rows), lambda t: (m, 0, 0, t)),
        pl.BlockSpec((CIN, 1), lambda t: (0, 0)),
    ]
    operands = [place, across, gain_column]
    aliases = {}
    if earlier is not None:
        in_specs.append(pl.BlockSpec(memory_space=pl.ANY))
        aliases = {len(operands): 0}
        operands.append(earlier)
    return pl.pallas_call(
        functools.partial(prepare_body, micro_index=m),
        grid=(rows_dev // rows,),
        in_specs=in_specs,
        out_specs=pl.BlockSpec((1, CEXT, rows), lambda t: (m, 0, t)),
        out_shape=jax.ShapeDtypeStruct((micro, CEXT, rows_dev), jnp.bfloat16),
        input_output_aliases=aliases,
        cost_estimate=cost(0, 12 * rows_dev * CEXT),
        name="prepare_pixels",
    )(*operands)


def attend_body(feat_ref, query_ref, exp_ref, out_ref, sum_ref):
    tile = pl.program_id(1)
    feats = feat_ref[0]
    weights = jnp.exp(contract_rows(feats, query_ref[...])).astype(jnp.bfloat16)
    exp_ref[0] = weights

    @pl.when(tile == 0)
    def _():
        sum_ref[...] = jnp.zeros_like(sum_ref)

    sum_ref[...] += dot(feats, weights)

    @pl.when(tile == pl.num_programs(1) - 1)
    def _():
        sums = sum_ref[...]
        low = sums.astype(jnp.bfloat16)
        rest = (sums - low.astype(jnp.float32))[ONES_ROW : ONES_ROW + 1]
        row = lax.broadcasted_iota(jnp.int32, sums.shape, 0)
        out_ref[0] = jnp.where(row == ONES_ROW + 1, rest, sums).astype(jnp.bfloat16)


def attend(feats, query_cols):
    micro, _, rows_dev = feats.shape
    rows = tile_of(rows_dev, 1152)
    return pl.pallas_call(
        attend_body,
        grid=(micro, rows_dev // rows),
        in_specs=[
            pl.BlockSpec((1, CEXT, rows), lambda m, t: (m, 0, t)),
            pl.BlockSpec((CEXT, LAT), lambda m, t: (0, 0)),
        ],
        out_specs=[
            pl.BlockSpec((1, rows, LAT), lambda m, t: (m, t, 0)),
            pl.BlockSpec((1, CEXT, LAT), lambda m, t: (m, 0, 0)),
        ],
        out_shape=[
            jax.ShapeDtypeStruct((micro, rows_dev, LAT), jnp.bfloat16),
            jax.ShapeDtypeStruct((micro, CEXT, LAT), jnp.bfloat16),
        ],
        scratch_shapes=[pltpu.VMEM((CEXT, LAT), jnp.float32)],
        cost_estimate=cost(8 * micro * rows_dev * LAT * CEXT, 4 * micro * rows_dev * LAT),
        name="attend",
    )(feats, query_cols)


def tiles_of(feats):
    rows_dev = feats.shape[2]
    return rows_dev // tile_of(rows_dev, 1152)


def parts_of(feats):
    micro = feats.shape[0]
    tiles = tiles_of(feats)
    parts = []
    for m in range(micro):
        head = max(tiles // 3 if m == micro - 1 else tiles - tiles // 2, 1)
        parts.append((m, 0, head))
        if head < tiles:
            parts.append((m, head, tiles - head))
    return parts


def attend_back_body(pix_ref, feat_ref, exp_ref, gain_ref, dc_ref, qc_ref, *rest):
    grad_ref, score_ref, gain_sum_ref = rest[-3:]
    feats = feat_ref[0]
    weights = exp_ref[0]
    d_exp = contract_rows(feats, dc_ref[0])
    d_scores = (weights.astype(jnp.float32) * d_exp).astype(jnp.bfloat16)

    @pl.when(pl.program_id(0) == 0)
    def _():
        score_ref[...] = jnp.zeros_like(score_ref)
        gain_sum_ref[...] = jnp.zeros_like(gain_sum_ref)

    score_ref[...] += dot(feats, d_scores)
    d_pix = (dot_last(qc_ref[...], d_scores) + dot_last(dc_ref[0], weights))[:CIN]
    normed, scale = centre(pix_ref[0, :, 0, :])
    gain_sum_ref[...] += jnp.sum(d_pix * normed, axis=1, keepdims=True)
    d_normed = d_pix * gain_ref[...]
    along = jnp.mean(d_normed * normed, axis=0, keepdims=True)
    level = jnp.mean(d_normed, axis=0, keepdims=True)
    grad_ref[0, :, 0, :] = (d_normed - level - normed * along) * scale


def attend_back(part, earlier, across, feats, weights, gain_column, d_cols, query_cols):
    m, first, tiles = part
    rows = feats.shape[2] // tiles_of(feats)
    in_specs = [
        pl.BlockSpec((1, CIN, 1, rows), lambda t: (m, 0, 0, first + t)),
        pl.BlockSpec((1, CEXT, rows), lambda t: (m, 0, first + t)),
        pl.BlockSpec((1, rows, LAT), lambda t: (m, first + t, 0)),
        pl.BlockSpec((CIN, 1), lambda t: (0, 0)),
        pl.BlockSpec((1, CEXT, LAT), lambda t: (m, 0, 0)),
        pl.BlockSpec((CEXT, LAT), lambda t: (0, 0)),
    ]
    operands = [across, feats, weights, gain_column, d_cols, query_cols]
    aliases = {}
    if earlier is not None:
        in_specs.append(pl.BlockSpec(memory_space=pl.ANY))
        aliases = {len(operands): 0}
        operands.append(earlier)
    return pl.pallas_call(
        attend_back_body,
        grid=(tiles,),
        in_specs=in_specs,
        out_specs=[
            pl.BlockSpec((1, CIN, 1, rows), lambda t: (m, 0, 0, first + t)),
            pl.BlockSpec((CEXT, LAT), lambda t: (0, 0)),
            pl.BlockSpec((CIN, 1), lambda t: (0, 0)),
        ],
        out_shape=[
            jax.ShapeDtypeStruct(across.shape, jnp.float32),
            jax.ShapeDtypeStruct((CEXT, LAT), jnp.float32),
            jax.ShapeDtypeStruct((CIN, 1), jnp.float32),
        ],
        input_output_aliases=aliases,
        cost_estimate=cost(16 * tiles * rows * LAT * CEXT, tiles * rows * 4000),
        name="attend_back",
    )(*operands)


def query_body(block_ref, lat_ref, gain_ref, key_ref, *rest):
    sources, (low_ref, query_ref, cols_ref, wq_ref, wo_ref, w1_ref, w2_ref, sems) = (
        rest[:-8],
        rest[-8:],
    )
    squares = (wq_ref, wo_ref, w1_ref, w2_ref)
    side = DL // BLK
    first = 0
    for source in sources:

        @pl.loop(0, source.shape[0])
        def _(at, source=source, first=first):
            block = block_ref[first + at]
            row = pl.multiple_of((block % PER_MATRIX // side) * BLK, BLK)
            column = pl.multiple_of((block % side) * BLK, BLK)
            for matrix in range(4):

                @pl.when(block // PER_MATRIX == matrix)
                def _(matrix=matrix):
                    pltpu.make_async_copy(
                        source.at[at],
                        squares[matrix].at[pl.ds(row, BLK), pl.ds(column, BLK)],
                        sems.at[matrix],
                    ).start()

        first += source.shape[0]

    def settle(matrix):
        pltpu.make_async_copy(squares[matrix], squares[matrix], sems.at[matrix]).wait()

    lat_low = (standardize(lat_ref[...]) * gain_ref[...]).astype(jnp.bfloat16)
    low_ref[...] = lat_low
    settle(0)
    query = dot(lat_low, wq_ref[...]).astype(jnp.bfloat16)
    query_ref[...] = query
    scores = dot_last(key_ref[...], query) * (1.0 / math.sqrt(DL))
    row = lax.broadcasted_iota(jnp.int32, scores.shape, 0)
    cols_ref[...] = jnp.where(row == MASK_ROW, 1.0, scores).astype(jnp.bfloat16)
    for matrix in range(1, 4):
        settle(matrix)


def make_query(blocks, sources, latent_array, gain, w_key):
    vmem = pl.BlockSpec(memory_space=pltpu.VMEM)
    hbm = pl.BlockSpec(memory_space=pl.ANY)
    rows = jax.ShapeDtypeStruct((LAT, DL), jnp.bfloat16)
    square = jax.ShapeDtypeStruct((DL, DL), jnp.bfloat16)
    return pl.pallas_call(
        query_body,
        in_specs=[pl.BlockSpec(memory_space=pltpu.SMEM), vmem, vmem, vmem] + [hbm] * len(sources),
        out_specs=[vmem] * 7,
        out_shape=[rows, rows, jax.ShapeDtypeStruct((CEXT, LAT), jnp.bfloat16)] + [square] * 4,
        scratch_shapes=[pltpu.SemaphoreType.DMA((4,))],
        cost_estimate=cost(3 * LAT * DL * DL, 4 * NBLK * BLK * BLK),
        name="make_query",
    )(blocks, latent_array, gain[None], w_key, *sources)


def image_sums_body(where_ref, *rest):
    n_img = len(rest) - 7
    pieces, (grads_ref, value_ref, resid_ref, rows_ref, full_ref, zero_ref, sems) = (
        rest[:n_img],
        rest[n_img:],
    )
    side = DL // BLK
    count = pieces[0].shape[1]

    def put(source, block):
        place = where_ref[n_img + block]

        @pl.when(place >= 0)
        def _():
            pltpu.make_async_copy(source, grads_ref.at[place], sems.at[1]).start()

    for piece in range(n_img):
        first = pl.multiple_of(where_ref[piece] * count, count)
        pltpu.make_async_copy(
            pieces[piece], rows_ref.at[:, pl.ds(first, count), :], sems.at[0]
        ).start()
    zero_ref[...] = jnp.zeros_like(zero_ref)

    @pl.loop(0, PER_MATRIX)
    def _(block):
        put(zero_ref, block)

    pltpu.make_async_copy(rows_ref, rows_ref, sems.at[0]).wait()
    for matrix in range(3):
        full_ref[matrix] = contract_rows(rows_ref[matrix], rows_ref[3 + matrix]).astype(jnp.bfloat16)

        @pl.loop(0, PER_MATRIX)
        def _(block, matrix=matrix):
            row = pl.multiple_of((block // side) * BLK, BLK)
            column = pl.multiple_of((block % side) * BLK, BLK)
            put(
                full_ref.at[matrix, pl.ds(row, BLK), pl.ds(column, BLK)],
                (matrix + 1) * PER_MATRIX + block,
            )

    value_ref[...] = contract_rows(rows_ref[7, :, :CEXT], rows_ref[6]).astype(jnp.bfloat16)
    each = resid_ref.shape[0]
    total = rows_ref[3, :each, :].astype(jnp.float32)
    for first in range(each, rows_ref.shape[1], each):
        total = total + rows_ref[3, first : first + each, :].astype(jnp.float32)
    resid_ref[...] = total.astype(jnp.bfloat16)
    pltpu.make_async_copy(grads_ref, grads_ref, sems.at[1]).wait()


def image_sums(where, pieces, lat_rows):
    n_img = len(pieces)
    slabs, count, _ = pieces[0].shape
    hbm = pl.BlockSpec(memory_space=pl.ANY)
    vmem = pl.BlockSpec(memory_space=pltpu.VMEM)
    return pl.pallas_call(
        image_sums_body,
        in_specs=[pl.BlockSpec(memory_space=pltpu.SMEM)] + [hbm] * n_img,
        out_specs=[hbm, vmem, vmem],
        out_shape=[
            jax.ShapeDtypeStruct((NBLK // n_img, BLK, BLK), jnp.bfloat16),
            jax.ShapeDtypeStruct((CEXT, DL), jnp.bfloat16),
            jax.ShapeDtypeStruct((lat_rows, DL), jnp.bfloat16),
        ],
        scratch_shapes=[
            pltpu.VMEM((slabs, n_img * count, DL), jnp.bfloat16),
            pltpu.VMEM((3, DL, DL), jnp.bfloat16),
            pltpu.VMEM((BLK, BLK), jnp.bfloat16),
            pltpu.SemaphoreType.DMA((2,)),
        ],
        cost_estimate=cost(8 * n_img * count * DL * DL, 16 * DL * DL),
        name="image_sums",
    )(where, *pieces)


def two_bf16(values_in):
    head = values_in.astype(jnp.bfloat16)
    return (head, (values_in - head.astype(jnp.float32)).astype(jnp.bfloat16))


def product_f32(left_side, right_side):
    left_head, left_rest = two_bf16(left_side)
    right_head, right_rest = two_bf16(right_side)
    both = dot(
        jnp.concatenate([left_head, left_rest], axis=1),
        jnp.concatenate([right_head, right_head], axis=0),
    )
    return both + dot(left_head, right_rest)


def update_body(block_ref, lat_ref, dq_ref, sum_ref, ls_ref, rs_ref, lr_ref, rr_ref, ma_ref, *outs):
    new_left, new_right, new_master, new_copy = outs
    side = DL // BLK
    for slot in range(ma_ref.shape[0]):
        block = block_ref[slot]
        is_query = block < PER_MATRIX
        inside = jnp.where(is_query, block, 0)
        row = pl.multiple_of(inside // side * BLK, BLK)
        column = pl.multiple_of(inside % side * BLK, BLK)
        own = contract_rows(lat_ref[:, pl.ds(row, BLK)], dq_ref[:, pl.ds(column, BLK)])
        grad = jnp.where(is_query, own, sum_ref[slot])
        turned = grad.T
        new_left[slot] = 0.5 * ls_ref[slot] + 0.5 * product_f32(grad, turned)
        new_right[slot] = 0.5 * rs_ref[slot] + 0.5 * product_f32(turned, grad)
        shampoo = product_f32(product_f32(lr_ref[slot], grad), rr_ref[slot])
        mean_square = jnp.mean(shampoo * shampoo)
        updated = ma_ref[slot] - 0.5 / math.sqrt(DL) * (shampoo / jnp.sqrt(mean_square + 1e-06))
        new_master[slot] = updated
        new_copy[slot] = updated.astype(jnp.bfloat16)


def update_slots(blocks, lat_low, d_query, sums, left_stat, right_stat, left_root, right_root, master):
    vmem = pl.BlockSpec(memory_space=pltpu.VMEM)
    shape = jax.ShapeDtypeStruct(master.shape, jnp.float32)
    return pl.pallas_call(
        update_body,
        in_specs=[pl.BlockSpec(memory_space=pltpu.SMEM)] + [vmem] * 8,
        out_specs=[vmem] * 4,
        out_shape=[shape, shape, shape, jax.ShapeDtypeStruct(master.shape, jnp.bfloat16)],
        name="update_slots",
    )(blocks, lat_low, d_query, sums, left_stat, right_stat, left_root, right_root, master)


def root_mean(total, count):
    return jnp.sqrt(total / count + 1e-06)


def finish_body(late_ref, key_ref, query_ref, wq_ref, early_ref, kv_ref, lat_ref, gains_ref, *outs):
    dq_ref, kv_grad_ref, new_kv_ref, lat_grad_ref, new_lat_ref, gain_ref, new_gain_ref = outs
    inv_root = 1.0 / math.sqrt(DL)
    late = late_ref[...]
    d_query = (contract_rows(late, key_ref[...]) * inv_root).astype(jnp.bfloat16)
    dq_ref[...] = d_query
    key_total = (dot(late, query_ref[...]) * inv_root)[:CIN]
    value_total = early_ref[:CEXT, :].astype(jnp.float32)[:CIN]
    for at, grad in enumerate((key_total, value_total)):
        kv_grad_ref[:, at, :] = grad
        step = 0.3 / math.sqrt(CIN) / root_mean(jnp.sum(grad * grad), CIN * DL)
        new_kv_ref[:, at, :] = kv_ref[:, at, :] - step * grad
    d_lat_norm = dot_last(d_query, wq_ref[...])
    lat = lat_ref[...]
    centred = lat - jnp.mean(lat, axis=-1, keepdims=True)
    scale = lax.rsqrt(jnp.mean(centred * centred, axis=-1, keepdims=True) + 1e-05)
    normed = centred * scale
    dy = d_lat_norm * gains_ref[0:1]
    along = jnp.mean(dy * normed, axis=-1, keepdims=True)
    back = (dy - jnp.mean(dy, axis=-1, keepdims=True) - normed * along) * scale
    lat_grad = early_ref[CEXT:, :].astype(jnp.float32) + back
    lat_grad_ref[...] = lat_grad
    new_lat_ref[...] = lat - 0.3 / root_mean(jnp.sum(lat_grad * lat_grad), LAT * DL) * lat_grad
    tail = late[CIN + 1 : CEXT].astype(jnp.float32)
    second = jnp.concatenate([tail[0:1], tail[1:2]], axis=1)
    for at, grad in enumerate((jnp.sum(d_lat_norm * normed, axis=0, keepdims=True), second)):
        gain_ref[at : at + 1] = grad
        step = 0.2 / root_mean(jnp.sum(grad * grad), DL)
        new_gain_ref[at : at + 1] = gains_ref[at : at + 1] - step * grad


def finish(late, w_key, query, w_query, early, kv_weight, latent_array, lat_gains):
    vmem = pl.BlockSpec(memory_space=pltpu.VMEM)
    kv = jnp.swapaxes(kv_weight, 0, 1)
    kv_shape = jax.ShapeDtypeStruct(kv.shape, jnp.float32)
    lat_shape = jax.ShapeDtypeStruct((LAT, DL), jnp.float32)
    gain_shape = jax.ShapeDtypeStruct(lat_gains.shape, jnp.float32)
    outs = pl.pallas_call(
        finish_body,
        in_specs=[vmem] * 8,
        out_specs=[vmem] * 7,
        out_shape=[jax.ShapeDtypeStruct((LAT, DL), jnp.bfloat16)]
        + [kv_shape] * 2
        + [lat_shape] * 2
        + [gain_shape] * 2,
        name="finish",
    )(late, w_key, query, w_query, early, kv, latent_array, lat_gains)
    d_query, kv_grad, new_kv, *others = outs
    return (d_query, jnp.swapaxes(kv_grad, 0, 1), jnp.swapaxes(new_kv, 0, 1), *others)


def swap(array, axis):
    return lax.all_to_all(array, axis, 0, 0, tiled=True)


def everyone(array, axis):
    return swap(jnp.broadcast_to(array[None], (lax.axis_size(axis), *array.shape)), axis)


def near_hop(array, axis):
    size = lax.axis_size(axis)
    return lax.ppermute(array, axis, [(i, i ^ 1) for i in range(size)])


def far_hop(array, axis, step):
    size = lax.axis_size(axis)
    return lax.ppermute(array, axis, [(i, (i + 2 * step) % size) for i in range(size)])


def spread(array, rows, axis, hops):
    size = lax.axis_size(axis)
    column = {("img", "far"): 0, ("img", "near"): 1, ("pix", "far"): 2, ("pix", "near"): 3}
    got = [array]
    places = [rows]
    for step in range(1, 2 if hops == "near" else size // 2):
        got.append(near_hop(array, axis) if hops == "near" else far_hop(array, axis, step))
        moved = rows.copy()
        moved[:, column[axis, hops]] += step
        places.append(moved)
    return (jnp.concatenate(got), np.concatenate(places))


ROUTES = (
    (("pix", "near"), ("img", "far"), ("pix", "far")),
    (("img", "far"), ("pix", "far"), ("pix", "near")),
    (("pix", "far"), ("pix", "near"), ("img", "far")),
)


def gather_blocks(low, feats):
    slots_dev = low.shape[0]
    n_pix = lax.axis_size("pix")
    if slots_dev < 4 or n_pix > 8:
        low = lax.all_gather(low, ("img", "pix"), axis=0, tiled=True)
        return ([low], jnp.arange(NBLK), feats)
    quarter = slots_dev // 4
    states = []
    bounds = (0, quarter, 2 * quarter, slots_dev)
    for part in range(3):
        start, stop = bounds[part], bounds[part + 1]
        rows = np.zeros((stop - start, 5), np.int32)
        rows[:, 4] = np.arange(start, stop)
        states.append((low[start:stop], rows))
    for phase in range(3):
        states = [spread(*state, *ROUTES[part][phase]) for part, state in enumerate(states)]
    held, feats = lax.optimization_barrier(([array for array, _ in states], feats))
    arrays = []
    places = []
    for array, (_, rows) in zip(held, states):
        arrays += [array, near_hop(array, "img")]
        mate = rows.copy()
        mate[:, 1] += 1
        places += [rows, mate]
    img_far, img_near, pix_far, pix_near, slot = np.concatenate(places).T
    img = lax.axis_index("img")
    pix = lax.axis_index("pix")
    n_far = lax.axis_size("img") // 2
    img_of = (img // 2 - img_far) % n_far * 2 + (img + img_near) % 2
    pix_of = (pix // 2 - pix_far) % (n_pix // 2) * 2 + (pix + pix_near) % 2
    return (arrays, (img_of * n_pix + pix_of) * slots_dev + slot, feats)


def split_near(array, axis):
    size = lax.axis_size(axis)
    near = lax.axis_index(axis) % 2
    pairs = array.reshape(size // 2, 2, *array.shape[1:])
    return (
        lax.dynamic_index_in_dim(pairs, near, 1, False),
        lax.dynamic_index_in_dim(pairs, 1 - near, 1, False),
    )


def join_near(kept, sent, axis):
    got = near_hop(sent, axis)
    return (kept.astype(jnp.float32) + got.astype(jnp.float32)).astype(jnp.bfloat16)


def sum_far(kept, axis):
    size = lax.axis_size(axis)
    far = lax.axis_index(axis) // 2
    total = lax.dynamic_index_in_dim(kept, far, 0, False).astype(jnp.float32)
    for step in range(1, size // 2):
        part = lax.dynamic_index_in_dim(kept, (far + step) % (size // 2), 0, False)
        total = total + far_hop(part, axis, step).astype(jnp.float32)
    return total


def gather_far(array, axis):
    size = lax.axis_size(axis)
    far = lax.axis_index(axis) // 2
    got = [array] + [far_hop(array, axis, step) for step in range(1, size // 2)]
    return lax.dynamic_slice_in_dim(jnp.stack(got[::-1] * 2), size // 2 - 1 - far, size // 2, 0)


def gather_near(array, axis):
    near = lax.axis_index(axis) % 2
    other = near_hop(array, axis)
    both = jnp.where(
        near == 0, jnp.stack([array, other], axis=1), jnp.stack([other, array], axis=1)
    )
    return both.reshape(lax.axis_size(axis), *array.shape[1:])


def latent_pass(numerator, denominator, lat_part, cot_rows, lat_gain, w_out, w_up, w_down):
    attended = numerator / denominator[..., None]
    att_low = attended.astype(jnp.bfloat16)
    resid = lat_part[None] + product("mrd,de->mre", att_low, w_out)
    normed, normed_back = jax.vjp(standardize, resid)
    hn_low = (normed * lat_gain).astype(jnp.bfloat16)
    hidden = product("mrd,de->mre", hn_low, w_up)
    active, active_back = jax.vjp(gelu_exact, hidden)
    act_low = active.astype(jnp.bfloat16)
    latents_out = resid + product("mrd,de->mre", act_low, w_down)
    g_mlp = cot_rows.astype(jnp.bfloat16)
    d_active = product("mre,de->mrd", g_mlp, w_down)
    d_hidden = active_back(d_active)[0].astype(jnp.bfloat16)
    d_normed = product("mre,de->mrd", d_hidden, w_up)
    d_resid = cot_rows + normed_back(d_normed * lat_gain)[0]
    d_branch = d_resid.astype(jnp.bfloat16)
    d_attended = product("mre,de->mrd", d_branch, w_out)
    d_numer = d_attended / denominator[..., None]
    d_denom = -jnp.sum(d_attended * numerator / (denominator * denominator)[..., None], axis=-1)
    gain_mlp = jnp.sum(d_normed * normed, axis=(0, 1))
    row_arrays = (att_low, hn_low, act_low, d_branch, d_hidden, g_mlp)
    return (latents_out, d_numer.astype(jnp.bfloat16), d_denom, (row_arrays, gain_mlp))


def shards(
    pixels,
    sides,
    owner,
    master,
    left_stat,
    right_stat,
    left_root,
    right_root,
    kv_weight,
    latent_array,
    in_gain,
    lat_gains,
    cotangent,
):
    micro = pixels.shape[0]
    rows_dev = pixels.shape[2]
    n_pix = lax.axis_size("pix")
    n_img = lax.axis_size("img")
    img = lax.axis_index("img")
    pix = lax.axis_index("pix")
    slots_dev = master.shape[0]
    lat_rows = LAT // n_pix
    row_start = pix * lat_rows
    inv_root = 1.0 / math.sqrt(DL)

    place = jnp.concatenate([(pix * rows_dev)[None], sides * sides]).astype(jnp.int32)
    across = lies_across(pixels)
    gain_column = in_gain[:, None]
    feats = None
    for micro_index in range(micro - 1):
        feats = prepare_pixels(micro_index, feats, place, across, gain_column)
    sources, source_slots, feats = gather_blocks(master.astype(jnp.bfloat16), feats)
    feats = prepare_pixels(micro - 1, feats, place, across, gain_column)
    all_blocks = jnp.arange(NBLK, dtype=jnp.int32)
    source_blocks = jnp.sum(
        jnp.where(source_slots[:, None] == owner[None], all_blocks[None], 0), axis=1
    )
    kv_low = kv_weight.astype(jnp.bfloat16)
    w_key = jnp.pad(kv_low[0], ((0, CEXT - CIN), (0, 0)))
    w_value = kv_low[1]
    lat_low, query, query_cols, w_query, w_out, w_up, w_down = make_query(
        source_blocks.astype(jnp.int32), sources, latent_array, lat_gains[0], w_key
    )

    weights, sums = attend(feats, query_cols)
    sums = sums.reshape(micro, CEXT, n_pix, lat_rows).transpose(2, 1, 0, 3)
    sums = swap(sums.reshape(n_pix, CEXT, micro * lat_rows), "pix")
    sums = jnp.sum(sums.astype(jnp.float32), axis=0)
    numer_in = sums[:CIN]
    denominator = (sums[ONES_ROW] + sums[ONES_ROW + 1]).reshape(micro, lat_rows)
    numerator = fine("cr,cd->rd", numer_in, w_value).reshape(micro, lat_rows, DL)
    latents_out, d_numer, d_denom, latent_grads = latent_pass(
        numerator,
        denominator,
        lax.dynamic_slice_in_dim(latent_array, row_start, lat_rows, 0),
        cotangent[:, 0],
        lat_gains[1],
        w_out,
        w_up,
        w_down,
    )
    row_arrays, gain_mlp = latent_grads
    d_numer = d_numer.reshape(micro * lat_rows, DL)
    head, rest = two_terms(d_denom.reshape(1, micro * lat_rows))
    d_cols = product("rd,cd->cr", d_numer, w_value).astype(jnp.bfloat16)
    d_cols = jnp.concatenate([d_cols, head, rest, jnp.zeros_like(head)], axis=0)
    d_cols = everyone(d_cols, "pix").reshape(n_pix, CEXT, micro, lat_rows)
    d_cols = d_cols.transpose(2, 1, 0, 3).reshape(micro, CEXT, LAT)

    numer_rows = jnp.pad(numer_in.astype(jnp.bfloat16).T, ((0, 0), (0, DL - CIN)))
    own = jnp.stack(
        [array.reshape(micro * lat_rows, DL) for array in row_arrays] + [d_numer, numer_rows]
    )
    mate = [(i, i ^ 1) for i in range(n_img)]
    pieces = [own, lax.ppermute(own, "img", mate)]
    images = [img, img ^ 1]
    far = []
    for step in range(1, n_img // 2):
        hop = [(i, (i + 2 * step) % n_img) for i in range(n_img)]
        far.append(lax.ppermute(own, "img", hop))
        images += [(img - 2 * step) % n_img, (img - 2 * step) % n_img ^ 1]
    device_of = owner // slots_dev
    place_of = device_of % n_pix * slots_dev + owner % slots_dev
    where = jnp.where(device_of // n_pix == img, place_of, -1)

    results = (None,)
    score_sum = jnp.zeros((CEXT, LAT), jnp.float32)
    gain_sum = jnp.zeros((CIN, 1), jnp.float32)
    width = DL // 2
    each = -(-CEXT // n_pix)
    parts = parts_of(feats)
    for at, part in enumerate(parts):
        if at == len(parts) - 2:
            far, gain_sum = lax.optimization_barrier((far, gain_sum))
            for piece in far:
                pieces += [piece, lax.ppermute(piece, "img", mate)]
        if at == len(parts) - 1:
            pieces, gain_sum = lax.optimization_barrier((pieces, gain_sum))
            where = jnp.concatenate([jnp.stack(images), where]).astype(jnp.int32)
            grads, value_part, resid_part = image_sums(where, pieces, lat_rows)
            value_part = jnp.pad(value_part, ((0, each * n_pix - CEXT), (0, 0)))
            value_part = lax.dynamic_slice_in_dim(value_part, img % 2 * width, width, 1)
            value_sides = split_near(value_part.reshape(n_pix, each, width), "pix")
            grad_sides = split_near(grads.reshape(n_pix, slots_dev, BLK, BLK), "pix")
            gain_column, value_sides, grad_sides = lax.optimization_barrier(
                (gain_column, value_sides, grad_sides)
            )
        results = attend_back(
            part, results[0], across, feats, weights, gain_column, d_cols, query_cols
        )
        score_sum = score_sum + results[1]
        gain_sum = gain_sum + results[2]
    pixel_grad = jnp.swapaxes(results[0].reshape(micro, 1, CIN, rows_dev), 2, 3)

    late = jnp.concatenate(
        [
            score_sum[:CIN],
            jnp.pad(gain_sum.T, ((0, 0), (0, LAT - CIN))),
            gain_mlp.reshape(DL // LAT, LAT),
        ],
        axis=0,
    ).astype(jnp.bfloat16)
    late = jnp.pad(late, ((0, each * n_pix - CEXT), (0, 0))).reshape(n_pix, each, LAT)
    value_part = join_near(*value_sides, "pix")
    grads = join_near(*grad_sides, "pix")
    late, value_part, grads = lax.optimization_barrier((late, value_part, grads))
    late = jnp.sum(swap(late, "pix").astype(jnp.float32), axis=0)
    value_part = sum_far(value_part, "pix").astype(jnp.bfloat16)
    late, value_part = lax.optimization_barrier((late, value_part))
    late = jnp.sum(everyone(late, "img"), axis=0).astype(jnp.bfloat16)
    grads = sum_far(grads, "pix")
    resid_part = lax.dynamic_slice_in_dim(resid_part, img % 2 * width, width, 1)
    early = gather_far(jnp.concatenate([value_part, resid_part], axis=0), "pix")
    late, early, grads = lax.optimization_barrier((late, early, grads))
    late = everyone(late, "pix").reshape(n_pix * each, LAT)[:CEXT]
    early = gather_near(early, "pix")
    value_part = early[:, :each].reshape(n_pix * each, width)[:CEXT]
    early = jnp.concatenate([value_part, early[:, each:].reshape(LAT, width)], axis=0)
    other = near_hop(early, "img")
    early = jnp.where(
        img % 2 == 0,
        jnp.concatenate([early, other], axis=1),
        jnp.concatenate([other, early], axis=1),
    )
    d_query, kv_grad, new_kv, latent_grad, new_latent, lat_gain_grad, new_lat_gains = finish(
        late, w_key, query, w_query, early, kv_weight, latent_array, lat_gains
    )
    in_gain_grad = late[CIN, :CIN].astype(jnp.float32)

    mine = (img * n_pix + pix) * slots_dev + jnp.arange(slots_dev, dtype=jnp.int32)
    blocks = jnp.sum(
        jnp.where(owner[None] == mine[:, None], all_blocks[None], 0), axis=1
    )
    new_left, new_right, new_master, new_copy = update_slots(
        blocks.astype(jnp.int32),
        lat_low,
        d_query,
        grads,
        left_stat,
        right_stat,
        left_root,
        right_root,
        master,
    )
    new_in_gain = in_gain - 0.2 * normalized(in_gain_grad, (0,))
    return (
        latents_out[:, None],
        pixel_grad,
        new_left,
        new_right,
        new_master,
        new_copy,
        kv_grad,
        new_kv,
        latent_grad,
        new_latent,
        in_gain_grad,
        new_in_gain,
        lat_gain_grad,
        new_lat_gains,
    )


def solution(mesh):
    pixel_spec = P(None, "img", "pix", None)
    slot_spec = P(("img", "pix"), None, None)
    in_specs = (
        (pixel_spec, P(), P()) + (slot_spec,) * 5 + (P(),) * 4 + (pixel_spec,)
    )
    out_specs = (pixel_spec, pixel_spec) + (slot_spec,) * 4 + (P(),) * 8
    return jax.shard_map(shards, mesh=mesh, in_specs=in_specs, out_specs=out_specs, check_vma=False)
```

```python
import functools
import math

import jax
import jax.numpy as jnp
from jax import lax
import numpy as np
from jax.experimental import pallas as pl
from jax.experimental.pallas import tpu as pltpu
from jax.sharding import PartitionSpec as P

CIN = 261
DL = 1024
LAT = 512
BLK = 128
NBLK = 256
PER_MATRIX = NBLK // 4
CEXT = 264
WHOLE = CIN // 8 * 8
ONES_ROW = 261
MASK_ROW = 263
MASKED = -1e30

HIGHEST_PRECISION = lax.Precision.HIGHEST


def standardize(values_in):
    average = jnp.mean(values_in, axis=-1, keepdims=True)
    centred = values_in - average
    variance = jnp.mean(centred * centred, axis=-1, keepdims=True)
    return centred * lax.rsqrt(variance + 1e-05)


def gelu_exact(values_in):
    return jax.nn.gelu(values_in, approximate=False)


def normalized(gradient, reduce_axes):
    return gradient / jnp.sqrt(
        jnp.mean(gradient * gradient, axis=reduce_axes, keepdims=True) + 1e-06
    )


def product(pattern, left_side, right_side):
    return jnp.einsum(pattern, left_side, right_side, preferred_element_type=jnp.float32)


def fine(pattern, left_side, right_side):
    return jnp.einsum(
        pattern,
        left_side.astype(jnp.float32),
        right_side.astype(jnp.float32),
        precision=HIGHEST_PRECISION,
    )


def two_terms(values_in):
    head = lax.reduce_precision(values_in, 8, 7)
    return (head.astype(jnp.bfloat16), (values_in - head).astype(jnp.bfloat16))


def contract_rows(left_side, right_side, precision=None):
    return lax.dot_general(
        left_side,
        right_side,
        (((0,), (0,)), ((), ())),
        precision=precision,
        preferred_element_type=jnp.float32,
    )


def dot(left_side, right_side):
    return jnp.dot(left_side, right_side, preferred_element_type=jnp.float32)


def dot_last(left_side, right_side):
    return lax.dot_general(
        left_side, right_side, (((1,), (1,)), ((), ())), preferred_element_type=jnp.float32
    )


def tile_of(rows, most):
    return max((size for size in range(128, most + 1, 128) if rows % size == 0), default=rows)


def lies_across(pixels):
    micro, _, rows_dev, _ = pixels.shape
    return jnp.swapaxes(pixels, 2, 3).reshape(micro, CIN, 1, rows_dev)


def centre(pix):
    centred = pix - jnp.mean(pix, axis=0, keepdims=True)
    scale = lax.rsqrt(jnp.mean(centred * centred, axis=0, keepdims=True) + 1e-05)
    return (centred * scale, scale)


def cost(flops, count):
    return pl.CostEstimate(flops=int(flops), bytes_accessed=int(count), transcendentals=0)


def prepare_body(place_ref, pix_ref, gain_ref, *rest, micro_index):
    out_ref, scale_ref = rest[-2:]
    columns = pix_ref.shape[3]
    gain = gain_ref[...]
    width = BLK if columns % BLK == 0 else columns
    if width == BLK:
        pix_rows = pix_ref.reshape(CIN * columns // BLK, BLK)
    extra = (CEXT - CIN, width)
    row = lax.broadcasted_iota(jnp.int32, extra, 0) + CIN
    slot = place_ref[0] + pl.program_id(0) * columns + lax.broadcasted_iota(jnp.int32, extra, 1)
    for column in range(0, columns, width):
        inside = slice(column, column + width)
        if width == BLK:
            pix = jnp.concatenate(
                [
                    pix_rows[pl.ds(column // BLK, WHOLE, stride=columns // BLK), :],
                    pix_ref[0, WHOLE:, 0, inside],
                ],
                axis=0,
            )
        else:
            pix = pix_ref[0, :, 0, :]
        normed, scale_ref[0, :, inside] = centre(pix)
        mask = jnp.where(slot + column < place_ref[1 + micro_index], 0.0, MASKED)
        tail = jnp.where(row == MASK_ROW, mask, 1.0)
        full = jnp.concatenate([normed * gain, tail], axis=0)
        out_ref[0, :, inside] = full.astype(jnp.bfloat16)


def prepare_pixels(micro_index, earlier, place, across, gain_column):
    micro, _, _, rows_dev = across.shape
    rows = tile_of(rows_dev, 1152)
    m = micro_index
    in_specs = [
        pl.BlockSpec(memory_space=pltpu.SMEM),
        pl.BlockSpec((1, CIN, 1, rows), lambda t: (m, 0, 0, t)),
        pl.BlockSpec((CIN, 1), lambda t: (0, 0)),
    ]
    operands = [place, across, gain_column]
    aliases = {}
    if earlier is not None:
        in_specs += [pl.BlockSpec(memory_space=pl.ANY)] * 2
        aliases = {len(operands): 0, len(operands) + 1: 1}
        operands += earlier
    return pl.pallas_call(
        functools.partial(prepare_body, micro_index=m),
        grid=(rows_dev // rows,),
        in_specs=in_specs,
        out_specs=[
            pl.BlockSpec((1, CEXT, rows), lambda t: (m, 0, t)),
            pl.BlockSpec((1, 1, rows), lambda t: (m, 0, t)),
        ],
        out_shape=[
            jax.ShapeDtypeStruct((micro, CEXT, rows_dev), jnp.bfloat16),
            jax.ShapeDtypeStruct((micro, 1, rows_dev), jnp.float32),
        ],
        input_output_aliases=aliases,
        cost_estimate=cost(0, 12 * rows_dev * CEXT),
        name="prepare_pixels",
    )(*operands)


def spans_of(columns):
    if columns == 1152:
        return ((0, 512), (512, 384), (896, 256))
    return ((0, columns),)


def short_spans_of(columns):
    if columns == 1152:
        return tuple((first, min(256, columns - first)) for first in range(0, columns, 256))
    return ((0, columns),)


def attend_body(feat_ref, query_ref, exp_ref, out_ref, sum_ref):
    tile = pl.program_id(1)
    spans = spans_of(feat_ref.shape[2])
    query = query_ref[...]

    def scores_of(at):
        first, size = spans[at]
        return contract_rows(feat_ref[0, :, first : first + size], query)

    @pl.when(tile == 0)
    def _():
        sum_ref[...] = jnp.zeros_like(sum_ref)

    scores = scores_of(0)
    total = sum_ref[...]
    for at, (first, size) in enumerate(spans):
        ahead = scores_of(at + 1) if at + 1 < len(spans) else None
        weights = jnp.exp(scores).astype(jnp.bfloat16)
        exp_ref[0, first : first + size] = weights
        total = total + dot(feat_ref[0, :, first : first + size], weights)
        scores = ahead
    sum_ref[...] = total

    @pl.when(tile == pl.num_programs(1) - 1)
    def _():
        sums = sum_ref[...]
        low = sums.astype(jnp.bfloat16)
        rest = (sums - low.astype(jnp.float32))[ONES_ROW : ONES_ROW + 1]
        row = lax.broadcasted_iota(jnp.int32, sums.shape, 0)
        out_ref[0] = jnp.where(row == ONES_ROW + 1, rest, sums).astype(jnp.bfloat16)


def attend(feats, query_cols):
    micro, _, rows_dev = feats.shape
    rows = tile_of(rows_dev, 1152)
    return pl.pallas_call(
        attend_body,
        grid=(micro, rows_dev // rows),
        in_specs=[
            pl.BlockSpec((1, CEXT, rows), lambda m, t: (m, 0, t)),
            pl.BlockSpec((CEXT, LAT), lambda m, t: (0, 0)),
        ],
        out_specs=[
            pl.BlockSpec((1, rows, LAT), lambda m, t: (m, t, 0)),
            pl.BlockSpec((1, CEXT, LAT), lambda m, t: (m, 0, 0)),
        ],
        out_shape=[
            jax.ShapeDtypeStruct((micro, rows_dev, LAT), jnp.bfloat16),
            jax.ShapeDtypeStruct((micro, CEXT, LAT), jnp.bfloat16),
        ],
        scratch_shapes=[pltpu.VMEM((CEXT, LAT), jnp.float32)],
        cost_estimate=cost(8 * micro * rows_dev * LAT * CEXT, 4 * micro * rows_dev * LAT),
        name="attend",
    )(feats, query_cols)


def tiles_of(feats):
    rows_dev = feats.shape[2]
    return rows_dev // tile_of(rows_dev, 1152)


def parts_of(feats):
    micro = feats.shape[0]
    tiles = tiles_of(feats)
    parts = []
    for m in range(micro):
        sizes = [tiles]
        if m == micro - 1 and tiles >= 4:
            sizes = [tiles // 4, tiles // 2, tiles - tiles // 4 - tiles // 2]
        parts += [(m, sum(sizes[:at]), size) for at, size in enumerate(sizes)]
    return parts


def attend_back_body(scale_ref, feat_ref, exp_ref, gain_ref, dc_ref, qc_ref, *rest):
    grad_ref, score_ref, gain_sum_ref = rest[-3:]
    spans = short_spans_of(feat_ref.shape[2])
    d_cols = dc_ref[0]
    both_cols = jnp.concatenate([qc_ref[...], d_cols], axis=1)

    @pl.when(pl.program_id(0) == 0)
    def _():
        score_ref[...] = jnp.zeros_like(score_ref)
        gain_sum_ref[...] = jnp.zeros_like(gain_sum_ref)

    def products(at):
        first, size = spans[at]
        feats = feat_ref[0, :, first : first + size]
        weights = exp_ref[0, first : first + size]
        d_exp = contract_rows(feats, d_cols)
        d_scores = (weights.astype(jnp.float32) * d_exp).astype(jnp.bfloat16)
        d_pix = dot_last(both_cols, jnp.concatenate([d_scores, weights], axis=1))
        return (dot(feats, d_scores), d_pix)

    columns = feat_ref.shape[2]
    whole_lanes = columns % BLK == 0
    if whole_lanes:
        grad_rows = grad_ref.reshape(CIN * columns // BLK, BLK)
    gain = gain_ref[...]
    inverse = 1.0 / gain
    score, d_pix = products(0)
    gain_sum = gain_sum_ref[...]
    for at, (first, size) in enumerate(spans):
        ahead = products(at + 1) if at + 1 < len(spans) else None
        for column in range(0, size, BLK):
            width = min(BLK, size - column)
            inside = slice(first + column, first + column + width)
            feats = feat_ref[0, :, inside].astype(jnp.float32)[:CIN]
            part = d_pix[:CIN, column : column + width]
            scale = scale_ref[0, :, inside]
            along = feats * part
            if width == BLK:
                gain_sum = gain_sum + along
            else:
                gain_sum = gain_sum + jnp.sum(along, axis=1, keepdims=True) * (1.0 / BLK)
            along = jnp.mean(along, axis=0, keepdims=True) * scale
            d_normed = part * gain
            level = jnp.mean(d_normed, axis=0, keepdims=True) * scale
            grad = d_normed * scale - level - feats * inverse * along
            if whole_lanes:
                at_row = (first + column) // BLK
                grad_rows[pl.ds(at_row, WHOLE, stride=columns // BLK), :] = grad[:WHOLE]
                grad_ref[0, WHOLE:, 0, inside] = grad[WHOLE:]
            else:
                grad_ref[0, :, 0, inside] = grad
        if ahead is not None:
            score = score + ahead[0]
            d_pix = ahead[1]
    score_ref[...] += score
    gain_sum_ref[...] = gain_sum


def attend_back(part, earlier, scales, feats, weights, gain_column, d_cols, query_cols):
    m, first, tiles = part
    rows = feats.shape[2] // tiles_of(feats)
    in_specs = [
        pl.BlockSpec((1, 1, rows), lambda t: (m, 0, first + t)),
        pl.BlockSpec((1, CEXT, rows), lambda t: (m, 0, first + t)),
        pl.BlockSpec((1, rows, LAT), lambda t: (m, first + t, 0)),
        pl.BlockSpec((CIN, 1), lambda t: (0, 0)),
        pl.BlockSpec((1, CEXT, LAT), lambda t: (m, 0, 0)),
        pl.BlockSpec((CEXT, LAT), lambda t: (0, 0)),
    ]
    operands = [scales, feats, weights, gain_column, d_cols, query_cols]
    aliases = {}
    if earlier is not None:
        in_specs.append(pl.BlockSpec(memory_space=pl.ANY))
        aliases = {len(operands): 0}
        operands.append(earlier)
    return pl.pallas_call(
        attend_back_body,
        grid=(tiles,),
        in_specs=in_specs,
        out_specs=[
            pl.BlockSpec((1, CIN, 1, rows), lambda t: (m, 0, 0, first + t)),
            pl.BlockSpec((CEXT, LAT), lambda t: (0, 0)),
            pl.BlockSpec((CIN, BLK), lambda t: (0, 0)),
        ],
        out_shape=[
            jax.ShapeDtypeStruct((feats.shape[0], CIN, 1, feats.shape[2]), jnp.float32),
            jax.ShapeDtypeStruct((CEXT, LAT), jnp.float32),
            jax.ShapeDtypeStruct((CIN, BLK), jnp.float32),
        ],
        input_output_aliases=aliases,
        cost_estimate=cost(16 * tiles * rows * LAT * CEXT, tiles * rows * 4000),
        name="attend_back",
    )(*operands)


def query_body(block_ref, lat_ref, gain_ref, key_ref, *rest):
    sources, (low_ref, query_ref, cols_ref, wq_ref, wo_ref, w1_ref, w2_ref, sems) = (
        rest[:-8],
        rest[-8:],
    )
    squares = (wq_ref, wo_ref, w1_ref, w2_ref)
    side = DL // BLK
    first = 0
    for source in sources:

        @pl.loop(0, source.shape[0])
        def _(at, source=source, first=first):
            block = block_ref[first + at]
            row = pl.multiple_of((block % PER_MATRIX // side) * BLK, BLK)
            column = pl.multiple_of((block % side) * BLK, BLK)
            for matrix in range(4):

                @pl.when(block // PER_MATRIX == matrix)
                def _(matrix=matrix):
                    pltpu.make_async_copy(
                        source.at[at],
                        squares[matrix].at[pl.ds(row, BLK), pl.ds(column, BLK)],
                        sems.at[matrix],
                    ).start()

        first += source.shape[0]

    def settle(matrix):
        pltpu.make_async_copy(squares[matrix], squares[matrix], sems.at[matrix]).wait()

    lat_low = (standardize(lat_ref[...]) * gain_ref[...]).astype(jnp.bfloat16)
    low_ref[...] = lat_low
    settle(0)
    query = dot(lat_low, wq_ref[...]).astype(jnp.bfloat16)
    query_ref[...] = query
    scores = dot_last(key_ref[...], query) * (1.0 / math.sqrt(DL))
    row = lax.broadcasted_iota(jnp.int32, scores.shape, 0)
    cols_ref[...] = jnp.where(row == MASK_ROW, 1.0, scores).astype(jnp.bfloat16)
    for matrix in range(1, 4):
        settle(matrix)


def make_query(blocks, sources, latent_array, gain, w_key):
    vmem = pl.BlockSpec(memory_space=pltpu.VMEM)
    hbm = pl.BlockSpec(memory_space=pl.ANY)
    rows = jax.ShapeDtypeStruct((LAT, DL), jnp.bfloat16)
    square = jax.ShapeDtypeStruct((DL, DL), jnp.bfloat16)
    return pl.pallas_call(
        query_body,
        in_specs=[pl.BlockSpec(memory_space=pltpu.SMEM), vmem, vmem, vmem] + [hbm] * len(sources),
        out_specs=[vmem] * 7,
        out_shape=[rows, rows, jax.ShapeDtypeStruct((CEXT, LAT), jnp.bfloat16)] + [square] * 4,
        scratch_shapes=[pltpu.SemaphoreType.DMA((4,))],
        cost_estimate=cost(3 * LAT * DL * DL, 4 * NBLK * BLK * BLK),
        name="make_query",
    )(blocks, latent_array, gain[None], w_key, *sources)


def image_sums_body(where_ref, *rest):
    n_img = len(rest) - 7
    pieces, (grads_ref, value_ref, resid_ref, rows_ref, full_ref, zero_ref, sems) = (
        rest[:n_img],
        rest[n_img:],
    )
    side = DL // BLK
    count = pieces[0].shape[1]

    def put(source, block):
        place = where_ref[n_img + block]

        @pl.when(place >= 0)
        def _():
            pltpu.make_async_copy(source, grads_ref.at[place], sems.at[1]).start()

    for piece in range(n_img):
        first = pl.multiple_of(where_ref[piece] * count, count)
        pltpu.make_async_copy(
            pieces[piece], rows_ref.at[:, pl.ds(first, count), :], sems.at[0]
        ).start()
    zero_ref[...] = jnp.zeros_like(zero_ref)

    @pl.loop(0, PER_MATRIX)
    def _(block):
        put(zero_ref, block)

    pltpu.make_async_copy(rows_ref, rows_ref, sems.at[0]).wait()
    for matrix in range(3):
        full_ref[matrix] = contract_rows(rows_ref[matrix], rows_ref[3 + matrix]).astype(jnp.bfloat16)

        @pl.loop(0, PER_MATRIX)
        def _(block, matrix=matrix):
            row = pl.multiple_of((block // side) * BLK, BLK)
            column = pl.multiple_of((block % side) * BLK, BLK)
            put(
                full_ref.at[matrix, pl.ds(row, BLK), pl.ds(column, BLK)],
                (matrix + 1) * PER_MATRIX + block,
            )

    value_ref[...] = contract_rows(rows_ref[7, :, :CEXT], rows_ref[6]).astype(jnp.bfloat16)
    each = resid_ref.shape[0]
    total = rows_ref[3, :each, :].astype(jnp.float32)
    for first in range(each, rows_ref.shape[1], each):
        total = total + rows_ref[3, first : first + each, :].astype(jnp.float32)
    resid_ref[...] = total.astype(jnp.bfloat16)
    pltpu.make_async_copy(grads_ref, grads_ref, sems.at[1]).wait()


def image_sums(where, pieces, lat_rows):
    n_img = len(pieces)
    slabs, count, _ = pieces[0].shape
    hbm = pl.BlockSpec(memory_space=pl.ANY)
    vmem = pl.BlockSpec(memory_space=pltpu.VMEM)
    return pl.pallas_call(
        image_sums_body,
        in_specs=[pl.BlockSpec(memory_space=pltpu.SMEM)] + [hbm] * n_img,
        out_specs=[hbm, vmem, vmem],
        out_shape=[
            jax.ShapeDtypeStruct((NBLK // n_img, BLK, BLK), jnp.bfloat16),
            jax.ShapeDtypeStruct((CEXT, DL), jnp.bfloat16),
            jax.ShapeDtypeStruct((lat_rows, DL), jnp.bfloat16),
        ],
        scratch_shapes=[
            pltpu.VMEM((slabs, n_img * count, DL), jnp.bfloat16),
            pltpu.VMEM((3, DL, DL), jnp.bfloat16),
            pltpu.VMEM((BLK, BLK), jnp.bfloat16),
            pltpu.SemaphoreType.DMA((2,)),
        ],
        cost_estimate=cost(8 * n_img * count * DL * DL, 16 * DL * DL),
        name="image_sums",
    )(where, *pieces)


def two_bf16(values_in):
    head = values_in.astype(jnp.bfloat16)
    return (head, (values_in - head.astype(jnp.float32)).astype(jnp.bfloat16))


def product_f32(left_side, right_side):
    left_head, left_rest = two_bf16(left_side)
    right_head, right_rest = two_bf16(right_side)
    both = dot(
        jnp.concatenate([left_head, left_rest], axis=1),
        jnp.concatenate([right_head, right_head], axis=0),
    )
    return both + dot(left_head, right_rest)


def update_body(block_ref, lat_ref, dq_ref, sum_ref, ls_ref, rs_ref, lr_ref, rr_ref, ma_ref, *outs):
    new_left, new_right, new_master, new_copy = outs
    side = DL // BLK
    for slot in range(ma_ref.shape[0]):
        block = block_ref[slot]
        is_query = block < PER_MATRIX
        inside = jnp.where(is_query, block, 0)
        row = pl.multiple_of(inside // side * BLK, BLK)
        column = pl.multiple_of(inside % side * BLK, BLK)
        own = contract_rows(lat_ref[:, pl.ds(row, BLK)], dq_ref[:, pl.ds(column, BLK)])
        grad = jnp.where(is_query, own, sum_ref[slot])
        turned = grad.T
        new_left[slot] = 0.5 * ls_ref[slot] + 0.5 * product_f32(grad, turned)
        new_right[slot] = 0.5 * rs_ref[slot] + 0.5 * product_f32(turned, grad)
        shampoo = product_f32(product_f32(lr_ref[slot], grad), rr_ref[slot])
        mean_square = jnp.mean(shampoo * shampoo)
        updated = ma_ref[slot] - 0.5 / math.sqrt(DL) * (shampoo / jnp.sqrt(mean_square + 1e-06))
        new_master[slot] = updated
        new_copy[slot] = updated.astype(jnp.bfloat16)


def update_slots(blocks, lat_low, d_query, sums, left_stat, right_stat, left_root, right_root, master):
    vmem = pl.BlockSpec(memory_space=pltpu.VMEM)
    shape = jax.ShapeDtypeStruct(master.shape, jnp.float32)
    return pl.pallas_call(
        update_body,
        in_specs=[pl.BlockSpec(memory_space=pltpu.SMEM)] + [vmem] * 8,
        out_specs=[vmem] * 4,
        out_shape=[shape, shape, shape, jax.ShapeDtypeStruct(master.shape, jnp.bfloat16)],
        name="update_slots",
    )(blocks, lat_low, d_query, sums, left_stat, right_stat, left_root, right_root, master)


def root_mean(total, count):
    return jnp.sqrt(total / count + 1e-06)


def finish_body(late_ref, key_ref, query_ref, wq_ref, early_ref, kv_ref, lat_ref, gains_ref, *outs):
    dq_ref, kv_grad_ref, new_kv_ref, lat_grad_ref, new_lat_ref, gain_ref, new_gain_ref = outs
    inv_root = 1.0 / math.sqrt(DL)
    late = late_ref[...]
    d_query = (contract_rows(late, key_ref[...]) * inv_root).astype(jnp.bfloat16)
    dq_ref[...] = d_query
    key_total = (dot(late, query_ref[...]) * inv_root)[:CIN]
    value_total = early_ref[:CEXT, :].astype(jnp.float32)[:CIN]
    for at, grad in enumerate((key_total, value_total)):
        kv_grad_ref[:, at, :] = grad
        step = 0.3 / math.sqrt(CIN) / root_mean(jnp.sum(grad * grad), CIN * DL)
        new_kv_ref[:, at, :] = kv_ref[:, at, :] - step * grad
    d_lat_norm = dot_last(d_query, wq_ref[...])
    lat = lat_ref[...]
    centred = lat - jnp.mean(lat, axis=-1, keepdims=True)
    scale = lax.rsqrt(jnp.mean(centred * centred, axis=-1, keepdims=True) + 1e-05)
    normed = centred * scale
    dy = d_lat_norm * gains_ref[0:1]
    along = jnp.mean(dy * normed, axis=-1, keepdims=True)
    back = (dy - jnp.mean(dy, axis=-1, keepdims=True) - normed * along) * scale
    lat_grad = early_ref[CEXT:, :].astype(jnp.float32) + back
    lat_grad_ref[...] = lat_grad
    new_lat_ref[...] = lat - 0.3 / root_mean(jnp.sum(lat_grad * lat_grad), LAT * DL) * lat_grad
    tail = late[CIN + 1 : CEXT].astype(jnp.float32)
    second = jnp.concatenate([tail[0:1], tail[1:2]], axis=1)
    for at, grad in enumerate((jnp.sum(d_lat_norm * normed, axis=0, keepdims=True), second)):
        gain_ref[at : at + 1] = grad
        step = 0.2 / root_mean(jnp.sum(grad * grad), DL)
        new_gain_ref[at : at + 1] = gains_ref[at : at + 1] - step * grad


def finish(late, w_key, query, w_query, early, kv_weight, latent_array, lat_gains):
    vmem = pl.BlockSpec(memory_space=pltpu.VMEM)
    kv = jnp.swapaxes(kv_weight, 0, 1)
    kv_shape = jax.ShapeDtypeStruct(kv.shape, jnp.float32)
    lat_shape = jax.ShapeDtypeStruct((LAT, DL), jnp.float32)
    gain_shape = jax.ShapeDtypeStruct(lat_gains.shape, jnp.float32)
    outs = pl.pallas_call(
        finish_body,
        in_specs=[vmem] * 8,
        out_specs=[vmem] * 7,
        out_shape=[jax.ShapeDtypeStruct((LAT, DL), jnp.bfloat16)]
        + [kv_shape] * 2
        + [lat_shape] * 2
        + [gain_shape] * 2,
        name="finish",
    )(late, w_key, query, w_query, early, kv, latent_array, lat_gains)
    d_query, kv_grad, new_kv, *others = outs
    return (d_query, jnp.swapaxes(kv_grad, 0, 1), jnp.swapaxes(new_kv, 0, 1), *others)


def swap(array, axis):
    return lax.all_to_all(array, axis, 0, 0, tiled=True)


def everyone(array, axis):
    return swap(jnp.broadcast_to(array[None], (lax.axis_size(axis), *array.shape)), axis)


def near_hop(array, axis):
    size = lax.axis_size(axis)
    return lax.ppermute(array, axis, [(i, i ^ 1) for i in range(size)])


def far_hop(array, axis, step):
    size = lax.axis_size(axis)
    return lax.ppermute(array, axis, [(i, (i + 2 * step) % size) for i in range(size)])


def spread(array, rows, axis, hops):
    size = lax.axis_size(axis)
    column = {("img", "far"): 0, ("img", "near"): 1, ("pix", "far"): 2, ("pix", "near"): 3}
    got = [array]
    places = [rows]
    for step in range(1, 2 if hops == "near" else size // 2):
        got.append(near_hop(array, axis) if hops == "near" else far_hop(array, axis, step))
        moved = rows.copy()
        moved[:, column[axis, hops]] += step
        places.append(moved)
    return (jnp.concatenate(got), np.concatenate(places))


ROUTES = (
    (("pix", "near"), ("img", "far"), ("pix", "far")),
    (("img", "far"), ("pix", "far"), ("pix", "near")),
    (("pix", "far"), ("pix", "near"), ("img", "far")),
)


def gather_blocks(low, feats):
    slots_dev = low.shape[0]
    n_pix = lax.axis_size("pix")
    if slots_dev < 4 or n_pix > 8:
        low = lax.all_gather(low, ("img", "pix"), axis=0, tiled=True)
        return ([low], jnp.arange(NBLK), feats)
    quarter = slots_dev // 4
    states = []
    bounds = (0, quarter, 2 * quarter, slots_dev)
    for part in range(3):
        start, stop = bounds[part], bounds[part + 1]
        rows = np.zeros((stop - start, 5), np.int32)
        rows[:, 4] = np.arange(start, stop)
        states.append((low[start:stop], rows))
    for phase in range(3):
        states = [spread(*state, *ROUTES[part][phase]) for part, state in enumerate(states)]
    held, feats = lax.optimization_barrier(([array for array, _ in states], feats))
    arrays = []
    places = []
    for array, (_, rows) in zip(held, states):
        arrays += [array, near_hop(array, "img")]
        mate = rows.copy()
        mate[:, 1] += 1
        places += [rows, mate]
    img_far, img_near, pix_far, pix_near, slot = np.concatenate(places).T
    img = lax.axis_index("img")
    pix = lax.axis_index("pix")
    n_far = lax.axis_size("img") // 2
    img_of = (img // 2 - img_far) % n_far * 2 + (img + img_near) % 2
    pix_of = (pix // 2 - pix_far) % (n_pix // 2) * 2 + (pix + pix_near) % 2
    return (arrays, (img_of * n_pix + pix_of) * slots_dev + slot, feats)


def split_near(array, axis):
    size = lax.axis_size(axis)
    near = lax.axis_index(axis) % 2
    pairs = array.reshape(size // 2, 2, *array.shape[1:])
    return (
        lax.dynamic_index_in_dim(pairs, near, 1, False),
        lax.dynamic_index_in_dim(pairs, 1 - near, 1, False),
    )


def join_near(kept, sent, axis):
    got = near_hop(sent, axis)
    return (kept.astype(jnp.float32) + got.astype(jnp.float32)).astype(jnp.bfloat16)


def sum_far(kept, axis):
    size = lax.axis_size(axis)
    far = lax.axis_index(axis) // 2
    total = lax.dynamic_index_in_dim(kept, far, 0, False).astype(jnp.float32)
    for step in range(1, size // 2):
        part = lax.dynamic_index_in_dim(kept, (far + step) % (size // 2), 0, False)
        total = total + far_hop(part, axis, step).astype(jnp.float32)
    return total


def gather_far(array, axis):
    size = lax.axis_size(axis)
    far = lax.axis_index(axis) // 2
    got = [array] + [far_hop(array, axis, step) for step in range(1, size // 2)]
    return lax.dynamic_slice_in_dim(jnp.stack(got[::-1] * 2), size // 2 - 1 - far, size // 2, 0)


def gather_near(array, axis):
    near = lax.axis_index(axis) % 2
    other = near_hop(array, axis)
    both = jnp.where(
        near == 0, jnp.stack([array, other], axis=1), jnp.stack([other, array], axis=1)
    )
    return both.reshape(lax.axis_size(axis), *array.shape[1:])


def latent_pass(numerator, denominator, lat_part, cot_rows, lat_gain, w_out, w_up, w_down):
    attended = numerator / denominator[..., None]
    att_low = attended.astype(jnp.bfloat16)
    resid = lat_part[None] + product("mrd,de->mre", att_low, w_out)
    normed, normed_back = jax.vjp(standardize, resid)
    hn_low = (normed * lat_gain).astype(jnp.bfloat16)
    hidden = product("mrd,de->mre", hn_low, w_up)
    active, active_back = jax.vjp(gelu_exact, hidden)
    act_low = active.astype(jnp.bfloat16)
    latents_out = resid + product("mrd,de->mre", act_low, w_down)
    g_mlp = cot_rows.astype(jnp.bfloat16)
    d_active = product("mre,de->mrd", g_mlp, w_down)
    d_hidden = active_back(d_active)[0].astype(jnp.bfloat16)
    d_normed = product("mre,de->mrd", d_hidden, w_up)
    d_resid = cot_rows + normed_back(d_normed * lat_gain)[0]
    d_branch = d_resid.astype(jnp.bfloat16)
    d_attended = product("mre,de->mrd", d_branch, w_out)
    d_numer = d_attended / denominator[..., None]
    d_denom = -jnp.sum(d_attended * numerator / (denominator * denominator)[..., None], axis=-1)
    gain_mlp = jnp.sum(d_normed * normed, axis=(0, 1))
    row_arrays = (att_low, hn_low, act_low, d_branch, d_hidden, g_mlp)
    return (latents_out, d_numer.astype(jnp.bfloat16), d_denom, (row_arrays, gain_mlp))


def shards(
    pixels,
    sides,
    owner,
    master,
    left_stat,
    right_stat,
    left_root,
    right_root,
    kv_weight,
    latent_array,
    in_gain,
    lat_gains,
    cotangent,
):
    micro = pixels.shape[0]
    rows_dev = pixels.shape[2]
    n_pix = lax.axis_size("pix")
    n_img = lax.axis_size("img")
    img = lax.axis_index("img")
    pix = lax.axis_index("pix")
    slots_dev = master.shape[0]
    lat_rows = LAT // n_pix
    row_start = pix * lat_rows
    inv_root = 1.0 / math.sqrt(DL)

    place = jnp.concatenate([(pix * rows_dev)[None], sides * sides]).astype(jnp.int32)
    across = lies_across(pixels)
    gain_column = in_gain[:, None]
    feats = None
    for micro_index in range(micro - 1):
        feats = prepare_pixels(micro_index, feats, place, across, gain_column)
    sources, source_slots, feats = gather_blocks(master.astype(jnp.bfloat16), feats)
    feats, scales = prepare_pixels(micro - 1, feats, place, across, gain_column)
    all_blocks = jnp.arange(NBLK, dtype=jnp.int32)
    source_blocks = jnp.sum(
        jnp.where(source_slots[:, None] == owner[None], all_blocks[None], 0), axis=1
    )
    kv_low = kv_weight.astype(jnp.bfloat16)
    w_key = jnp.pad(kv_low[0], ((0, CEXT - CIN), (0, 0)))
    w_value = kv_low[1]
    lat_low, query, query_cols, w_query, w_out, w_up, w_down = make_query(
        source_blocks.astype(jnp.int32), sources, latent_array, lat_gains[0], w_key
    )

    weights, sums = attend(feats, query_cols)
    sums = sums.reshape(micro, CEXT, n_pix, lat_rows).transpose(2, 1, 0, 3)
    sums = swap(sums.reshape(n_pix, CEXT, micro * lat_rows), "pix")
    sums = jnp.sum(sums.astype(jnp.float32), axis=0)
    numer_in = sums[:CIN]
    denominator = (sums[ONES_ROW] + sums[ONES_ROW + 1]).reshape(micro, lat_rows)
    numerator = fine("cr,cd->rd", numer_in, w_value).reshape(micro, lat_rows, DL)
    latents_out, d_numer, d_denom, latent_grads = latent_pass(
        numerator,
        denominator,
        lax.dynamic_slice_in_dim(latent_array, row_start, lat_rows, 0),
        cotangent[:, 0],
        lat_gains[1],
        w_out,
        w_up,
        w_down,
    )
    row_arrays, gain_mlp = latent_grads
    d_numer = d_numer.reshape(micro * lat_rows, DL)
    head, rest = two_terms(d_denom.reshape(1, micro * lat_rows))
    d_cols = product("rd,cd->cr", d_numer, w_value).astype(jnp.bfloat16)
    d_cols = jnp.concatenate([d_cols, head, rest, jnp.zeros_like(head)], axis=0)
    d_cols = everyone(d_cols, "pix").reshape(n_pix, CEXT, micro, lat_rows)
    d_cols = d_cols.transpose(2, 1, 0, 3).reshape(micro, CEXT, LAT)

    numer_rows = jnp.pad(numer_in.astype(jnp.bfloat16).T, ((0, 0), (0, DL - CIN)))
    own = jnp.stack(
        [array.reshape(micro * lat_rows, DL) for array in row_arrays] + [d_numer, numer_rows]
    )
    mate = [(i, i ^ 1) for i in range(n_img)]
    pieces = [own, lax.ppermute(own, "img", mate)]
    images = [img, img ^ 1]
    far = []
    for step in range(1, n_img // 2):
        hop = [(i, (i + 2 * step) % n_img) for i in range(n_img)]
        far.append(lax.ppermute(own, "img", hop))
        images += [(img - 2 * step) % n_img, (img - 2 * step) % n_img ^ 1]
    device_of = owner // slots_dev
    place_of = device_of % n_pix * slots_dev + owner % slots_dev
    where = jnp.where(device_of // n_pix == img, place_of, -1)

    results = (None,)
    score_sum = jnp.zeros((CEXT, LAT), jnp.float32)
    gain_sum = jnp.zeros((CIN, BLK), jnp.float32)
    width = DL // 2
    each = -(-CEXT // n_pix)
    parts = parts_of(feats)
    for at, part in enumerate(parts):
        if at == len(parts) - 2:
            far, gain_sum = lax.optimization_barrier((far, gain_sum))
            for piece in far:
                pieces += [piece, lax.ppermute(piece, "img", mate)]
        if at == len(parts) - 1:
            pieces, gain_sum = lax.optimization_barrier((pieces, gain_sum))
            where = jnp.concatenate([jnp.stack(images), where]).astype(jnp.int32)
            grads, value_part, resid_part = image_sums(where, pieces, lat_rows)
            value_part = jnp.pad(value_part, ((0, each * n_pix - CEXT), (0, 0)))
            value_part = lax.dynamic_slice_in_dim(value_part, img % 2 * width, width, 1)
            value_sides = split_near(value_part.reshape(n_pix, each, width), "pix")
            grad_sides = split_near(grads.reshape(n_pix, slots_dev, BLK, BLK), "pix")
            gain_column, value_sides, grad_sides = lax.optimization_barrier(
                (gain_column, value_sides, grad_sides)
            )
        results = attend_back(
            part, results[0], scales, feats, weights, gain_column, d_cols, query_cols
        )
        score_sum = score_sum + results[1]
        gain_sum = gain_sum + results[2]
    pixel_grad = jnp.swapaxes(results[0].reshape(micro, 1, CIN, rows_dev), 2, 3)

    gain_sum = jnp.sum(gain_sum, axis=1)[None] / in_gain[None]
    late = jnp.concatenate(
        [
            score_sum[:CIN],
            jnp.pad(gain_sum, ((0, 0), (0, LAT - CIN))),
            gain_mlp.reshape(DL // LAT, LAT),
        ],
        axis=0,
    ).astype(jnp.bfloat16)
    late = jnp.pad(late, ((0, each * n_pix - CEXT), (0, 0))).reshape(n_pix, each, LAT)
    value_part = join_near(*value_sides, "pix")
    late, value_part = lax.optimization_barrier((late, value_part))
    late = jnp.sum(swap(late, "pix").astype(jnp.float32), axis=0)
    value_part = sum_far(value_part, "pix").astype(jnp.bfloat16)
    grads = join_near(*grad_sides, "pix")
    late, value_part, grads = lax.optimization_barrier((late, value_part, grads))
    late = jnp.sum(everyone(late, "img"), axis=0).astype(jnp.bfloat16)
    resid_part = lax.dynamic_slice_in_dim(resid_part, img % 2 * width, width, 1)
    early = gather_far(jnp.concatenate([value_part, resid_part], axis=0), "pix")
    late, early = lax.optimization_barrier((late, early))
    grads = sum_far(grads, "pix")
    late = everyone(late, "pix").reshape(n_pix * each, LAT)[:CEXT]
    early = gather_near(early, "pix")
    value_part = early[:, :each].reshape(n_pix * each, width)[:CEXT]
    early = jnp.concatenate([value_part, early[:, each:].reshape(LAT, width)], axis=0)
    other = near_hop(early, "img")
    early = jnp.where(
        img % 2 == 0,
        jnp.concatenate([early, other], axis=1),
        jnp.concatenate([other, early], axis=1),
    )
    d_query, kv_grad, new_kv, latent_grad, new_latent, lat_gain_grad, new_lat_gains = finish(
        late, w_key, query, w_query, early, kv_weight, latent_array, lat_gains
    )
    in_gain_grad = late[CIN, :CIN].astype(jnp.float32)

    mine = (img * n_pix + pix) * slots_dev + jnp.arange(slots_dev, dtype=jnp.int32)
    blocks = jnp.sum(
        jnp.where(owner[None] == mine[:, None], all_blocks[None], 0), axis=1
    )
    new_left, new_right, new_master, new_copy = update_slots(
        blocks.astype(jnp.int32),
        lat_low,
        d_query,
        grads,
        left_stat,
        right_stat,
        left_root,
        right_root,
        master,
    )
    new_in_gain = in_gain - 0.2 * normalized(in_gain_grad, (0,))
    return (
        latents_out[:, None],
        pixel_grad,
        new_left,
        new_right,
        new_master,
        new_copy,
        kv_grad,
        new_kv,
        latent_grad,
        new_latent,
        in_gain_grad,
        new_in_gain,
        lat_gain_grad,
        new_lat_gains,
    )


def solution(mesh):
    pixel_spec = P(None, "img", "pix", None)
    slot_spec = P(("img", "pix"), None, None)
    in_specs = (
        (pixel_spec, P(), P()) + (slot_spec,) * 5 + (P(),) * 4 + (pixel_spec,)
    )
    out_specs = (pixel_spec, pixel_spec) + (slot_spec,) * 4 + (P(),) * 8
    return jax.shard_map(shards, mesh=mesh, in_specs=in_specs, out_specs=out_specs, check_vma=False)
```

```python
import functools
import math

import jax
import jax.numpy as jnp
from jax import lax
import numpy as np
from jax.experimental import pallas as pl
from jax.experimental.pallas import tpu as pltpu
from jax.sharding import PartitionSpec as P

CIN = 261
DL = 1024
LAT = 512
BLK = 128
NBLK = 256
PER_MATRIX = NBLK // 4
CEXT = 264
WHOLE = CIN // 8 * 8
ONES_ROW = 261
MASK_ROW = 263
MASKED = -1e30

HIGHEST_PRECISION = lax.Precision.HIGHEST


def standardize(values_in):
    average = jnp.mean(values_in, axis=-1, keepdims=True)
    centred = values_in - average
    variance = jnp.mean(centred * centred, axis=-1, keepdims=True)
    return centred * lax.rsqrt(variance + 1e-05)


def gelu_exact(values_in):
    return jax.nn.gelu(values_in, approximate=False)


def normalized(gradient, reduce_axes):
    return gradient / jnp.sqrt(
        jnp.mean(gradient * gradient, axis=reduce_axes, keepdims=True) + 1e-06
    )


def product(pattern, left_side, right_side):
    return jnp.einsum(pattern, left_side, right_side, preferred_element_type=jnp.float32)


def fine(pattern, left_side, right_side):
    return jnp.einsum(
        pattern,
        left_side.astype(jnp.float32),
        right_side.astype(jnp.float32),
        precision=HIGHEST_PRECISION,
    )


def two_terms(values_in):
    head = lax.reduce_precision(values_in, 8, 7)
    return (head.astype(jnp.bfloat16), (values_in - head).astype(jnp.bfloat16))


def contract_rows(left_side, right_side, precision=None):
    return lax.dot_general(
        left_side,
        right_side,
        (((0,), (0,)), ((), ())),
        precision=precision,
        preferred_element_type=jnp.float32,
    )


def dot(left_side, right_side):
    return jnp.dot(left_side, right_side, preferred_element_type=jnp.float32)


def dot_last(left_side, right_side):
    return lax.dot_general(
        left_side, right_side, (((1,), (1,)), ((), ())), preferred_element_type=jnp.float32
    )


def tile_of(rows, most):
    return max((size for size in range(128, most + 1, 128) if rows % size == 0), default=rows)


def lies_across(pixels):
    micro, _, rows_dev, _ = pixels.shape
    return jnp.swapaxes(pixels, 2, 3).reshape(micro, CIN, 1, rows_dev)


def centre(pix):
    centred = pix - jnp.mean(pix, axis=0, keepdims=True)
    scale = lax.rsqrt(jnp.mean(centred * centred, axis=0, keepdims=True) + 1e-05)
    return (centred * scale, scale)


def cost(flops, count):
    return pl.CostEstimate(flops=int(flops), bytes_accessed=int(count), transcendentals=0)


def prepare_body(place_ref, pix_ref, gain_ref, *rest, micro_index):
    out_ref, scale_ref = rest[-2:]
    columns = pix_ref.shape[3]
    gain = gain_ref[...]
    width = BLK if columns % BLK == 0 else columns
    if width == BLK:
        pix_rows = pix_ref.reshape(CIN * columns // BLK, BLK)
    extra = (CEXT - CIN, width)
    row = lax.broadcasted_iota(jnp.int32, extra, 0) + CIN
    slot = place_ref[0] + pl.program_id(0) * columns + lax.broadcasted_iota(jnp.int32, extra, 1)
    for column in range(0, columns, width):
        inside = slice(column, column + width)
        if width == BLK:
            pix = jnp.concatenate(
                [
                    pix_rows[pl.ds(column // BLK, WHOLE, stride=columns // BLK), :],
                    pix_ref[0, WHOLE:, 0, inside],
                ],
                axis=0,
            )
        else:
            pix = pix_ref[0, :, 0, :]
        normed, scale_ref[0, :, inside] = centre(pix)
        mask = jnp.where(slot + column < place_ref[1 + micro_index], 0.0, MASKED)
        tail = jnp.where(row == MASK_ROW, mask, 1.0)
        full = jnp.concatenate([normed * gain, tail], axis=0)
        out_ref[0, :, inside] = full.astype(jnp.bfloat16)


def prepare_pixels(micro_index, earlier, place, across, gain_column):
    micro, _, _, rows_dev = across.shape
    rows = tile_of(rows_dev, 1152)
    m = micro_index
    in_specs = [
        pl.BlockSpec(memory_space=pltpu.SMEM),
        pl.BlockSpec((1, CIN, 1, rows), lambda t: (m, 0, 0, t)),
        pl.BlockSpec((CIN, 1), lambda t: (0, 0)),
    ]
    operands = [place, across, gain_column]
    aliases = {}
    if earlier is not None:
        in_specs += [pl.BlockSpec(memory_space=pl.ANY)] * 2
        aliases = {len(operands): 0, len(operands) + 1: 1}
        operands += earlier
    return pl.pallas_call(
        functools.partial(prepare_body, micro_index=m),
        grid=(rows_dev // rows,),
        in_specs=in_specs,
        out_specs=[
            pl.BlockSpec((1, CEXT, rows), lambda t: (m, 0, t)),
            pl.BlockSpec((1, 1, rows), lambda t: (m, 0, t)),
        ],
        out_shape=[
            jax.ShapeDtypeStruct((micro, CEXT, rows_dev), jnp.bfloat16),
            jax.ShapeDtypeStruct((micro, 1, rows_dev), jnp.float32),
        ],
        input_output_aliases=aliases,
        cost_estimate=cost(0, 12 * rows_dev * CEXT),
        name="prepare_pixels",
    )(*operands)


def spans_of(columns):
    if columns == 1152:
        return ((0, 512), (512, 384), (896, 256))
    return ((0, columns),)


def short_spans_of(columns):
    if columns == 1152:
        return tuple((first, min(256, columns - first)) for first in range(0, columns, 256))
    return ((0, columns),)


def attend_body(feat_ref, query_ref, exp_ref, out_ref, sum_ref):
    tile = pl.program_id(1)
    spans = spans_of(feat_ref.shape[2])
    query = query_ref[...]

    def scores_of(at):
        first, size = spans[at]
        return contract_rows(feat_ref[0, :, first : first + size], query)

    @pl.when(tile == 0)
    def _():
        sum_ref[...] = jnp.zeros_like(sum_ref)

    scores = scores_of(0)
    total = sum_ref[...]
    for at, (first, size) in enumerate(spans):
        ahead = scores_of(at + 1) if at + 1 < len(spans) else None
        weights = jnp.exp(scores).astype(jnp.bfloat16)
        exp_ref[0, first : first + size] = weights
        total = total + dot(feat_ref[0, :, first : first + size], weights)
        scores = ahead
    sum_ref[...] = total

    @pl.when(tile == pl.num_programs(1) - 1)
    def _():
        sums = sum_ref[...]
        low = sums.astype(jnp.bfloat16)
        rest = (sums - low.astype(jnp.float32))[ONES_ROW : ONES_ROW + 1]
        row = lax.broadcasted_iota(jnp.int32, sums.shape, 0)
        out_ref[0] = jnp.where(row == ONES_ROW + 1, rest, sums).astype(jnp.bfloat16)


def attend(feats, query_cols):
    micro, _, rows_dev = feats.shape
    rows = tile_of(rows_dev, 1152)
    return pl.pallas_call(
        attend_body,
        grid=(micro, rows_dev // rows),
        in_specs=[
            pl.BlockSpec((1, CEXT, rows), lambda m, t: (m, 0, t)),
            pl.BlockSpec((CEXT, LAT), lambda m, t: (0, 0)),
        ],
        out_specs=[
            pl.BlockSpec((1, rows, LAT), lambda m, t: (m, t, 0)),
            pl.BlockSpec((1, CEXT, LAT), lambda m, t: (m, 0, 0)),
        ],
        out_shape=[
            jax.ShapeDtypeStruct((micro, rows_dev, LAT), jnp.bfloat16),
            jax.ShapeDtypeStruct((micro, CEXT, LAT), jnp.bfloat16),
        ],
        scratch_shapes=[pltpu.VMEM((CEXT, LAT), jnp.float32)],
        cost_estimate=cost(8 * micro * rows_dev * LAT * CEXT, 4 * micro * rows_dev * LAT),
        name="attend",
    )(feats, query_cols)


def tiles_of(feats):
    rows_dev = feats.shape[2]
    return rows_dev // tile_of(rows_dev, 1152)


def parts_of(feats):
    micro = feats.shape[0]
    tiles = tiles_of(feats)
    parts = []
    for m in range(micro):
        sizes = [tiles]
        if m == micro - 1 and tiles >= 4:
            sizes = [tiles // 4, tiles // 2, tiles - tiles // 4 - tiles // 2]
        parts += [(m, sum(sizes[:at]), size) for at, size in enumerate(sizes)]
    return parts


def attend_back_body(scale_ref, feat_ref, exp_ref, gain_ref, dc_ref, qc_ref, *rest):
    grad_ref, score_ref, gain_sum_ref = rest[-3:]
    spans = short_spans_of(feat_ref.shape[2])
    d_cols = dc_ref[0]
    both_cols = jnp.concatenate([qc_ref[...], d_cols], axis=1)

    @pl.when(pl.program_id(0) == 0)
    def _():
        score_ref[...] = jnp.zeros_like(score_ref)
        gain_sum_ref[...] = jnp.zeros_like(gain_sum_ref)

    def products(at):
        first, size = spans[at]
        feats = feat_ref[0, :, first : first + size]
        weights = exp_ref[0, first : first + size]
        d_exp = contract_rows(feats, d_cols)
        d_scores = (weights.astype(jnp.float32) * d_exp).astype(jnp.bfloat16)
        d_pix = dot_last(both_cols, jnp.concatenate([d_scores, weights], axis=1))
        return (dot(feats, d_scores), d_pix)

    columns = feat_ref.shape[2]
    whole_lanes = columns % BLK == 0
    if whole_lanes:
        grad_rows = grad_ref.reshape(CIN * columns // BLK, BLK)
    gain = gain_ref[...]
    inverse = 1.0 / gain
    score, d_pix = products(0)
    gain_sum = gain_sum_ref[...]
    for at, (first, size) in enumerate(spans):
        ahead = products(at + 1) if at + 1 < len(spans) else None
        for column in range(0, size, BLK):
            width = min(BLK, size - column)
            inside = slice(first + column, first + column + width)
            feats = feat_ref[0, :, inside].astype(jnp.float32)[:CIN]
            part = d_pix[:CIN, column : column + width]
            scale = scale_ref[0, :, inside]
            along = feats * part
            if width == BLK:
                gain_sum = gain_sum + along
            else:
                gain_sum = gain_sum + jnp.sum(along, axis=1, keepdims=True) * (1.0 / BLK)
            along = jnp.mean(along, axis=0, keepdims=True) * scale
            d_normed = part * gain
            level = jnp.mean(d_normed, axis=0, keepdims=True) * scale
            grad = d_normed * scale - level - feats * inverse * along
            if whole_lanes:
                at_row = (first + column) // BLK
                grad_rows[pl.ds(at_row, WHOLE, stride=columns // BLK), :] = grad[:WHOLE]
                grad_ref[0, WHOLE:, 0, inside] = grad[WHOLE:]
            else:
                grad_ref[0, :, 0, inside] = grad
        if ahead is not None:
            score = score + ahead[0]
            d_pix = ahead[1]
    score_ref[...] += score
    gain_sum_ref[...] = gain_sum


def attend_back(part, earlier, scales, feats, weights, gain_column, d_cols, query_cols):
    m, first, tiles = part
    rows = feats.shape[2] // tiles_of(feats)
    in_specs = [
        pl.BlockSpec((1, 1, rows), lambda t: (m, 0, first + t)),
        pl.BlockSpec((1, CEXT, rows), lambda t: (m, 0, first + t)),
        pl.BlockSpec((1, rows, LAT), lambda t: (m, first + t, 0)),
        pl.BlockSpec((CIN, 1), lambda t: (0, 0)),
        pl.BlockSpec((1, CEXT, LAT), lambda t: (m, 0, 0)),
        pl.BlockSpec((CEXT, LAT), lambda t: (0, 0)),
    ]
    operands = [scales, feats, weights, gain_column, d_cols, query_cols]
    aliases = {}
    if earlier is not None:
        in_specs.append(pl.BlockSpec(memory_space=pl.ANY))
        aliases = {len(operands): 0}
        operands.append(earlier)
    return pl.pallas_call(
        attend_back_body,
        grid=(tiles,),
        in_specs=in_specs,
        out_specs=[
            pl.BlockSpec((1, CIN, 1, rows), lambda t: (m, 0, 0, first + t)),
            pl.BlockSpec((CEXT, LAT), lambda t: (0, 0)),
            pl.BlockSpec((CIN, BLK), lambda t: (0, 0)),
        ],
        out_shape=[
            jax.ShapeDtypeStruct((feats.shape[0], CIN, 1, feats.shape[2]), jnp.float32),
            jax.ShapeDtypeStruct((CEXT, LAT), jnp.float32),
            jax.ShapeDtypeStruct((CIN, BLK), jnp.float32),
        ],
        input_output_aliases=aliases,
        cost_estimate=cost(16 * tiles * rows * LAT * CEXT, tiles * rows * 4000),
        name="attend_back",
    )(*operands)


def query_body(block_ref, lat_ref, gain_ref, key_ref, *rest):
    sources, (low_ref, query_ref, cols_ref, *squares, full_ref, sems) = (rest[:-9], rest[-9:])
    side = DL // BLK
    first = 0
    for source in sources:

        @pl.loop(0, source.shape[0])
        def _(at, source=source, first=first):
            block = block_ref[first + at]
            matrix = block // PER_MATRIX
            row = pl.multiple_of(block % PER_MATRIX // side * BLK, BLK)
            column = pl.multiple_of(block % side * BLK, BLK)
            pltpu.make_async_copy(
                source.at[at],
                full_ref.at[matrix, pl.ds(row, BLK), pl.ds(column, BLK)],
                sems.at[matrix],
            ).start()

        first += source.shape[0]

    def keep(matrix):
        return pltpu.make_async_copy(full_ref.at[matrix], squares[matrix], sems.at[4 + matrix])

    lat_low = (standardize(lat_ref[...]) * gain_ref[...]).astype(jnp.bfloat16)
    low_ref[...] = lat_low
    for matrix in range(4):
        pltpu.make_async_copy(full_ref.at[matrix], full_ref.at[matrix], sems.at[matrix]).wait()
        keep(matrix).start()
    query = dot(lat_low, full_ref[0]).astype(jnp.bfloat16)
    query_ref[...] = query
    scores = dot_last(key_ref[...], query) * (1.0 / math.sqrt(DL))
    row = lax.broadcasted_iota(jnp.int32, scores.shape, 0)
    cols_ref[...] = jnp.where(row == MASK_ROW, 1.0, scores).astype(jnp.bfloat16)
    for matrix in range(4):
        keep(matrix).wait()


def make_query(blocks, sources, latent_array, gain, w_key):
    vmem = pl.BlockSpec(memory_space=pltpu.VMEM)
    hbm = pl.BlockSpec(memory_space=pl.ANY)
    rows = jax.ShapeDtypeStruct((LAT, DL), jnp.bfloat16)
    square = jax.ShapeDtypeStruct((DL, DL), jnp.bfloat16)
    return pl.pallas_call(
        query_body,
        in_specs=[pl.BlockSpec(memory_space=pltpu.SMEM), vmem, vmem, vmem] + [hbm] * len(sources),
        out_specs=[vmem] * 3 + [hbm] * 4,
        out_shape=[rows, rows, jax.ShapeDtypeStruct((CEXT, LAT), jnp.bfloat16)] + [square] * 4,
        scratch_shapes=[pltpu.VMEM((4, DL, DL), jnp.bfloat16), pltpu.SemaphoreType.DMA((8,))],
        cost_estimate=cost(3 * LAT * DL * DL, 4 * NBLK * BLK * BLK),
        name="make_query",
    )(blocks, latent_array, gain[None], w_key, *sources)


def image_sums_body(where_ref, *rest):
    n_img = len(rest) - 7
    pieces, (grads_ref, value_ref, resid_ref, rows_ref, full_ref, zero_ref, sems) = (
        rest[:n_img],
        rest[n_img:],
    )
    side = DL // BLK
    count = pieces[0].shape[1]

    def put(source, block):
        place = where_ref[n_img + block]

        @pl.when(place >= 0)
        def _():
            pltpu.make_async_copy(source, grads_ref.at[place], sems.at[1]).start()

    for piece in range(n_img):
        first = pl.multiple_of(where_ref[piece] * count, count)
        pltpu.make_async_copy(
            pieces[piece], rows_ref.at[:, pl.ds(first, count), :], sems.at[0]
        ).start()
    zero_ref[...] = jnp.zeros_like(zero_ref)

    @pl.loop(0, PER_MATRIX)
    def _(block):
        put(zero_ref, block)

    pltpu.make_async_copy(rows_ref, rows_ref, sems.at[0]).wait()
    for matrix in range(3):
        full_ref[matrix] = contract_rows(rows_ref[matrix], rows_ref[3 + matrix]).astype(jnp.bfloat16)

        @pl.loop(0, PER_MATRIX)
        def _(block, matrix=matrix):
            row = pl.multiple_of((block // side) * BLK, BLK)
            column = pl.multiple_of((block % side) * BLK, BLK)
            put(
                full_ref.at[matrix, pl.ds(row, BLK), pl.ds(column, BLK)],
                (matrix + 1) * PER_MATRIX + block,
            )

    value_ref[...] = contract_rows(rows_ref[7, :, :CEXT], rows_ref[6]).astype(jnp.bfloat16)
    each = resid_ref.shape[0]
    total = rows_ref[3, :each, :].astype(jnp.float32)
    for first in range(each, rows_ref.shape[1], each):
        total = total + rows_ref[3, first : first + each, :].astype(jnp.float32)
    resid_ref[...] = total.astype(jnp.bfloat16)
    pltpu.make_async_copy(grads_ref, grads_ref, sems.at[1]).wait()


def image_sums(where, pieces, lat_rows):
    n_img = len(pieces)
    slabs, count, _ = pieces[0].shape
    hbm = pl.BlockSpec(memory_space=pl.ANY)
    vmem = pl.BlockSpec(memory_space=pltpu.VMEM)
    return pl.pallas_call(
        image_sums_body,
        in_specs=[pl.BlockSpec(memory_space=pltpu.SMEM)] + [hbm] * n_img,
        out_specs=[hbm, vmem, vmem],
        out_shape=[
            jax.ShapeDtypeStruct((NBLK // n_img, BLK, BLK), jnp.bfloat16),
            jax.ShapeDtypeStruct((CEXT, DL), jnp.bfloat16),
            jax.ShapeDtypeStruct((lat_rows, DL), jnp.bfloat16),
        ],
        scratch_shapes=[
            pltpu.VMEM((slabs, n_img * count, DL), jnp.bfloat16),
            pltpu.VMEM((3, DL, DL), jnp.bfloat16),
            pltpu.VMEM((BLK, BLK), jnp.bfloat16),
            pltpu.SemaphoreType.DMA((2,)),
        ],
        cost_estimate=cost(8 * n_img * count * DL * DL, 16 * DL * DL),
        name="image_sums",
    )(where, *pieces)


def two_bf16(values_in):
    head = values_in.astype(jnp.bfloat16)
    return (head, (values_in - head.astype(jnp.float32)).astype(jnp.bfloat16))


def product_f32(left_side, right_side):
    left_head, left_rest = two_bf16(left_side)
    right_head, right_rest = two_bf16(right_side)
    both = dot(
        jnp.concatenate([left_head, left_rest], axis=1),
        jnp.concatenate([right_head, right_head], axis=0),
    )
    return both + dot(left_head, right_rest)


def update_body(block_ref, lat_ref, dq_ref, sum_ref, ls_ref, rs_ref, lr_ref, rr_ref, ma_ref, *outs):
    new_left, new_right, new_master, new_copy = outs
    side = DL // BLK
    for slot in range(ma_ref.shape[0]):
        block = block_ref[slot]
        is_query = block < PER_MATRIX
        inside = jnp.where(is_query, block, 0)
        row = pl.multiple_of(inside // side * BLK, BLK)
        column = pl.multiple_of(inside % side * BLK, BLK)
        own = contract_rows(lat_ref[:, pl.ds(row, BLK)], dq_ref[:, pl.ds(column, BLK)])
        grad = jnp.where(is_query, own, sum_ref[slot])
        turned = grad.T
        new_left[slot] = 0.5 * ls_ref[slot] + 0.5 * product_f32(grad, turned)
        new_right[slot] = 0.5 * rs_ref[slot] + 0.5 * product_f32(turned, grad)
        shampoo = product_f32(product_f32(lr_ref[slot], grad), rr_ref[slot])
        mean_square = jnp.mean(shampoo * shampoo)
        updated = ma_ref[slot] - 0.5 / math.sqrt(DL) * (shampoo / jnp.sqrt(mean_square + 1e-06))
        new_master[slot] = updated
        new_copy[slot] = updated.astype(jnp.bfloat16)


def update_slots(blocks, lat_low, d_query, sums, left_stat, right_stat, left_root, right_root, master):
    vmem = pl.BlockSpec(memory_space=pltpu.VMEM)
    shape = jax.ShapeDtypeStruct(master.shape, jnp.float32)
    return pl.pallas_call(
        update_body,
        in_specs=[pl.BlockSpec(memory_space=pltpu.SMEM)] + [vmem] * 8,
        out_specs=[vmem] * 4,
        out_shape=[shape, shape, shape, jax.ShapeDtypeStruct(master.shape, jnp.bfloat16)],
        name="update_slots",
    )(blocks, lat_low, d_query, sums, left_stat, right_stat, left_root, right_root, master)


def root_mean(total, count):
    return jnp.sqrt(total / count + 1e-06)


def finish_body(even_ref, late_ref, key_ref, query_ref, wq_ref, *rest):
    own_ref, other_ref, kv_ref, lat_ref, gains_ref, *outs = rest
    dq_ref, kv_grad_ref, new_kv_ref, lat_grad_ref, new_lat_ref, gain_ref, new_gain_ref = outs
    inv_root = 1.0 / math.sqrt(DL)
    late = late_ref[...]
    even = even_ref[0] == 0

    def early(first, stop):
        own = own_ref[first:stop].astype(jnp.float32)
        other = other_ref[first:stop].astype(jnp.float32)
        return jnp.concatenate(
            [jnp.where(even, own, other), jnp.where(even, other, own)], axis=1
        )

    d_query = (contract_rows(late, key_ref[...]) * inv_root).astype(jnp.bfloat16)
    dq_ref[...] = d_query
    key_total = (dot(late, query_ref[...]) * inv_root)[:CIN]
    value_total = early(0, CEXT)[:CIN]
    for at, grad in enumerate((key_total, value_total)):
        kv_grad_ref[:, at, :] = grad
        step = 0.3 / math.sqrt(CIN) / root_mean(jnp.sum(grad * grad), CIN * DL)
        new_kv_ref[:, at, :] = kv_ref[:, at, :] - step * grad
    d_lat_norm = dot_last(d_query, wq_ref[...])
    lat = lat_ref[...]
    centred = lat - jnp.mean(lat, axis=-1, keepdims=True)
    scale = lax.rsqrt(jnp.mean(centred * centred, axis=-1, keepdims=True) + 1e-05)
    normed = centred * scale
    dy = d_lat_norm * gains_ref[0:1]
    along = jnp.mean(dy * normed, axis=-1, keepdims=True)
    back = (dy - jnp.mean(dy, axis=-1, keepdims=True) - normed * along) * scale
    lat_grad = early(CEXT, CEXT + LAT) + back
    lat_grad_ref[...] = lat_grad
    new_lat_ref[...] = lat - 0.3 / root_mean(jnp.sum(lat_grad * lat_grad), LAT * DL) * lat_grad
    tail = late[CIN + 1 : CEXT].astype(jnp.float32)
    second = jnp.concatenate([tail[0:1], tail[1:2]], axis=1)
    for at, grad in enumerate((jnp.sum(d_lat_norm * normed, axis=0, keepdims=True), second)):
        gain_ref[at : at + 1] = grad
        step = 0.2 / root_mean(jnp.sum(grad * grad), DL)
        new_gain_ref[at : at + 1] = gains_ref[at : at + 1] - step * grad


def finish(even, late, w_key, query, w_query, early, other, kv_weight, latent_array, lat_gains):
    vmem = pl.BlockSpec(memory_space=pltpu.VMEM)
    kv = jnp.swapaxes(kv_weight, 0, 1)
    kv_shape = jax.ShapeDtypeStruct(kv.shape, jnp.float32)
    lat_shape = jax.ShapeDtypeStruct((LAT, DL), jnp.float32)
    gain_shape = jax.ShapeDtypeStruct(lat_gains.shape, jnp.float32)
    outs = pl.pallas_call(
        finish_body,
        in_specs=[pl.BlockSpec(memory_space=pltpu.SMEM)] + [vmem] * 9,
        out_specs=[vmem] * 7,
        out_shape=[jax.ShapeDtypeStruct((LAT, DL), jnp.bfloat16)]
        + [kv_shape] * 2
        + [lat_shape] * 2
        + [gain_shape] * 2,
        name="finish",
    )(even, late, w_key, query, w_query, early, other, kv, latent_array, lat_gains)
    d_query, kv_grad, new_kv, *others = outs
    return (d_query, jnp.swapaxes(kv_grad, 0, 1), jnp.swapaxes(new_kv, 0, 1), *others)


def swap(array, axis):
    return lax.all_to_all(array, axis, 0, 0, tiled=True)


def everyone(array, axis):
    return swap(jnp.broadcast_to(array[None], (lax.axis_size(axis), *array.shape)), axis)


def near_hop(array, axis):
    size = lax.axis_size(axis)
    return lax.ppermute(array, axis, [(i, i ^ 1) for i in range(size)])


def far_hop(array, axis, step):
    size = lax.axis_size(axis)
    return lax.ppermute(array, axis, [(i, (i + 2 * step) % size) for i in range(size)])


def spread(array, rows, axis, hops):
    size = lax.axis_size(axis)
    column = {("img", "far"): 0, ("img", "near"): 1, ("pix", "far"): 2, ("pix", "near"): 3}
    got = [array]
    places = [rows]
    for step in range(1, 2 if hops == "near" else size // 2):
        got.append(near_hop(array, axis) if hops == "near" else far_hop(array, axis, step))
        moved = rows.copy()
        moved[:, column[axis, hops]] += step
        places.append(moved)
    return (jnp.concatenate(got), np.concatenate(places))


ROUTES = (
    (("pix", "near"), ("img", "far"), ("pix", "far")),
    (("img", "far"), ("pix", "far"), ("pix", "near")),
    (("pix", "far"), ("pix", "near"), ("img", "far")),
)


def gather_blocks(low, feats):
    slots_dev = low.shape[0]
    n_pix = lax.axis_size("pix")
    if slots_dev < 4 or n_pix > 8:
        low = lax.all_gather(low, ("img", "pix"), axis=0, tiled=True)
        return ([low], jnp.arange(NBLK), feats)
    quarter = slots_dev // 4
    states = []
    bounds = (0, quarter, 2 * quarter, slots_dev)
    for part in range(3):
        start, stop = bounds[part], bounds[part + 1]
        rows = np.zeros((stop - start, 5), np.int32)
        rows[:, 4] = np.arange(start, stop)
        states.append((low[start:stop], rows))
    for phase in range(3):
        states = [spread(*state, *ROUTES[part][phase]) for part, state in enumerate(states)]
    held, feats = lax.optimization_barrier(([array for array, _ in states], feats))
    arrays = []
    places = []
    for array, (_, rows) in zip(held, states):
        arrays += [array, near_hop(array, "img")]
        mate = rows.copy()
        mate[:, 1] += 1
        places += [rows, mate]
    img_far, img_near, pix_far, pix_near, slot = np.concatenate(places).T
    img = lax.axis_index("img")
    pix = lax.axis_index("pix")
    n_far = lax.axis_size("img") // 2
    img_of = (img // 2 - img_far) % n_far * 2 + (img + img_near) % 2
    pix_of = (pix // 2 - pix_far) % (n_pix // 2) * 2 + (pix + pix_near) % 2
    return (arrays, (img_of * n_pix + pix_of) * slots_dev + slot, feats)


def split_near(array, axis):
    size = lax.axis_size(axis)
    near = lax.axis_index(axis) % 2
    pairs = array.reshape(size // 2, 2, *array.shape[1:])
    return (
        lax.dynamic_index_in_dim(pairs, near, 1, False),
        lax.dynamic_index_in_dim(pairs, 1 - near, 1, False),
    )


def join_near(kept, sent, axis):
    got = near_hop(sent, axis)
    return (kept.astype(jnp.float32) + got.astype(jnp.float32)).astype(jnp.bfloat16)


def sum_far(kept, axis):
    size = lax.axis_size(axis)
    far = lax.axis_index(axis) // 2
    total = lax.dynamic_index_in_dim(kept, far, 0, False).astype(jnp.float32)
    for step in range(1, size // 2):
        part = lax.dynamic_index_in_dim(kept, (far + step) % (size // 2), 0, False)
        total = total + far_hop(part, axis, step).astype(jnp.float32)
    return total


def gather_far(array, axis):
    size = lax.axis_size(axis)
    far = lax.axis_index(axis) // 2
    got = [array] + [far_hop(array, axis, step) for step in range(1, size // 2)]
    return lax.dynamic_slice_in_dim(jnp.stack(got[::-1] * 2), size // 2 - 1 - far, size // 2, 0)


def gather_near(array, axis):
    near = lax.axis_index(axis) % 2
    other = near_hop(array, axis)
    both = jnp.where(
        near == 0, jnp.stack([array, other], axis=1), jnp.stack([other, array], axis=1)
    )
    return both.reshape(lax.axis_size(axis), *array.shape[1:])


def latent_pass(numerator, denominator, lat_part, cot_rows, lat_gain, w_out, w_up, w_down):
    attended = numerator / denominator[..., None]
    att_low = attended.astype(jnp.bfloat16)
    resid = lat_part[None] + product("mrd,de->mre", att_low, w_out)
    normed, normed_back = jax.vjp(standardize, resid)
    hn_low = (normed * lat_gain).astype(jnp.bfloat16)
    hidden = product("mrd,de->mre", hn_low, w_up)
    active, active_back = jax.vjp(gelu_exact, hidden)
    act_low = active.astype(jnp.bfloat16)
    latents_out = resid + product("mrd,de->mre", act_low, w_down)
    g_mlp = cot_rows.astype(jnp.bfloat16)
    d_active = product("mre,de->mrd", g_mlp, w_down)
    d_hidden = active_back(d_active)[0].astype(jnp.bfloat16)
    d_normed = product("mre,de->mrd", d_hidden, w_up)
    d_resid = cot_rows + normed_back(d_normed * lat_gain)[0]
    d_branch = d_resid.astype(jnp.bfloat16)
    d_attended = product("mre,de->mrd", d_branch, w_out)
    d_numer = d_attended / denominator[..., None]
    d_denom = -jnp.sum(d_attended * numerator / (denominator * denominator)[..., None], axis=-1)
    gain_mlp = jnp.sum(d_normed * normed, axis=(0, 1))
    row_arrays = (att_low, hn_low, act_low, d_branch, d_hidden, g_mlp)
    return (latents_out, d_numer.astype(jnp.bfloat16), d_denom, (row_arrays, gain_mlp))


def shards(
    pixels,
    sides,
    owner,
    master,
    left_stat,
    right_stat,
    left_root,
    right_root,
    kv_weight,
    latent_array,
    in_gain,
    lat_gains,
    cotangent,
):
    micro = pixels.shape[0]
    rows_dev = pixels.shape[2]
    n_pix = lax.axis_size("pix")
    n_img = lax.axis_size("img")
    img = lax.axis_index("img")
    pix = lax.axis_index("pix")
    slots_dev = master.shape[0]
    lat_rows = LAT // n_pix
    row_start = pix * lat_rows
    inv_root = 1.0 / math.sqrt(DL)

    place = jnp.concatenate([(pix * rows_dev)[None], sides * sides]).astype(jnp.int32)
    across = lies_across(pixels)
    gain_column = in_gain[:, None]
    feats = None
    for micro_index in range(micro - 1):
        feats = prepare_pixels(micro_index, feats, place, across, gain_column)
    sources, source_slots, feats = gather_blocks(master.astype(jnp.bfloat16), feats)
    feats, scales = prepare_pixels(micro - 1, feats, place, across, gain_column)
    all_blocks = jnp.arange(NBLK, dtype=jnp.int32)
    source_blocks = jnp.sum(
        jnp.where(source_slots[:, None] == owner[None], all_blocks[None], 0), axis=1
    )
    kv_low = kv_weight.astype(jnp.bfloat16)
    w_key = jnp.pad(kv_low[0], ((0, CEXT - CIN), (0, 0)))
    w_value = kv_low[1]
    lat_low, query, query_cols, w_query, w_out, w_up, w_down = make_query(
        source_blocks.astype(jnp.int32), sources, latent_array, lat_gains[0], w_key
    )

    weights, sums = attend(feats, query_cols)
    sums = sums.reshape(micro, CEXT, n_pix, lat_rows).transpose(2, 1, 0, 3)
    sums = swap(sums.reshape(n_pix, CEXT, micro * lat_rows), "pix")
    sums = jnp.sum(sums.astype(jnp.float32), axis=0)
    numer_in = sums[:CIN]
    denominator = (sums[ONES_ROW] + sums[ONES_ROW + 1]).reshape(micro, lat_rows)
    numerator = fine("cr,cd->rd", numer_in, w_value).reshape(micro, lat_rows, DL)
    latents_out, d_numer, d_denom, latent_grads = latent_pass(
        numerator,
        denominator,
        lax.dynamic_slice_in_dim(latent_array, row_start, lat_rows, 0),
        cotangent[:, 0],
        lat_gains[1],
        w_out,
        w_up,
        w_down,
    )
    row_arrays, gain_mlp = latent_grads
    d_numer = d_numer.reshape(micro * lat_rows, DL)
    head, rest = two_terms(d_denom.reshape(1, micro * lat_rows))
    d_cols = product("rd,cd->cr", d_numer, w_value).astype(jnp.bfloat16)
    d_cols = jnp.concatenate([d_cols, head, rest, jnp.zeros_like(head)], axis=0)
    d_cols = everyone(d_cols, "pix").reshape(n_pix, CEXT, micro, lat_rows)
    d_cols = d_cols.transpose(2, 1, 0, 3).reshape(micro, CEXT, LAT)

    numer_rows = jnp.pad(numer_in.astype(jnp.bfloat16).T, ((0, 0), (0, DL - CIN)))
    own = jnp.stack(
        [array.reshape(micro * lat_rows, DL) for array in row_arrays] + [d_numer, numer_rows]
    )
    mate = [(i, i ^ 1) for i in range(n_img)]
    pieces = [own, lax.ppermute(own, "img", mate)]
    images = [img, img ^ 1]
    far = []
    for step in range(1, n_img // 2):
        hop = [(i, (i + 2 * step) % n_img) for i in range(n_img)]
        far.append(lax.ppermute(own, "img", hop))
        images += [(img - 2 * step) % n_img, (img - 2 * step) % n_img ^ 1]
    device_of = owner // slots_dev
    place_of = device_of % n_pix * slots_dev + owner % slots_dev
    where = jnp.where(device_of // n_pix == img, place_of, -1)

    results = (None,)
    score_sum = jnp.zeros((CEXT, LAT), jnp.float32)
    gain_sum = jnp.zeros((CIN, BLK), jnp.float32)
    width = DL // 2
    each = -(-CEXT // n_pix)
    parts = parts_of(feats)
    for at, part in enumerate(parts):
        if at == len(parts) - 2:
            far, gain_sum = lax.optimization_barrier((far, gain_sum))
            for piece in far:
                pieces += [piece, lax.ppermute(piece, "img", mate)]
        if at == len(parts) - 1:
            pieces, gain_sum = lax.optimization_barrier((pieces, gain_sum))
            where = jnp.concatenate([jnp.stack(images), where]).astype(jnp.int32)
            grads, value_part, resid_part = image_sums(where, pieces, lat_rows)
            value_part = jnp.pad(value_part, ((0, each * n_pix - CEXT), (0, 0)))
            value_part = lax.dynamic_slice_in_dim(value_part, img % 2 * width, width, 1)
            value_sides = split_near(value_part.reshape(n_pix, each, width), "pix")
            grad_sides = split_near(grads.reshape(n_pix, slots_dev, BLK, BLK), "pix")
            value_part = join_near(*value_sides, "pix")
            gain_column, value_part, grad_sides = lax.optimization_barrier(
                (gain_column, value_part, grad_sides)
            )
        results = attend_back(
            part, results[0], scales, feats, weights, gain_column, d_cols, query_cols
        )
        score_sum = score_sum + results[1]
        gain_sum = gain_sum + results[2]
    pixel_grad = jnp.swapaxes(results[0].reshape(micro, 1, CIN, rows_dev), 2, 3)

    gain_sum = jnp.sum(gain_sum, axis=1)[None] / in_gain[None]
    late = jnp.concatenate(
        [
            score_sum[:CIN],
            jnp.pad(gain_sum, ((0, 0), (0, LAT - CIN))),
            gain_mlp.reshape(DL // LAT, LAT),
        ],
        axis=0,
    ).astype(jnp.bfloat16)
    late = jnp.pad(late, ((0, each * n_pix - CEXT), (0, 0))).reshape(n_pix, each, LAT)
    late = jnp.sum(swap(late, "pix").astype(jnp.float32), axis=0)
    value_part = sum_far(value_part, "pix").astype(jnp.bfloat16)
    grads = join_near(*grad_sides, "pix")
    late, value_part, grads = lax.optimization_barrier((late, value_part, grads))
    late = jnp.sum(everyone(late, "img"), axis=0).astype(jnp.bfloat16)
    resid_part = lax.dynamic_slice_in_dim(resid_part, img % 2 * width, width, 1)
    early = gather_far(jnp.concatenate([value_part, resid_part], axis=0), "pix")
    late, early = lax.optimization_barrier((late, early))
    grads = sum_far(grads, "pix")
    late = everyone(late, "pix").reshape(n_pix * each, LAT)[:CEXT]
    early = gather_near(early, "pix")
    value_part = early[:, :each].reshape(n_pix * each, width)[:CEXT]
    early = jnp.concatenate([value_part, early[:, each:].reshape(LAT, width)], axis=0)
    other = near_hop(early, "img")
    d_query, kv_grad, new_kv, latent_grad, new_latent, lat_gain_grad, new_lat_gains = finish(
        (img % 2)[None], late, w_key, query, w_query, early, other, kv_weight, latent_array, lat_gains
    )
    in_gain_grad = late[CIN, :CIN].astype(jnp.float32)

    mine = (img * n_pix + pix) * slots_dev + jnp.arange(slots_dev, dtype=jnp.int32)
    blocks = jnp.sum(
        jnp.where(owner[None] == mine[:, None], all_blocks[None], 0), axis=1
    )
    new_left, new_right, new_master, new_copy = update_slots(
        blocks.astype(jnp.int32),
        lat_low,
        d_query,
        grads,
        left_stat,
        right_stat,
        left_root,
        right_root,
        master,
    )
    new_in_gain = in_gain - 0.2 * normalized(in_gain_grad, (0,))
    return (
        latents_out[:, None],
        pixel_grad,
        new_left,
        new_right,
        new_master,
        new_copy,
        kv_grad,
        new_kv,
        latent_grad,
        new_latent,
        in_gain_grad,
        new_in_gain,
        lat_gain_grad,
        new_lat_gains,
    )


def solution(mesh):
    pixel_spec = P(None, "img", "pix", None)
    slot_spec = P(("img", "pix"), None, None)
    in_specs = (
        (pixel_spec, P(), P()) + (slot_spec,) * 5 + (P(),) * 4 + (pixel_spec,)
    )
    out_specs = (pixel_spec, pixel_spec) + (slot_spec,) * 4 + (P(),) * 8
    return jax.shard_map(shards, mesh=mesh, in_specs=in_specs, out_specs=out_specs, check_vma=False)
```

```python
import functools
import math

import jax
import jax.numpy as jnp
from jax import lax
import numpy as np
from jax.experimental import pallas as pl
from jax.experimental.pallas import tpu as pltpu
from jax.sharding import PartitionSpec as P

CIN = 261
DL = 1024
LAT = 512
BLK = 128
NBLK = 256
PER_MATRIX = NBLK // 4
CEXT = 264
WHOLE = CIN // 8 * 8
ONES_ROW = 261
MASK_ROW = 263
MASKED = -1e30

HIGHEST_PRECISION = lax.Precision.HIGHEST


def standardize(values_in):
    average = jnp.mean(values_in, axis=-1, keepdims=True)
    centred = values_in - average
    variance = jnp.mean(centred * centred, axis=-1, keepdims=True)
    return centred * lax.rsqrt(variance + 1e-05)


def gelu_exact(values_in):
    return jax.nn.gelu(values_in, approximate=False)


def normalized(gradient, reduce_axes):
    return gradient / jnp.sqrt(
        jnp.mean(gradient * gradient, axis=reduce_axes, keepdims=True) + 1e-06
    )


def product(pattern, left_side, right_side):
    return jnp.einsum(pattern, left_side, right_side, preferred_element_type=jnp.float32)


def fine(pattern, left_side, right_side):
    return jnp.einsum(
        pattern,
        left_side.astype(jnp.float32),
        right_side.astype(jnp.float32),
        precision=HIGHEST_PRECISION,
    )


def two_terms(values_in):
    head = lax.reduce_precision(values_in, 8, 7)
    return (head.astype(jnp.bfloat16), (values_in - head).astype(jnp.bfloat16))


def contract_rows(left_side, right_side, precision=None):
    return lax.dot_general(
        left_side,
        right_side,
        (((0,), (0,)), ((), ())),
        precision=precision,
        preferred_element_type=jnp.float32,
    )


def dot(left_side, right_side):
    return jnp.dot(left_side, right_side, preferred_element_type=jnp.float32)


def dot_last(left_side, right_side):
    return lax.dot_general(
        left_side, right_side, (((1,), (1,)), ((), ())), preferred_element_type=jnp.float32
    )


def tile_of(rows, most):
    return max((size for size in range(128, most + 1, 128) if rows % size == 0), default=rows)


def lies_across(pixels):
    micro, _, rows_dev, _ = pixels.shape
    return jnp.swapaxes(pixels, 2, 3).reshape(micro, CIN, 1, rows_dev)


def centre(pix):
    centred = pix - jnp.mean(pix, axis=0, keepdims=True)
    scale = lax.rsqrt(jnp.mean(centred * centred, axis=0, keepdims=True) + 1e-05)
    return (centred * scale, scale)


def cost(flops, count):
    return pl.CostEstimate(flops=int(flops), bytes_accessed=int(count), transcendentals=0)


def prepare_body(place_ref, pix_ref, gain_ref, *rest, micro_index):
    out_ref, scale_ref = rest[-2:]
    columns = pix_ref.shape[3]
    gain = gain_ref[...]
    width = BLK if columns % BLK == 0 else columns
    if width == BLK:
        pix_rows = pix_ref.reshape(CIN * columns // BLK, BLK)
    extra = (CEXT - CIN, width)
    row = lax.broadcasted_iota(jnp.int32, extra, 0) + CIN
    slot = place_ref[0] + pl.program_id(0) * columns + lax.broadcasted_iota(jnp.int32, extra, 1)
    for column in range(0, columns, width):
        inside = slice(column, column + width)
        if width == BLK:
            pix = jnp.concatenate(
                [
                    pix_rows[pl.ds(column // BLK, WHOLE, stride=columns // BLK), :],
                    pix_ref[0, WHOLE:, 0, inside],
                ],
                axis=0,
            )
        else:
            pix = pix_ref[0, :, 0, :]
        normed, scale_ref[0, :, inside] = centre(pix)
        mask = jnp.where(slot + column < place_ref[1 + micro_index], 0.0, MASKED)
        tail = jnp.where(row == MASK_ROW, mask, 1.0)
        full = jnp.concatenate([normed * gain, tail], axis=0)
        out_ref[0, :, inside] = full.astype(jnp.bfloat16)


def prepare_pixels(micro_index, earlier, place, across, gain_column):
    micro, _, _, rows_dev = across.shape
    rows = tile_of(rows_dev, 1152)
    m = micro_index
    in_specs = [
        pl.BlockSpec(memory_space=pltpu.SMEM),
        pl.BlockSpec((1, CIN, 1, rows), lambda t: (m, 0, 0, t)),
        pl.BlockSpec((CIN, 1), lambda t: (0, 0)),
    ]
    operands = [place, across, gain_column]
    aliases = {}
    if earlier is not None:
        in_specs += [pl.BlockSpec(memory_space=pl.ANY)] * 2
        aliases = {len(operands): 0, len(operands) + 1: 1}
        operands += earlier
    return pl.pallas_call(
        functools.partial(prepare_body, micro_index=m),
        grid=(rows_dev // rows,),
        in_specs=in_specs,
        out_specs=[
            pl.BlockSpec((1, CEXT, rows), lambda t: (m, 0, t)),
            pl.BlockSpec((1, 1, rows), lambda t: (m, 0, t)),
        ],
        out_shape=[
            jax.ShapeDtypeStruct((micro, CEXT, rows_dev), jnp.bfloat16),
            jax.ShapeDtypeStruct((micro, 1, rows_dev), jnp.float32),
        ],
        input_output_aliases=aliases,
        cost_estimate=cost(0, 12 * rows_dev * CEXT),
        name="prepare_pixels",
    )(*operands)


def spans_of(columns):
    if columns == 1152:
        return ((0, 512), (512, 384), (896, 256))
    return ((0, columns),)


def short_spans_of(columns):
    if columns == 1152:
        return tuple((first, min(256, columns - first)) for first in range(0, columns, 256))
    return ((0, columns),)


def attend_body(feat_ref, query_ref, exp_ref, out_ref, sum_ref):
    tile = pl.program_id(1)
    spans = spans_of(feat_ref.shape[2])
    query = query_ref[...]

    def scores_of(at):
        first, size = spans[at]
        return contract_rows(feat_ref[0, :, first : first + size], query)

    @pl.when(tile == 0)
    def _():
        sum_ref[...] = jnp.zeros_like(sum_ref)

    scores = scores_of(0)
    total = sum_ref[...]
    for at, (first, size) in enumerate(spans):
        ahead = scores_of(at + 1) if at + 1 < len(spans) else None
        weights = jnp.exp(scores).astype(jnp.bfloat16)
        exp_ref[0, first : first + size] = weights
        total = total + dot(feat_ref[0, :, first : first + size], weights)
        scores = ahead
    sum_ref[...] = total

    @pl.when(tile == pl.num_programs(1) - 1)
    def _():
        sums = sum_ref[...]
        low = sums.astype(jnp.bfloat16)
        rest = (sums - low.astype(jnp.float32))[ONES_ROW : ONES_ROW + 1]
        row = lax.broadcasted_iota(jnp.int32, sums.shape, 0)
        out_ref[0] = jnp.where(row == ONES_ROW + 1, rest, sums).astype(jnp.bfloat16)


def attend(feats, query_cols):
    micro, _, rows_dev = feats.shape
    rows = tile_of(rows_dev, 1152)
    return pl.pallas_call(
        attend_body,
        grid=(micro, rows_dev // rows),
        in_specs=[
            pl.BlockSpec((1, CEXT, rows), lambda m, t: (m, 0, t)),
            pl.BlockSpec((CEXT, LAT), lambda m, t: (0, 0)),
        ],
        out_specs=[
            pl.BlockSpec((1, rows, LAT), lambda m, t: (m, t, 0)),
            pl.BlockSpec((1, CEXT, LAT), lambda m, t: (m, 0, 0)),
        ],
        out_shape=[
            jax.ShapeDtypeStruct((micro, rows_dev, LAT), jnp.bfloat16),
            jax.ShapeDtypeStruct((micro, CEXT, LAT), jnp.bfloat16),
        ],
        scratch_shapes=[pltpu.VMEM((CEXT, LAT), jnp.float32)],
        cost_estimate=cost(8 * micro * rows_dev * LAT * CEXT, 4 * micro * rows_dev * LAT),
        name="attend",
    )(feats, query_cols)


def tiles_of(feats):
    rows_dev = feats.shape[2]
    return rows_dev // tile_of(rows_dev, 1152)


def parts_of(feats):
    micro = feats.shape[0]
    tiles = tiles_of(feats)
    parts = []
    for m in range(micro):
        sizes = [tiles]
        if m == micro - 1 and tiles >= 4:
            sizes = [tiles // 4, tiles // 2, tiles - tiles // 4 - tiles // 2]
        parts += [(m, sum(sizes[:at]), size) for at, size in enumerate(sizes)]
    return parts


def attend_back_body(scale_ref, feat_ref, exp_ref, gain_ref, dc_ref, qc_ref, *rest):
    grad_ref, score_ref, gain_sum_ref = rest[-3:]
    spans = short_spans_of(feat_ref.shape[2])
    d_cols = dc_ref[0]
    both_cols = jnp.concatenate([qc_ref[...], d_cols], axis=1)

    @pl.when(pl.program_id(0) == 0)
    def _():
        score_ref[...] = jnp.zeros_like(score_ref)
        gain_sum_ref[...] = jnp.zeros_like(gain_sum_ref)

    def products(at):
        first, size = spans[at]
        feats = feat_ref[0, :, first : first + size]
        weights = exp_ref[0, first : first + size]
        d_exp = contract_rows(feats, d_cols)
        d_scores = (weights.astype(jnp.float32) * d_exp).astype(jnp.bfloat16)
        d_pix = dot_last(both_cols, jnp.concatenate([d_scores, weights], axis=1))
        return (dot(feats, d_scores), d_pix)

    columns = feat_ref.shape[2]
    whole_lanes = columns % BLK == 0
    if whole_lanes:
        grad_rows = grad_ref.reshape(CIN * columns // BLK, BLK)
    gain = gain_ref[...]
    inverse = 1.0 / gain
    score, d_pix = products(0)
    gain_sum = gain_sum_ref[...]
    for at, (first, size) in enumerate(spans):
        ahead = products(at + 1) if at + 1 < len(spans) else None
        for column in range(0, size, BLK):
            width = min(BLK, size - column)
            inside = slice(first + column, first + column + width)
            feats = feat_ref[0, :, inside].astype(jnp.float32)[:CIN]
            part = d_pix[:CIN, column : column + width]
            scale = scale_ref[0, :, inside]
            along = feats * part
            if width == BLK:
                gain_sum = gain_sum + along
            else:
                gain_sum = gain_sum + jnp.sum(along, axis=1, keepdims=True) * (1.0 / BLK)
            along = jnp.mean(along, axis=0, keepdims=True) * scale
            d_normed = part * gain
            level = jnp.mean(d_normed, axis=0, keepdims=True) * scale
            grad = d_normed * scale - level - feats * inverse * along
            if whole_lanes:
                at_row = (first + column) // BLK
                grad_rows[pl.ds(at_row, WHOLE, stride=columns // BLK), :] = grad[:WHOLE]
                grad_ref[0, WHOLE:, 0, inside] = grad[WHOLE:]
            else:
                grad_ref[0, :, 0, inside] = grad
        if ahead is not None:
            score = score + ahead[0]
            d_pix = ahead[1]
    score_ref[...] += score
    gain_sum_ref[...] = gain_sum


def attend_back(part, earlier, scales, feats, weights, gain_column, d_cols, query_cols):
    m, first, tiles = part
    rows = feats.shape[2] // tiles_of(feats)
    in_specs = [
        pl.BlockSpec((1, 1, rows), lambda t: (m, 0, first + t)),
        pl.BlockSpec((1, CEXT, rows), lambda t: (m, 0, first + t)),
        pl.BlockSpec((1, rows, LAT), lambda t: (m, first + t, 0)),
        pl.BlockSpec((CIN, 1), lambda t: (0, 0)),
        pl.BlockSpec((1, CEXT, LAT), lambda t: (m, 0, 0)),
        pl.BlockSpec((CEXT, LAT), lambda t: (0, 0)),
    ]
    operands = [scales, feats, weights, gain_column, d_cols, query_cols]
    aliases = {}
    if earlier is not None:
        in_specs.append(pl.BlockSpec(memory_space=pl.ANY))
        aliases = {len(operands): 0}
        operands.append(earlier)
    return pl.pallas_call(
        attend_back_body,
        grid=(tiles,),
        in_specs=in_specs,
        out_specs=[
            pl.BlockSpec((1, CIN, 1, rows), lambda t: (m, 0, 0, first + t)),
            pl.BlockSpec((CEXT, LAT), lambda t: (0, 0)),
            pl.BlockSpec((CIN, BLK), lambda t: (0, 0)),
        ],
        out_shape=[
            jax.ShapeDtypeStruct((feats.shape[0], CIN, 1, feats.shape[2]), jnp.float32),
            jax.ShapeDtypeStruct((CEXT, LAT), jnp.float32),
            jax.ShapeDtypeStruct((CIN, BLK), jnp.float32),
        ],
        input_output_aliases=aliases,
        cost_estimate=cost(16 * tiles * rows * LAT * CEXT, tiles * rows * 4000),
        name="attend_back",
    )(*operands)


def query_body(block_ref, lat_ref, gain_ref, key_ref, *rest):
    sources, (low_ref, query_ref, cols_ref, *squares, full_ref, sems) = (rest[:-9], rest[-9:])
    side = DL // BLK
    first = 0
    for source in sources:

        @pl.loop(0, source.shape[0])
        def _(at, source=source, first=first):
            block = block_ref[first + at]
            matrix = block // PER_MATRIX
            row = pl.multiple_of(block % PER_MATRIX // side * BLK, BLK)
            column = pl.multiple_of(block % side * BLK, BLK)
            pltpu.make_async_copy(
                source.at[at],
                full_ref.at[matrix, pl.ds(row, BLK), pl.ds(column, BLK)],
                sems.at[matrix],
            ).start()

        first += source.shape[0]

    def keep(matrix):
        return pltpu.make_async_copy(full_ref.at[matrix], squares[matrix], sems.at[4 + matrix])

    lat_low = (standardize(lat_ref[...]) * gain_ref[...]).astype(jnp.bfloat16)
    low_ref[...] = lat_low
    for matrix in range(4):
        pltpu.make_async_copy(full_ref.at[matrix], full_ref.at[matrix], sems.at[matrix]).wait()
        keep(matrix).start()
    query = dot(lat_low, full_ref[0]).astype(jnp.bfloat16)
    query_ref[...] = query
    scores = dot_last(key_ref[...], query) * (1.0 / math.sqrt(DL))
    row = lax.broadcasted_iota(jnp.int32, scores.shape, 0)
    cols_ref[...] = jnp.where(row == MASK_ROW, 1.0, scores).astype(jnp.bfloat16)
    for matrix in range(4):
        keep(matrix).wait()


def make_query(blocks, sources, latent_array, gain, w_key):
    vmem = pl.BlockSpec(memory_space=pltpu.VMEM)
    hbm = pl.BlockSpec(memory_space=pl.ANY)
    rows = jax.ShapeDtypeStruct((LAT, DL), jnp.bfloat16)
    square = jax.ShapeDtypeStruct((DL, DL), jnp.bfloat16)
    return pl.pallas_call(
        query_body,
        in_specs=[pl.BlockSpec(memory_space=pltpu.SMEM), vmem, vmem, vmem] + [hbm] * len(sources),
        out_specs=[vmem] * 3 + [hbm] * 4,
        out_shape=[rows, rows, jax.ShapeDtypeStruct((CEXT, LAT), jnp.bfloat16)] + [square] * 4,
        scratch_shapes=[pltpu.VMEM((4, DL, DL), jnp.bfloat16), pltpu.SemaphoreType.DMA((8,))],
        cost_estimate=cost(3 * LAT * DL * DL, 4 * NBLK * BLK * BLK),
        name="make_query",
    )(blocks, latent_array, gain[None], w_key, *sources)


def image_sums_body(where_ref, *rest):
    n_img = len(rest) - 7
    pieces, (grads_ref, value_ref, resid_ref, rows_ref, full_ref, zero_ref, sems) = (
        rest[:n_img],
        rest[n_img:],
    )
    side = DL // BLK
    count = pieces[0].shape[1]

    def put(source, block):
        place = where_ref[n_img + block]

        @pl.when(place >= 0)
        def _():
            pltpu.make_async_copy(source, grads_ref.at[place], sems.at[8]).start()

    def settle(slab):
        pltpu.make_async_copy(rows_ref.at[slab], rows_ref.at[slab], sems.at[slab]).wait()

    order = (0, 3, 1, 4, 2, 5, 6, 7)
    for piece in range(n_img):
        first = pl.multiple_of(where_ref[piece] * count, count)
        for slab in order:
            pltpu.make_async_copy(
                pieces[piece].at[slab], rows_ref.at[slab, pl.ds(first, count), :], sems.at[slab]
            ).start()
    zero_ref[...] = jnp.zeros_like(zero_ref)

    @pl.loop(0, PER_MATRIX)
    def _(block):
        put(zero_ref, block)

    for matrix in range(3):
        settle(matrix)
        settle(3 + matrix)
        full_ref[matrix] = contract_rows(rows_ref[matrix], rows_ref[3 + matrix]).astype(jnp.bfloat16)

        @pl.loop(0, PER_MATRIX)
        def _(block, matrix=matrix):
            row = pl.multiple_of((block // side) * BLK, BLK)
            column = pl.multiple_of((block % side) * BLK, BLK)
            put(
                full_ref.at[matrix, pl.ds(row, BLK), pl.ds(column, BLK)],
                (matrix + 1) * PER_MATRIX + block,
            )

    settle(6)
    settle(7)
    value_ref[...] = contract_rows(rows_ref[7, :, :CEXT], rows_ref[6]).astype(jnp.bfloat16)
    each = resid_ref.shape[0]
    total = rows_ref[3, :each, :].astype(jnp.float32)
    for first in range(each, rows_ref.shape[1], each):
        total = total + rows_ref[3, first : first + each, :].astype(jnp.float32)
    resid_ref[...] = total.astype(jnp.bfloat16)
    pltpu.make_async_copy(grads_ref, grads_ref, sems.at[8]).wait()


def image_sums(where, pieces, lat_rows):
    n_img = len(pieces)
    slabs, count, _ = pieces[0].shape
    hbm = pl.BlockSpec(memory_space=pl.ANY)
    vmem = pl.BlockSpec(memory_space=pltpu.VMEM)
    return pl.pallas_call(
        image_sums_body,
        in_specs=[pl.BlockSpec(memory_space=pltpu.SMEM)] + [hbm] * n_img,
        out_specs=[hbm, vmem, vmem],
        out_shape=[
            jax.ShapeDtypeStruct((NBLK // n_img, BLK, BLK), jnp.bfloat16),
            jax.ShapeDtypeStruct((CEXT, DL), jnp.bfloat16),
            jax.ShapeDtypeStruct((lat_rows, DL), jnp.bfloat16),
        ],
        scratch_shapes=[
            pltpu.VMEM((slabs, n_img * count, DL), jnp.bfloat16),
            pltpu.VMEM((3, DL, DL), jnp.bfloat16),
            pltpu.VMEM((BLK, BLK), jnp.bfloat16),
            pltpu.SemaphoreType.DMA((9,)),
        ],
        cost_estimate=cost(8 * n_img * count * DL * DL, 16 * DL * DL),
        name="image_sums",
    )(where, *pieces)


def two_bf16(values_in):
    head = values_in.astype(jnp.bfloat16)
    return (head, (values_in - head.astype(jnp.float32)).astype(jnp.bfloat16))


def product_f32(left_side, right_side):
    left_head, left_rest = two_bf16(left_side)
    right_head, right_rest = two_bf16(right_side)
    both = dot(
        jnp.concatenate([left_head, left_rest], axis=1),
        jnp.concatenate([right_head, right_head], axis=0),
    )
    return both + dot(left_head, right_rest)


def update_body(block_ref, lat_ref, dq_ref, sum_ref, ls_ref, rs_ref, lr_ref, rr_ref, ma_ref, *outs):
    new_left, new_right, new_master, new_copy = outs
    side = DL // BLK
    for slot in range(ma_ref.shape[0]):
        block = block_ref[slot]
        is_query = block < PER_MATRIX
        inside = jnp.where(is_query, block, 0)
        row = pl.multiple_of(inside // side * BLK, BLK)
        column = pl.multiple_of(inside % side * BLK, BLK)
        own = contract_rows(lat_ref[:, pl.ds(row, BLK)], dq_ref[:, pl.ds(column, BLK)])
        grad = jnp.where(is_query, own, sum_ref[slot])
        turned = grad.T
        new_left[slot] = 0.5 * ls_ref[slot] + 0.5 * product_f32(grad, turned)
        new_right[slot] = 0.5 * rs_ref[slot] + 0.5 * product_f32(turned, grad)
        shampoo = product_f32(product_f32(lr_ref[slot], grad), rr_ref[slot])
        mean_square = jnp.mean(shampoo * shampoo)
        updated = ma_ref[slot] - 0.5 / math.sqrt(DL) * (shampoo / jnp.sqrt(mean_square + 1e-06))
        new_master[slot] = updated
        new_copy[slot] = updated.astype(jnp.bfloat16)


def update_slots(blocks, lat_low, d_query, sums, left_stat, right_stat, left_root, right_root, master):
    vmem = pl.BlockSpec(memory_space=pltpu.VMEM)
    shape = jax.ShapeDtypeStruct(master.shape, jnp.float32)
    return pl.pallas_call(
        update_body,
        in_specs=[pl.BlockSpec(memory_space=pltpu.SMEM)] + [vmem] * 8,
        out_specs=[vmem] * 4,
        out_shape=[shape, shape, shape, jax.ShapeDtypeStruct(master.shape, jnp.bfloat16)],
        name="update_slots",
    )(blocks, lat_low, d_query, sums, left_stat, right_stat, left_root, right_root, master)


def root_mean(total, count):
    return jnp.sqrt(total / count + 1e-06)


def finish_body(even_ref, late_ref, key_ref, query_ref, wq_ref, *rest):
    own_ref, other_ref, kv_ref, lat_ref, gains_ref, *outs = rest
    dq_ref, kv_grad_ref, new_kv_ref, lat_grad_ref, new_lat_ref, gain_ref, new_gain_ref = outs
    inv_root = 1.0 / math.sqrt(DL)
    late = late_ref[...]
    even = even_ref[0] == 0

    def early(first, stop):
        own = own_ref[first:stop].astype(jnp.float32)
        other = other_ref[first:stop].astype(jnp.float32)
        return jnp.concatenate(
            [jnp.where(even, own, other), jnp.where(even, other, own)], axis=1
        )

    d_query = (contract_rows(late, key_ref[...]) * inv_root).astype(jnp.bfloat16)
    dq_ref[...] = d_query
    key_total = (dot(late, query_ref[...]) * inv_root)[:CIN]
    value_total = early(0, CEXT)[:CIN]
    for at, grad in enumerate((key_total, value_total)):
        kv_grad_ref[:, at, :] = grad
        step = 0.3 / math.sqrt(CIN) / root_mean(jnp.sum(grad * grad), CIN * DL)
        new_kv_ref[:, at, :] = kv_ref[:, at, :] - step * grad
    d_lat_norm = dot_last(d_query, wq_ref[...])
    lat = lat_ref[...]
    centred = lat - jnp.mean(lat, axis=-1, keepdims=True)
    scale = lax.rsqrt(jnp.mean(centred * centred, axis=-1, keepdims=True) + 1e-05)
    normed = centred * scale
    dy = d_lat_norm * gains_ref[0:1]
    along = jnp.mean(dy * normed, axis=-1, keepdims=True)
    back = (dy - jnp.mean(dy, axis=-1, keepdims=True) - normed * along) * scale
    lat_grad = early(CEXT, CEXT + LAT) + back
    lat_grad_ref[...] = lat_grad
    new_lat_ref[...] = lat - 0.3 / root_mean(jnp.sum(lat_grad * lat_grad), LAT * DL) * lat_grad
    tail = late[CIN + 1 : CEXT].astype(jnp.float32)
    second = jnp.concatenate([tail[0:1], tail[1:2]], axis=1)
    for at, grad in enumerate((jnp.sum(d_lat_norm * normed, axis=0, keepdims=True), second)):
        gain_ref[at : at + 1] = grad
        step = 0.2 / root_mean(jnp.sum(grad * grad), DL)
        new_gain_ref[at : at + 1] = gains_ref[at : at + 1] - step * grad


def finish(even, late, w_key, query, w_query, early, other, kv_weight, latent_array, lat_gains):
    vmem = pl.BlockSpec(memory_space=pltpu.VMEM)
    kv = jnp.swapaxes(kv_weight, 0, 1)
    kv_shape = jax.ShapeDtypeStruct(kv.shape, jnp.float32)
    lat_shape = jax.ShapeDtypeStruct((LAT, DL), jnp.float32)
    gain_shape = jax.ShapeDtypeStruct(lat_gains.shape, jnp.float32)
    outs = pl.pallas_call(
        finish_body,
        in_specs=[pl.BlockSpec(memory_space=pltpu.SMEM)] + [vmem] * 9,
        out_specs=[vmem] * 7,
        out_shape=[jax.ShapeDtypeStruct((LAT, DL), jnp.bfloat16)]
        + [kv_shape] * 2
        + [lat_shape] * 2
        + [gain_shape] * 2,
        cost_estimate=cost(4 * LAT * DL * DL, 40 * LAT * DL),
        name="finish",
    )(even, late, w_key, query, w_query, early, other, kv, latent_array, lat_gains)
    d_query, kv_grad, new_kv, *others = outs
    return (d_query, jnp.swapaxes(kv_grad, 0, 1), jnp.swapaxes(new_kv, 0, 1), *others)


def swap(array, axis):
    return lax.all_to_all(array, axis, 0, 0, tiled=True)


def everyone(array, axis):
    return swap(jnp.broadcast_to(array[None], (lax.axis_size(axis), *array.shape)), axis)


def near_hop(array, axis):
    size = lax.axis_size(axis)
    return lax.ppermute(array, axis, [(i, i ^ 1) for i in range(size)])


def far_hop(array, axis, step):
    size = lax.axis_size(axis)
    return lax.ppermute(array, axis, [(i, (i + 2 * step) % size) for i in range(size)])


def spread(array, rows, axis, hops):
    size = lax.axis_size(axis)
    column = {("img", "far"): 0, ("img", "near"): 1, ("pix", "far"): 2, ("pix", "near"): 3}
    got = [array]
    places = [rows]
    for step in range(1, 2 if hops == "near" else size // 2):
        got.append(near_hop(array, axis) if hops == "near" else far_hop(array, axis, step))
        moved = rows.copy()
        moved[:, column[axis, hops]] += step
        places.append(moved)
    return (jnp.concatenate(got), np.concatenate(places))


ROUTES = (
    (("pix", "near"), ("img", "far"), ("pix", "far")),
    (("img", "far"), ("pix", "far"), ("pix", "near")),
    (("pix", "far"), ("pix", "near"), ("img", "far")),
)


def gather_blocks(low, feats):
    slots_dev = low.shape[0]
    n_pix = lax.axis_size("pix")
    if slots_dev < 4 or n_pix > 8:
        low = lax.all_gather(low, ("img", "pix"), axis=0, tiled=True)
        return ([low], jnp.arange(NBLK), feats)
    quarter = slots_dev // 4
    states = []
    bounds = (0, quarter, 2 * quarter, slots_dev)
    for part in range(3):
        start, stop = bounds[part], bounds[part + 1]
        rows = np.zeros((stop - start, 5), np.int32)
        rows[:, 4] = np.arange(start, stop)
        states.append((low[start:stop], rows))
    for phase in range(3):
        states = [spread(*state, *ROUTES[part][phase]) for part, state in enumerate(states)]
    held, feats = lax.optimization_barrier(([array for array, _ in states], feats))
    arrays = []
    places = []
    for array, (_, rows) in zip(held, states):
        arrays += [array, near_hop(array, "img")]
        mate = rows.copy()
        mate[:, 1] += 1
        places += [rows, mate]
    img_far, img_near, pix_far, pix_near, slot = np.concatenate(places).T
    img = lax.axis_index("img")
    pix = lax.axis_index("pix")
    n_far = lax.axis_size("img") // 2
    img_of = (img // 2 - img_far) % n_far * 2 + (img + img_near) % 2
    pix_of = (pix // 2 - pix_far) % (n_pix // 2) * 2 + (pix + pix_near) % 2
    return (arrays, (img_of * n_pix + pix_of) * slots_dev + slot, feats)


def split_near(array, axis):
    size = lax.axis_size(axis)
    near = lax.axis_index(axis) % 2
    pairs = array.reshape(size // 2, 2, *array.shape[1:])
    return (
        lax.dynamic_index_in_dim(pairs, near, 1, False),
        lax.dynamic_index_in_dim(pairs, 1 - near, 1, False),
    )


def join_near(kept, sent, axis):
    got = near_hop(sent, axis)
    return (kept.astype(jnp.float32) + got.astype(jnp.float32)).astype(jnp.bfloat16)


def own_far(kept, axis):
    return lax.dynamic_index_in_dim(kept, lax.axis_index(axis) // 2, 0, False).astype(jnp.float32)


def from_far_parts(kept, axis, steps):
    size = lax.axis_size(axis)
    parts = []
    for step in steps:
        at = (lax.axis_index(axis) // 2 + step) % (size // 2)
        part = lax.dynamic_index_in_dim(kept, at, 0, False)
        parts.append(far_hop(part, axis, step))
    return parts


def from_far(kept, axis, steps):
    total = 0.0
    for part in from_far_parts(kept, axis, steps):
        total = total + part.astype(jnp.float32)
    return total


def sum_far(kept, axis):
    return own_far(kept, axis) + from_far(kept, axis, range(1, lax.axis_size(axis) // 2))


def gather_far(array, axis):
    size = lax.axis_size(axis)
    far = lax.axis_index(axis) // 2
    got = [array] + [far_hop(array, axis, step) for step in range(1, size // 2)]
    return lax.dynamic_slice_in_dim(jnp.stack(got[::-1] * 2), size // 2 - 1 - far, size // 2, 0)


def gather_near(array, axis):
    near = lax.axis_index(axis) % 2
    other = near_hop(array, axis)
    both = jnp.where(
        near == 0, jnp.stack([array, other], axis=1), jnp.stack([other, array], axis=1)
    )
    return both.reshape(lax.axis_size(axis), *array.shape[1:])


def latent_pass(numerator, denominator, lat_part, cot_rows, lat_gain, w_out, w_up, w_down):
    attended = numerator / denominator[..., None]
    att_low = attended.astype(jnp.bfloat16)
    resid = lat_part[None] + product("mrd,de->mre", att_low, w_out)
    normed, normed_back = jax.vjp(standardize, resid)
    hn_low = (normed * lat_gain).astype(jnp.bfloat16)
    hidden = product("mrd,de->mre", hn_low, w_up)
    active, active_back = jax.vjp(gelu_exact, hidden)
    act_low = active.astype(jnp.bfloat16)
    latents_out = resid + product("mrd,de->mre", act_low, w_down)
    g_mlp = cot_rows.astype(jnp.bfloat16)
    d_active = product("mre,de->mrd", g_mlp, w_down)
    d_hidden = active_back(d_active)[0].astype(jnp.bfloat16)
    d_normed = product("mre,de->mrd", d_hidden, w_up)
    d_resid = cot_rows + normed_back(d_normed * lat_gain)[0]
    d_branch = d_resid.astype(jnp.bfloat16)
    d_attended = product("mre,de->mrd", d_branch, w_out)
    d_numer = d_attended / denominator[..., None]
    d_denom = -jnp.sum(d_attended * numerator / (denominator * denominator)[..., None], axis=-1)
    gain_mlp = jnp.sum(d_normed * normed, axis=(0, 1))
    row_arrays = (att_low, hn_low, act_low, d_branch, d_hidden, g_mlp)
    return (latents_out, d_numer.astype(jnp.bfloat16), d_denom, (row_arrays, gain_mlp))


def shards(
    pixels,
    sides,
    owner,
    master,
    left_stat,
    right_stat,
    left_root,
    right_root,
    kv_weight,
    latent_array,
    in_gain,
    lat_gains,
    cotangent,
):
    micro = pixels.shape[0]
    rows_dev = pixels.shape[2]
    n_pix = lax.axis_size("pix")
    n_img = lax.axis_size("img")
    img = lax.axis_index("img")
    pix = lax.axis_index("pix")
    slots_dev = master.shape[0]
    lat_rows = LAT // n_pix
    row_start = pix * lat_rows
    inv_root = 1.0 / math.sqrt(DL)

    place = jnp.concatenate([(pix * rows_dev)[None], sides * sides]).astype(jnp.int32)
    across = lies_across(pixels)
    gain_column = in_gain[:, None]
    feats = None
    for micro_index in range(micro - 1):
        feats = prepare_pixels(micro_index, feats, place, across, gain_column)
    sources, source_slots, feats = gather_blocks(master.astype(jnp.bfloat16), feats)
    feats, scales = prepare_pixels(micro - 1, feats, place, across, gain_column)
    all_blocks = jnp.arange(NBLK, dtype=jnp.int32)
    source_blocks = jnp.sum(
        jnp.where(source_slots[:, None] == owner[None], all_blocks[None], 0), axis=1
    )
    kv_low = kv_weight.astype(jnp.bfloat16)
    w_key = jnp.pad(kv_low[0], ((0, CEXT - CIN), (0, 0)))
    w_value = kv_low[1]
    lat_low, query, query_cols, w_query, w_out, w_up, w_down = make_query(
        source_blocks.astype(jnp.int32), sources, latent_array, lat_gains[0], w_key
    )

    weights, sums = attend(feats, query_cols)
    sums = sums.reshape(micro, CEXT, n_pix, lat_rows).transpose(2, 1, 0, 3)
    sums = swap(sums.reshape(n_pix, CEXT, micro * lat_rows), "pix")
    sums = jnp.sum(sums.astype(jnp.float32), axis=0)
    numer_in = sums[:CIN]
    denominator = (sums[ONES_ROW] + sums[ONES_ROW + 1]).reshape(micro, lat_rows)
    numerator = fine("cr,cd->rd", numer_in, w_value).reshape(micro, lat_rows, DL)
    latents_out, d_numer, d_denom, latent_grads = latent_pass(
        numerator,
        denominator,
        lax.dynamic_slice_in_dim(latent_array, row_start, lat_rows, 0),
        cotangent[:, 0],
        lat_gains[1],
        w_out,
        w_up,
        w_down,
    )
    row_arrays, gain_mlp = latent_grads
    d_numer = d_numer.reshape(micro * lat_rows, DL)
    head, rest = two_terms(d_denom.reshape(1, micro * lat_rows))
    d_cols = product("rd,cd->cr", d_numer, w_value).astype(jnp.bfloat16)
    d_cols = jnp.concatenate([d_cols, head, rest, jnp.zeros_like(head)], axis=0)
    d_cols = everyone(d_cols, "pix").reshape(n_pix, CEXT, micro, lat_rows)
    d_cols = d_cols.transpose(2, 1, 0, 3).reshape(micro, CEXT, LAT)

    numer_rows = jnp.pad(numer_in.astype(jnp.bfloat16).T, ((0, 0), (0, DL - CIN)))
    own = jnp.stack(
        [array.reshape(micro * lat_rows, DL) for array in row_arrays] + [d_numer, numer_rows]
    )
    mate = [(i, i ^ 1) for i in range(n_img)]
    pieces = [own, lax.ppermute(own, "img", mate)]
    images = [img, img ^ 1]
    far = []
    for step in range(1, n_img // 2):
        hop = [(i, (i + 2 * step) % n_img) for i in range(n_img)]
        far.append(lax.ppermute(own, "img", hop))
        images += [(img - 2 * step) % n_img, (img - 2 * step) % n_img ^ 1]
    device_of = owner // slots_dev
    place_of = device_of % n_pix * slots_dev + owner % slots_dev
    where = jnp.where(device_of // n_pix == img, place_of, -1)

    results = (None,)
    score_sum = jnp.zeros((CEXT, LAT), jnp.float32)
    gain_sum = jnp.zeros((CIN, BLK), jnp.float32)
    width = DL // 2
    each = -(-CEXT // n_pix)
    parts = parts_of(feats)
    for at, part in enumerate(parts):
        if at == len(parts) - 2:
            far, gain_sum = lax.optimization_barrier((far, gain_sum))
            for piece in far:
                pieces += [piece, lax.ppermute(piece, "img", mate)]
        if at == len(parts) - 1:
            pieces, gain_sum = lax.optimization_barrier((pieces, gain_sum))
            where = jnp.concatenate([jnp.stack(images), where]).astype(jnp.int32)
            grads, value_part, resid_part = image_sums(where, pieces, lat_rows)
            value_part = jnp.pad(value_part, ((0, each * n_pix - CEXT), (0, 0)))
            value_part = lax.dynamic_slice_in_dim(value_part, img % 2 * width, width, 1)
            value_sides = split_near(value_part.reshape(n_pix, each, width), "pix")
            grad_sides = split_near(grads.reshape(n_pix, slots_dev, BLK, BLK), "pix")
            value_part = join_near(*value_sides, "pix")
            gain_column, value_part, grad_sides = lax.optimization_barrier(
                (gain_column, value_part, grad_sides)
            )
        results = attend_back(
            part, results[0], scales, feats, weights, gain_column, d_cols, query_cols
        )
        score_sum = score_sum + results[1]
        gain_sum = gain_sum + results[2]
    pixel_grad = jnp.swapaxes(results[0].reshape(micro, 1, CIN, rows_dev), 2, 3)

    gain_sum = jnp.sum(gain_sum, axis=1)[None] / in_gain[None]
    late = jnp.concatenate(
        [
            score_sum[:CIN],
            jnp.pad(gain_sum, ((0, 0), (0, LAT - CIN))),
            gain_mlp.reshape(DL // LAT, LAT),
        ],
        axis=0,
    ).astype(jnp.bfloat16)
    late = jnp.pad(late, ((0, each * n_pix - CEXT), (0, 0))).reshape(n_pix, each, LAT)
    late = jnp.sum(swap(late, "pix").astype(jnp.float32), axis=0)
    value_part = sum_far(value_part, "pix").astype(jnp.bfloat16)
    grads = join_near(*grad_sides, "pix")
    late, value_part, grads = lax.optimization_barrier((late, value_part, grads))
    late = jnp.sum(everyone(late, "img"), axis=0).astype(jnp.bfloat16)
    resid_part = lax.dynamic_slice_in_dim(resid_part, img % 2 * width, width, 1)
    early = gather_far(jnp.concatenate([value_part, resid_part], axis=0), "pix")
    longest = n_pix // 4
    grad_sum = own_far(grads, "pix") + from_far(grads, "pix", (longest,))
    late, early, grad_sum = lax.optimization_barrier((late, early, grad_sum))
    late = everyone(late, "pix").reshape(n_pix * each, LAT)[:CEXT]
    late, grads = lax.optimization_barrier((late, grads))
    others = [step for step in range(1, n_pix // 2) if step != longest]
    grads = from_far_parts(grads, "pix", others)
    early = gather_near(early, "pix")
    value_part = early[:, :each].reshape(n_pix * each, width)[:CEXT]
    early = jnp.concatenate([value_part, early[:, each:].reshape(LAT, width)], axis=0)
    other = near_hop(early, "img")
    d_query, kv_grad, new_kv, latent_grad, new_latent, lat_gain_grad, new_lat_gains = finish(
        (img % 2)[None], late, w_key, query, w_query, early, other, kv_weight, latent_array, lat_gains
    )
    grad_sum, d_query = lax.optimization_barrier((grad_sum, d_query))
    for part in grads:
        grad_sum = grad_sum + part.astype(jnp.float32)
    grads = grad_sum
    in_gain_grad = late[CIN, :CIN].astype(jnp.float32)

    mine = (img * n_pix + pix) * slots_dev + jnp.arange(slots_dev, dtype=jnp.int32)
    blocks = jnp.sum(
        jnp.where(owner[None] == mine[:, None], all_blocks[None], 0), axis=1
    )
    new_left, new_right, new_master, new_copy = update_slots(
        blocks.astype(jnp.int32),
        lat_low,
        d_query,
        grads,
        left_stat,
        right_stat,
        left_root,
        right_root,
        master,
    )
    new_in_gain = in_gain - 0.2 * normalized(in_gain_grad, (0,))
    return (
        latents_out[:, None],
        pixel_grad,
        new_left,
        new_right,
        new_master,
        new_copy,
        kv_grad,
        new_kv,
        latent_grad,
        new_latent,
        in_gain_grad,
        new_in_gain,
        lat_gain_grad,
        new_lat_gains,
    )


def solution(mesh):
    pixel_spec = P(None, "img", "pix", None)
    slot_spec = P(("img", "pix"), None, None)
    in_specs = (
        (pixel_spec, P(), P()) + (slot_spec,) * 5 + (P(),) * 4 + (pixel_spec,)
    )
    out_specs = (pixel_spec, pixel_spec) + (slot_spec,) * 4 + (P(),) * 8
    return jax.shard_map(shards, mesh=mesh, in_specs=in_specs, out_specs=out_specs, check_vma=False)
```

```python
import functools
import math

import jax
import jax.numpy as jnp
from jax import lax
import numpy as np
from jax.experimental import pallas as pl
from jax.experimental.pallas import tpu as pltpu
from jax.sharding import PartitionSpec as P

CIN = 261
DL = 1024
LAT = 512
BLK = 128
NBLK = 256
PER_MATRIX = NBLK // 4
CEXT = 264
WHOLE = CIN // 8 * 8
ONES_ROW = 261
MASK_ROW = 263
MASKED = -1e30

HIGHEST_PRECISION = lax.Precision.HIGHEST


def standardize(values_in):
    average = jnp.mean(values_in, axis=-1, keepdims=True)
    centred = values_in - average
    variance = jnp.mean(centred * centred, axis=-1, keepdims=True)
    return centred * lax.rsqrt(variance + 1e-05)


def gelu_exact(values_in):
    return jax.nn.gelu(values_in, approximate=False)


def normalized(gradient, reduce_axes):
    return gradient / jnp.sqrt(
        jnp.mean(gradient * gradient, axis=reduce_axes, keepdims=True) + 1e-06
    )


def product(pattern, left_side, right_side):
    return jnp.einsum(pattern, left_side, right_side, preferred_element_type=jnp.float32)


def fine(pattern, left_side, right_side):
    return jnp.einsum(
        pattern,
        left_side.astype(jnp.float32),
        right_side.astype(jnp.float32),
        precision=HIGHEST_PRECISION,
    )


def two_terms(values_in):
    head = lax.reduce_precision(values_in, 8, 7)
    return (head.astype(jnp.bfloat16), (values_in - head).astype(jnp.bfloat16))


def contract_rows(left_side, right_side, precision=None):
    return lax.dot_general(
        left_side,
        right_side,
        (((0,), (0,)), ((), ())),
        precision=precision,
        preferred_element_type=jnp.float32,
    )


def dot(left_side, right_side):
    return jnp.dot(left_side, right_side, preferred_element_type=jnp.float32)


def dot_last(left_side, right_side):
    return lax.dot_general(
        left_side, right_side, (((1,), (1,)), ((), ())), preferred_element_type=jnp.float32
    )


def tile_of(rows, most):
    return max((size for size in range(128, most + 1, 128) if rows % size == 0), default=rows)


def lies_across(pixels):
    micro, _, rows_dev, _ = pixels.shape
    return jnp.swapaxes(pixels, 2, 3).reshape(micro, CIN, 1, rows_dev)


def centre(pix):
    centred = pix - jnp.mean(pix, axis=0, keepdims=True)
    scale = lax.rsqrt(jnp.mean(centred * centred, axis=0, keepdims=True) + 1e-05)
    return (centred * scale, scale)


def cost(flops, count):
    return pl.CostEstimate(flops=int(flops), bytes_accessed=int(count), transcendentals=0)


def prepare_body(place_ref, pix_ref, gain_ref, *rest, micro_index):
    out_ref, scale_ref = rest[-2:]
    columns = pix_ref.shape[3]
    gain = gain_ref[...]
    width = BLK if columns % BLK == 0 else columns
    if width == BLK:
        pix_rows = pix_ref.reshape(CIN * columns // BLK, BLK)
    extra = (CEXT - CIN, width)
    row = lax.broadcasted_iota(jnp.int32, extra, 0) + CIN
    slot = place_ref[0] + pl.program_id(0) * columns + lax.broadcasted_iota(jnp.int32, extra, 1)
    for column in range(0, columns, width):
        inside = slice(column, column + width)
        if width == BLK:
            pix = jnp.concatenate(
                [
                    pix_rows[pl.ds(column // BLK, WHOLE, stride=columns // BLK), :],
                    pix_ref[0, WHOLE:, 0, inside],
                ],
                axis=0,
            )
        else:
            pix = pix_ref[0, :, 0, :]
        normed, scale_ref[0, :, inside] = centre(pix)
        mask = jnp.where(slot + column < place_ref[1 + micro_index], 0.0, MASKED)
        tail = jnp.where(row == MASK_ROW, mask, 1.0)
        full = jnp.concatenate([normed * gain, tail], axis=0)
        out_ref[0, :, inside] = full.astype(jnp.bfloat16)


def prepare_pixels(micro_index, earlier, place, across, gain_column):
    micro, _, _, rows_dev = across.shape
    rows = tile_of(rows_dev, 1152)
    m = micro_index
    in_specs = [
        pl.BlockSpec(memory_space=pltpu.SMEM),
        pl.BlockSpec((1, CIN, 1, rows), lambda t: (m, 0, 0, t)),
        pl.BlockSpec((CIN, 1), lambda t: (0, 0)),
    ]
    operands = [place, across, gain_column]
    aliases = {}
    if earlier is not None:
        in_specs += [pl.BlockSpec(memory_space=pl.ANY)] * 2
        aliases = {len(operands): 0, len(operands) + 1: 1}
        operands += earlier
    return pl.pallas_call(
        functools.partial(prepare_body, micro_index=m),
        grid=(rows_dev // rows,),
        in_specs=in_specs,
        out_specs=[
            pl.BlockSpec((1, CEXT, rows), lambda t: (m, 0, t)),
            pl.BlockSpec((1, 1, rows), lambda t: (m, 0, t)),
        ],
        out_shape=[
            jax.ShapeDtypeStruct((micro, CEXT, rows_dev), jnp.bfloat16),
            jax.ShapeDtypeStruct((micro, 1, rows_dev), jnp.float32),
        ],
        input_output_aliases=aliases,
        cost_estimate=cost(0, 12 * rows_dev * CEXT),
        name="prepare_pixels",
    )(*operands)


def spans_of(columns):
    if columns == 1152:
        return ((0, 512), (512, 384), (896, 256))
    return ((0, columns),)


def short_spans_of(columns):
    if columns == 1152:
        return tuple((first, min(256, columns - first)) for first in range(0, columns, 256))
    return ((0, columns),)


def attend_body(feat_ref, query_ref, exp_ref, out_ref, sum_ref):
    tile = pl.program_id(1)
    spans = spans_of(feat_ref.shape[2])
    query = query_ref[...]

    def scores_of(at):
        first, size = spans[at]
        return contract_rows(feat_ref[0, :, first : first + size], query)

    @pl.when(tile == 0)
    def _():
        sum_ref[...] = jnp.zeros_like(sum_ref)

    scores = scores_of(0)
    total = sum_ref[...]
    for at, (first, size) in enumerate(spans):
        ahead = scores_of(at + 1) if at + 1 < len(spans) else None
        weights = jnp.exp(scores).astype(jnp.bfloat16)
        exp_ref[0, first : first + size] = weights
        total = total + dot(feat_ref[0, :, first : first + size], weights)
        scores = ahead
    sum_ref[...] = total

    @pl.when(tile == pl.num_programs(1) - 1)
    def _():
        sums = sum_ref[...]
        low = sums.astype(jnp.bfloat16)
        rest = (sums - low.astype(jnp.float32))[ONES_ROW : ONES_ROW + 1]
        row = lax.broadcasted_iota(jnp.int32, sums.shape, 0)
        out_ref[0] = jnp.where(row == ONES_ROW + 1, rest, sums).astype(jnp.bfloat16)


def attend(feats, query_cols):
    micro, _, rows_dev = feats.shape
    rows = tile_of(rows_dev, 1152)
    return pl.pallas_call(
        attend_body,
        grid=(micro, rows_dev // rows),
        in_specs=[
            pl.BlockSpec((1, CEXT, rows), lambda m, t: (m, 0, t)),
            pl.BlockSpec((CEXT, LAT), lambda m, t: (0, 0)),
        ],
        out_specs=[
            pl.BlockSpec((1, rows, LAT), lambda m, t: (m, t, 0)),
            pl.BlockSpec((1, CEXT, LAT), lambda m, t: (m, 0, 0)),
        ],
        out_shape=[
            jax.ShapeDtypeStruct((micro, rows_dev, LAT), jnp.bfloat16),
            jax.ShapeDtypeStruct((micro, CEXT, LAT), jnp.bfloat16),
        ],
        scratch_shapes=[pltpu.VMEM((CEXT, LAT), jnp.float32)],
        cost_estimate=cost(8 * micro * rows_dev * LAT * CEXT, 4 * micro * rows_dev * LAT),
        name="attend",
    )(feats, query_cols)


def tiles_of(feats):
    rows_dev = feats.shape[2]
    return rows_dev // tile_of(rows_dev, 1152)


def parts_of(feats):
    micro = feats.shape[0]
    tiles = tiles_of(feats)
    parts = []
    for m in range(micro):
        sizes = [tiles]
        if m == micro - 1 and tiles >= 4:
            sizes = [tiles // 4, tiles // 2, tiles - tiles // 4 - tiles // 2]
        parts += [(m, sum(sizes[:at]), size) for at, size in enumerate(sizes)]
    return parts


def attend_back_body(scale_ref, feat_ref, exp_ref, gain_ref, dc_ref, qc_ref, *rest):
    grad_ref, score_ref, gain_sum_ref = rest[-3:]
    spans = short_spans_of(feat_ref.shape[2])
    d_cols = dc_ref[0]
    both_cols = jnp.concatenate([qc_ref[...], d_cols], axis=1)

    @pl.when(pl.program_id(0) == 0)
    def _():
        score_ref[...] = jnp.zeros_like(score_ref)
        gain_sum_ref[...] = jnp.zeros_like(gain_sum_ref)

    def products(at):
        first, size = spans[at]
        feats = feat_ref[0, :, first : first + size]
        weights = exp_ref[0, first : first + size]
        d_exp = contract_rows(feats, d_cols)
        d_scores = (weights.astype(jnp.float32) * d_exp).astype(jnp.bfloat16)
        d_pix = dot_last(both_cols, jnp.concatenate([d_scores, weights], axis=1))
        return (dot(feats, d_scores), d_pix)

    columns = feat_ref.shape[2]
    whole_lanes = columns % BLK == 0
    if whole_lanes:
        grad_rows = grad_ref.reshape(CIN * columns // BLK, BLK)
    gain = gain_ref[...]
    inverse = 1.0 / gain
    score, d_pix = products(0)
    gain_sum = gain_sum_ref[...]
    for at, (first, size) in enumerate(spans):
        ahead = products(at + 1) if at + 1 < len(spans) else None
        for column in range(0, size, BLK):
            width = min(BLK, size - column)
            inside = slice(first + column, first + column + width)
            feats = feat_ref[0, :, inside].astype(jnp.float32)[:CIN]
            part = d_pix[:CIN, column : column + width]
            scale = scale_ref[0, :, inside]
            along = feats * part
            if width == BLK:
                gain_sum = gain_sum + along
            else:
                gain_sum = gain_sum + jnp.sum(along, axis=1, keepdims=True) * (1.0 / BLK)
            along = jnp.mean(along, axis=0, keepdims=True) * scale
            d_normed = part * gain
            level = jnp.mean(d_normed, axis=0, keepdims=True) * scale
            grad = d_normed * scale - level - feats * inverse * along
            if whole_lanes:
                at_row = (first + column) // BLK
                grad_rows[pl.ds(at_row, WHOLE, stride=columns // BLK), :] = grad[:WHOLE]
                grad_ref[0, WHOLE:, 0, inside] = grad[WHOLE:]
            else:
                grad_ref[0, :, 0, inside] = grad
        if ahead is not None:
            score = score + ahead[0]
            d_pix = ahead[1]
    score_ref[...] += score
    gain_sum_ref[...] = gain_sum


def attend_back(part, earlier, scales, feats, weights, gain_column, d_cols, query_cols):
    m, first, tiles = part
    rows = feats.shape[2] // tiles_of(feats)
    in_specs = [
        pl.BlockSpec((1, 1, rows), lambda t: (m, 0, first + t)),
        pl.BlockSpec((1, CEXT, rows), lambda t: (m, 0, first + t)),
        pl.BlockSpec((1, rows, LAT), lambda t: (m, first + t, 0)),
        pl.BlockSpec((CIN, 1), lambda t: (0, 0)),
        pl.BlockSpec((1, CEXT, LAT), lambda t: (m, 0, 0)),
        pl.BlockSpec((CEXT, LAT), lambda t: (0, 0)),
    ]
    operands = [scales, feats, weights, gain_column, d_cols, query_cols]
    aliases = {}
    if earlier is not None:
        in_specs.append(pl.BlockSpec(memory_space=pl.ANY))
        aliases = {len(operands): 0}
        operands.append(earlier)
    return pl.pallas_call(
        attend_back_body,
        grid=(tiles,),
        in_specs=in_specs,
        out_specs=[
            pl.BlockSpec((1, CIN, 1, rows), lambda t: (m, 0, 0, first + t)),
            pl.BlockSpec((CEXT, LAT), lambda t: (0, 0)),
            pl.BlockSpec((CIN, BLK), lambda t: (0, 0)),
        ],
        out_shape=[
            jax.ShapeDtypeStruct((feats.shape[0], CIN, 1, feats.shape[2]), jnp.float32),
            jax.ShapeDtypeStruct((CEXT, LAT), jnp.float32),
            jax.ShapeDtypeStruct((CIN, BLK), jnp.float32),
        ],
        input_output_aliases=aliases,
        cost_estimate=cost(16 * tiles * rows * LAT * CEXT, tiles * rows * 4000),
        name="attend_back",
    )(*operands)


def query_body(block_ref, lat_ref, gain_ref, key_ref, *rest):
    sources, (low_ref, query_ref, cols_ref, *squares, full_ref, sems) = (rest[:-9], rest[-9:])
    side = DL // BLK
    first = 0
    for source in sources:

        @pl.loop(0, source.shape[0], unroll=4)
        def _(at, source=source, first=first):
            block = block_ref[first + at]
            matrix = block // PER_MATRIX
            row = pl.multiple_of(block % PER_MATRIX // side * BLK, BLK)
            column = pl.multiple_of(block % side * BLK, BLK)
            pltpu.make_async_copy(
                source.at[at],
                full_ref.at[matrix, pl.ds(row, BLK), pl.ds(column, BLK)],
                sems.at[matrix],
            ).start()

        first += source.shape[0]

    def keep(matrix):
        return pltpu.make_async_copy(full_ref.at[matrix], squares[matrix], sems.at[4 + matrix])

    lat_low = (standardize(lat_ref[...]) * gain_ref[...]).astype(jnp.bfloat16)
    low_ref[...] = lat_low
    for matrix in range(4):
        pltpu.make_async_copy(full_ref.at[matrix], full_ref.at[matrix], sems.at[matrix]).wait()
        keep(matrix).start()
    query = dot(lat_low, full_ref[0]).astype(jnp.bfloat16)
    query_ref[...] = query
    scores = dot_last(key_ref[...], query) * (1.0 / math.sqrt(DL))
    row = lax.broadcasted_iota(jnp.int32, scores.shape, 0)
    cols_ref[...] = jnp.where(row == MASK_ROW, 1.0, scores).astype(jnp.bfloat16)
    for matrix in range(4):
        keep(matrix).wait()


def make_query(blocks, sources, latent_array, gain, w_key):
    vmem = pl.BlockSpec(memory_space=pltpu.VMEM)
    hbm = pl.BlockSpec(memory_space=pl.ANY)
    rows = jax.ShapeDtypeStruct((LAT, DL), jnp.bfloat16)
    square = jax.ShapeDtypeStruct((DL, DL), jnp.bfloat16)
    return pl.pallas_call(
        query_body,
        in_specs=[pl.BlockSpec(memory_space=pltpu.SMEM), vmem, vmem, vmem] + [hbm] * len(sources),
        out_specs=[vmem] * 3 + [hbm] * 4,
        out_shape=[rows, rows, jax.ShapeDtypeStruct((CEXT, LAT), jnp.bfloat16)] + [square] * 4,
        scratch_shapes=[pltpu.VMEM((4, DL, DL), jnp.bfloat16), pltpu.SemaphoreType.DMA((8,))],
        cost_estimate=cost(3 * LAT * DL * DL, 4 * NBLK * BLK * BLK),
        name="make_query",
    )(blocks, latent_array, gain[None], w_key, *sources)


def image_sums_body(where_ref, *rest):
    n_img = len(rest) - 7
    pieces, (grads_ref, value_ref, resid_ref, rows_ref, full_ref, zero_ref, sems) = (
        rest[:n_img],
        rest[n_img:],
    )
    side = DL // BLK
    count = pieces[0].shape[1]

    def put(source, block):
        place = where_ref[n_img + block]

        @pl.when(place >= 0)
        def _():
            pltpu.make_async_copy(source, grads_ref.at[place], sems.at[8]).start()

    def settle(slab):
        pltpu.make_async_copy(rows_ref.at[slab], rows_ref.at[slab], sems.at[slab]).wait()

    order = (0, 3, 1, 4, 2, 5, 6, 7)
    for piece in range(n_img):
        first = pl.multiple_of(where_ref[piece] * count, count)
        for slab in order:
            pltpu.make_async_copy(
                pieces[piece].at[slab], rows_ref.at[slab, pl.ds(first, count), :], sems.at[slab]
            ).start()
    zero_ref[...] = jnp.zeros_like(zero_ref)

    @pl.loop(0, PER_MATRIX)
    def _(block):
        put(zero_ref, block)

    for matrix in range(3):
        settle(matrix)
        settle(3 + matrix)
        full_ref[matrix] = contract_rows(rows_ref[matrix], rows_ref[3 + matrix]).astype(jnp.bfloat16)

        @pl.loop(0, PER_MATRIX, unroll=4)
        def _(block, matrix=matrix):
            row = pl.multiple_of((block // side) * BLK, BLK)
            column = pl.multiple_of((block % side) * BLK, BLK)
            put(
                full_ref.at[matrix, pl.ds(row, BLK), pl.ds(column, BLK)],
                (matrix + 1) * PER_MATRIX + block,
            )

    settle(6)
    settle(7)
    value_ref[...] = contract_rows(rows_ref[7, :, :CEXT], rows_ref[6]).astype(jnp.bfloat16)
    each = resid_ref.shape[0]
    total = rows_ref[3, :each, :].astype(jnp.float32)
    for first in range(each, rows_ref.shape[1], each):
        total = total + rows_ref[3, first : first + each, :].astype(jnp.float32)
    resid_ref[...] = total.astype(jnp.bfloat16)
    pltpu.make_async_copy(grads_ref, grads_ref, sems.at[8]).wait()


def image_sums(where, pieces, lat_rows):
    n_img = len(pieces)
    slabs, count, _ = pieces[0].shape
    hbm = pl.BlockSpec(memory_space=pl.ANY)
    vmem = pl.BlockSpec(memory_space=pltpu.VMEM)
    return pl.pallas_call(
        image_sums_body,
        in_specs=[pl.BlockSpec(memory_space=pltpu.SMEM)] + [hbm] * n_img,
        out_specs=[hbm, vmem, vmem],
        out_shape=[
            jax.ShapeDtypeStruct((NBLK // n_img, BLK, BLK), jnp.bfloat16),
            jax.ShapeDtypeStruct((CEXT, DL), jnp.bfloat16),
            jax.ShapeDtypeStruct((lat_rows, DL), jnp.bfloat16),
        ],
        scratch_shapes=[
            pltpu.VMEM((slabs, n_img * count, DL), jnp.bfloat16),
            pltpu.VMEM((3, DL, DL), jnp.bfloat16),
            pltpu.VMEM((BLK, BLK), jnp.bfloat16),
            pltpu.SemaphoreType.DMA((9,)),
        ],
        cost_estimate=cost(8 * n_img * count * DL * DL, 16 * DL * DL),
        name="image_sums",
    )(where, *pieces)


def two_bf16(values_in):
    head = values_in.astype(jnp.bfloat16)
    return (head, (values_in - head.astype(jnp.float32)).astype(jnp.bfloat16))


def product_f32(left_side, right_side):
    left_head, left_rest = two_bf16(left_side)
    right_head, right_rest = two_bf16(right_side)
    both = dot(
        jnp.concatenate([left_head, left_rest], axis=1),
        jnp.concatenate([right_head, right_head], axis=0),
    )
    return both + dot(left_head, right_rest)


def update_body(block_ref, lat_ref, dq_ref, sum_ref, ls_ref, rs_ref, lr_ref, rr_ref, ma_ref, *outs):
    new_left, new_right, new_master, new_copy = outs
    side = DL // BLK
    for slot in range(ma_ref.shape[0]):
        block = block_ref[slot]
        is_query = block < PER_MATRIX
        inside = jnp.where(is_query, block, 0)
        row = pl.multiple_of(inside // side * BLK, BLK)
        column = pl.multiple_of(inside % side * BLK, BLK)
        own = contract_rows(lat_ref[:, pl.ds(row, BLK)], dq_ref[:, pl.ds(column, BLK)])
        grad = jnp.where(is_query, own, sum_ref[slot])
        turned = grad.T
        new_left[slot] = 0.5 * ls_ref[slot] + 0.5 * product_f32(grad, turned)
        new_right[slot] = 0.5 * rs_ref[slot] + 0.5 * product_f32(turned, grad)
        shampoo = product_f32(product_f32(lr_ref[slot], grad), rr_ref[slot])
        mean_square = jnp.mean(shampoo * shampoo)
        updated = ma_ref[slot] - 0.5 / math.sqrt(DL) * (shampoo / jnp.sqrt(mean_square + 1e-06))
        new_master[slot] = updated
        new_copy[slot] = updated.astype(jnp.bfloat16)


def update_slots(blocks, lat_low, d_query, sums, left_stat, right_stat, left_root, right_root, master):
    vmem = pl.BlockSpec(memory_space=pltpu.VMEM)
    shape = jax.ShapeDtypeStruct(master.shape, jnp.float32)
    return pl.pallas_call(
        update_body,
        in_specs=[pl.BlockSpec(memory_space=pltpu.SMEM)] + [vmem] * 8,
        out_specs=[vmem] * 4,
        out_shape=[shape, shape, shape, jax.ShapeDtypeStruct(master.shape, jnp.bfloat16)],
        name="update_slots",
    )(blocks, lat_low, d_query, sums, left_stat, right_stat, left_root, right_root, master)


def root_mean(total, count):
    return jnp.sqrt(total / count + 1e-06)


def finish_body(even_ref, late_ref, key_ref, query_ref, wq_ref, *rest):
    own_ref, other_ref, kv_ref, lat_ref, gains_ref, *outs = rest
    dq_ref, kv_grad_ref, new_kv_ref, lat_grad_ref, new_lat_ref, gain_ref, new_gain_ref = outs
    inv_root = 1.0 / math.sqrt(DL)
    late = late_ref[...]
    even = even_ref[0] == 0

    def early(first, stop):
        own = own_ref[first:stop].astype(jnp.float32)
        other = other_ref[first:stop].astype(jnp.float32)
        return jnp.concatenate(
            [jnp.where(even, own, other), jnp.where(even, other, own)], axis=1
        )

    d_query = (contract_rows(late, key_ref[...]) * inv_root).astype(jnp.bfloat16)
    dq_ref[...] = d_query
    key_total = (dot(late, query_ref[...]) * inv_root)[:CIN]
    value_total = early(0, CEXT)[:CIN]
    for at, grad in enumerate((key_total, value_total)):
        kv_grad_ref[:, at, :] = grad
        step = 0.3 / math.sqrt(CIN) / root_mean(jnp.sum(grad * grad), CIN * DL)
        new_kv_ref[:, at, :] = kv_ref[:, at, :] - step * grad
    d_lat_norm = dot_last(d_query, wq_ref[...])
    lat = lat_ref[...]
    centred = lat - jnp.mean(lat, axis=-1, keepdims=True)
    scale = lax.rsqrt(jnp.mean(centred * centred, axis=-1, keepdims=True) + 1e-05)
    normed = centred * scale
    dy = d_lat_norm * gains_ref[0:1]
    along = jnp.mean(dy * normed, axis=-1, keepdims=True)
    back = (dy - jnp.mean(dy, axis=-1, keepdims=True) - normed * along) * scale
    lat_grad = early(CEXT, CEXT + LAT) + back
    lat_grad_ref[...] = lat_grad
    new_lat_ref[...] = lat - 0.3 / root_mean(jnp.sum(lat_grad * lat_grad), LAT * DL) * lat_grad
    tail = late[CIN + 1 : CEXT].astype(jnp.float32)
    second = jnp.concatenate([tail[0:1], tail[1:2]], axis=1)
    for at, grad in enumerate((jnp.sum(d_lat_norm * normed, axis=0, keepdims=True), second)):
        gain_ref[at : at + 1] = grad
        step = 0.2 / root_mean(jnp.sum(grad * grad), DL)
        new_gain_ref[at : at + 1] = gains_ref[at : at + 1] - step * grad


def finish(even, late, w_key, query, w_query, early, other, kv_weight, latent_array, lat_gains):
    vmem = pl.BlockSpec(memory_space=pltpu.VMEM)
    kv = jnp.swapaxes(kv_weight, 0, 1)
    kv_shape = jax.ShapeDtypeStruct(kv.shape, jnp.float32)
    lat_shape = jax.ShapeDtypeStruct((LAT, DL), jnp.float32)
    gain_shape = jax.ShapeDtypeStruct(lat_gains.shape, jnp.float32)
    outs = pl.pallas_call(
        finish_body,
        in_specs=[pl.BlockSpec(memory_space=pltpu.SMEM)] + [vmem] * 9,
        out_specs=[vmem] * 7,
        out_shape=[jax.ShapeDtypeStruct((LAT, DL), jnp.bfloat16)]
        + [kv_shape] * 2
        + [lat_shape] * 2
        + [gain_shape] * 2,
        cost_estimate=cost(4 * LAT * DL * DL, 40 * LAT * DL),
        name="finish",
    )(even, late, w_key, query, w_query, early, other, kv, latent_array, lat_gains)
    d_query, kv_grad, new_kv, *others = outs
    return (d_query, jnp.swapaxes(kv_grad, 0, 1), jnp.swapaxes(new_kv, 0, 1), *others)


def swap(array, axis):
    return lax.all_to_all(array, axis, 0, 0, tiled=True)


def everyone(array, axis):
    return swap(jnp.broadcast_to(array[None], (lax.axis_size(axis), *array.shape)), axis)


def near_hop(array, axis):
    size = lax.axis_size(axis)
    return lax.ppermute(array, axis, [(i, i ^ 1) for i in range(size)])


def far_hop(array, axis, step):
    size = lax.axis_size(axis)
    return lax.ppermute(array, axis, [(i, (i + 2 * step) % size) for i in range(size)])


def spread(array, rows, axis, hops):
    size = lax.axis_size(axis)
    column = {("img", "far"): 0, ("img", "near"): 1, ("pix", "far"): 2, ("pix", "near"): 3}
    got = [array]
    places = [rows]
    for step in range(1, 2 if hops == "near" else size // 2):
        got.append(near_hop(array, axis) if hops == "near" else far_hop(array, axis, step))
        moved = rows.copy()
        moved[:, column[axis, hops]] += step
        places.append(moved)
    return (jnp.concatenate(got), np.concatenate(places))


ROUTES = (
    (("pix", "near"), ("img", "far"), ("pix", "far")),
    (("img", "far"), ("pix", "far"), ("pix", "near")),
    (("pix", "far"), ("pix", "near"), ("img", "far")),
)


def gather_blocks(low, feats):
    slots_dev = low.shape[0]
    n_pix = lax.axis_size("pix")
    if slots_dev < 4 or n_pix > 8:
        low = lax.all_gather(low, ("img", "pix"), axis=0, tiled=True)
        return ([low], jnp.arange(NBLK), feats)
    quarter = slots_dev // 4
    states = []
    bounds = (0, quarter, 2 * quarter, slots_dev)
    for part in range(3):
        start, stop = bounds[part], bounds[part + 1]
        rows = np.zeros((stop - start, 5), np.int32)
        rows[:, 4] = np.arange(start, stop)
        states.append((low[start:stop], rows))
    for phase in range(3):
        states = [spread(*state, *ROUTES[part][phase]) for part, state in enumerate(states)]
    held, feats = lax.optimization_barrier(([array for array, _ in states], feats))
    arrays = []
    places = []
    for array, (_, rows) in zip(held, states):
        arrays += [array, near_hop(array, "img")]
        mate = rows.copy()
        mate[:, 1] += 1
        places += [rows, mate]
    img_far, img_near, pix_far, pix_near, slot = np.concatenate(places).T
    img = lax.axis_index("img")
    pix = lax.axis_index("pix")
    n_far = lax.axis_size("img") // 2
    img_of = (img // 2 - img_far) % n_far * 2 + (img + img_near) % 2
    pix_of = (pix // 2 - pix_far) % (n_pix // 2) * 2 + (pix + pix_near) % 2
    return (arrays, (img_of * n_pix + pix_of) * slots_dev + slot, feats)


def split_near(array, axis):
    size = lax.axis_size(axis)
    near = lax.axis_index(axis) % 2
    pairs = array.reshape(size // 2, 2, *array.shape[1:])
    return (
        lax.dynamic_index_in_dim(pairs, near, 1, False),
        lax.dynamic_index_in_dim(pairs, 1 - near, 1, False),
    )


def join_near(kept, sent, axis):
    got = near_hop(sent, axis)
    return (kept.astype(jnp.float32) + got.astype(jnp.float32)).astype(jnp.bfloat16)


def own_far(kept, axis):
    return lax.dynamic_index_in_dim(kept, lax.axis_index(axis) // 2, 0, False).astype(jnp.float32)


def from_far_parts(kept, axis, steps):
    size = lax.axis_size(axis)
    parts = []
    for step in steps:
        at = (lax.axis_index(axis) // 2 + step) % (size // 2)
        part = lax.dynamic_index_in_dim(kept, at, 0, False)
        parts.append(far_hop(part, axis, step))
    return parts


def from_far(kept, axis, steps):
    total = 0.0
    for part in from_far_parts(kept, axis, steps):
        total = total + part.astype(jnp.float32)
    return total


def sum_far(kept, axis):
    return own_far(kept, axis) + from_far(kept, axis, range(1, lax.axis_size(axis) // 2))


def gather_far(array, axis):
    size = lax.axis_size(axis)
    far = lax.axis_index(axis) // 2
    got = [array] + [far_hop(array, axis, step) for step in range(1, size // 2)]
    return lax.dynamic_slice_in_dim(jnp.stack(got[::-1] * 2), size // 2 - 1 - far, size // 2, 0)


def gather_near(array, axis):
    near = lax.axis_index(axis) % 2
    other = near_hop(array, axis)
    both = jnp.where(
        near == 0, jnp.stack([array, other], axis=1), jnp.stack([other, array], axis=1)
    )
    return both.reshape(lax.axis_size(axis), *array.shape[1:])


def latent_pass(numerator, denominator, lat_part, cot_rows, lat_gain, w_out, w_up, w_down):
    attended = numerator / denominator[..., None]
    att_low = attended.astype(jnp.bfloat16)
    resid = lat_part[None] + product("mrd,de->mre", att_low, w_out)
    normed, normed_back = jax.vjp(standardize, resid)
    hn_low = (normed * lat_gain).astype(jnp.bfloat16)
    hidden = product("mrd,de->mre", hn_low, w_up)
    active, active_back = jax.vjp(gelu_exact, hidden)
    act_low = active.astype(jnp.bfloat16)
    latents_out = resid + product("mrd,de->mre", act_low, w_down)
    g_mlp = cot_rows.astype(jnp.bfloat16)
    d_active = product("mre,de->mrd", g_mlp, w_down)
    d_hidden = active_back(d_active)[0].astype(jnp.bfloat16)
    d_normed = product("mre,de->mrd", d_hidden, w_up)
    d_resid = cot_rows + normed_back(d_normed * lat_gain)[0]
    d_branch = d_resid.astype(jnp.bfloat16)
    d_attended = product("mre,de->mrd", d_branch, w_out)
    d_numer = d_attended / denominator[..., None]
    d_denom = -jnp.sum(d_attended * numerator / (denominator * denominator)[..., None], axis=-1)
    gain_mlp = jnp.sum(d_normed * normed, axis=(0, 1))
    row_arrays = (att_low, hn_low, act_low, d_branch, d_hidden, g_mlp)
    return (latents_out, d_numer.astype(jnp.bfloat16), d_denom, (row_arrays, gain_mlp))


def shards(
    pixels,
    sides,
    owner,
    master,
    left_stat,
    right_stat,
    left_root,
    right_root,
    kv_weight,
    latent_array,
    in_gain,
    lat_gains,
    cotangent,
):
    micro = pixels.shape[0]
    rows_dev = pixels.shape[2]
    n_pix = lax.axis_size("pix")
    n_img = lax.axis_size("img")
    img = lax.axis_index("img")
    pix = lax.axis_index("pix")
    slots_dev = master.shape[0]
    lat_rows = LAT // n_pix
    row_start = pix * lat_rows
    inv_root = 1.0 / math.sqrt(DL)

    place = jnp.concatenate([(pix * rows_dev)[None], sides * sides]).astype(jnp.int32)
    across = lies_across(pixels)
    gain_column = in_gain[:, None]
    feats = None
    for micro_index in range(micro - 1):
        feats = prepare_pixels(micro_index, feats, place, across, gain_column)
    sources, source_slots, feats = gather_blocks(master.astype(jnp.bfloat16), feats)
    feats, scales = prepare_pixels(micro - 1, feats, place, across, gain_column)
    all_blocks = jnp.arange(NBLK, dtype=jnp.int32)
    source_blocks = jnp.sum(
        jnp.where(source_slots[:, None] == owner[None], all_blocks[None], 0), axis=1
    )
    kv_low = kv_weight.astype(jnp.bfloat16)
    w_key = jnp.pad(kv_low[0], ((0, CEXT - CIN), (0, 0)))
    w_value = kv_low[1]
    lat_low, query, query_cols, w_query, w_out, w_up, w_down = make_query(
        source_blocks.astype(jnp.int32), sources, latent_array, lat_gains[0], w_key
    )

    weights, sums = attend(feats, query_cols)
    sums = sums.reshape(micro, CEXT, n_pix, lat_rows).transpose(2, 1, 0, 3)
    sums = swap(sums.reshape(n_pix, CEXT, micro * lat_rows), "pix")
    sums = jnp.sum(sums.astype(jnp.float32), axis=0)
    numer_in = sums[:CIN]
    denominator = (sums[ONES_ROW] + sums[ONES_ROW + 1]).reshape(micro, lat_rows)
    numerator = fine("cr,cd->rd", numer_in, w_value).reshape(micro, lat_rows, DL)
    latents_out, d_numer, d_denom, latent_grads = latent_pass(
        numerator,
        denominator,
        lax.dynamic_slice_in_dim(latent_array, row_start, lat_rows, 0),
        cotangent[:, 0],
        lat_gains[1],
        w_out,
        w_up,
        w_down,
    )
    row_arrays, gain_mlp = latent_grads
    d_numer = d_numer.reshape(micro * lat_rows, DL)
    head, rest = two_terms(d_denom.reshape(1, micro * lat_rows))
    d_cols = product("rd,cd->cr", d_numer, w_value).astype(jnp.bfloat16)
    d_cols = jnp.concatenate([d_cols, head, rest, jnp.zeros_like(head)], axis=0)
    d_cols = everyone(d_cols, "pix").reshape(n_pix, CEXT, micro, lat_rows)
    d_cols = d_cols.transpose(2, 1, 0, 3).reshape(micro, CEXT, LAT)

    numer_rows = jnp.pad(numer_in.astype(jnp.bfloat16).T, ((0, 0), (0, DL - CIN)))
    own = jnp.stack(
        [array.reshape(micro * lat_rows, DL) for array in row_arrays] + [d_numer, numer_rows]
    )
    mate = [(i, i ^ 1) for i in range(n_img)]
    pieces = [own, lax.ppermute(own, "img", mate)]
    images = [img, img ^ 1]
    far = []
    for step in range(1, n_img // 2):
        hop = [(i, (i + 2 * step) % n_img) for i in range(n_img)]
        far.append(lax.ppermute(own, "img", hop))
        images += [(img - 2 * step) % n_img, (img - 2 * step) % n_img ^ 1]
    device_of = owner // slots_dev
    place_of = device_of % n_pix * slots_dev + owner % slots_dev
    where = jnp.where(device_of // n_pix == img, place_of, -1)

    results = (None,)
    score_sum = jnp.zeros((CEXT, LAT), jnp.float32)
    gain_sum = jnp.zeros((CIN, BLK), jnp.float32)
    width = DL // 2
    each = -(-CEXT // n_pix)
    parts = parts_of(feats)
    for at, part in enumerate(parts):
        if at == len(parts) - 2:
            far, gain_sum = lax.optimization_barrier((far, gain_sum))
            for piece in far:
                pieces += [piece, lax.ppermute(piece, "img", mate)]
        if at == len(parts) - 1:
            pieces, gain_sum = lax.optimization_barrier((pieces, gain_sum))
            where = jnp.concatenate([jnp.stack(images), where]).astype(jnp.int32)
            grads, value_part, resid_part = image_sums(where, pieces, lat_rows)
            value_part = jnp.pad(value_part, ((0, each * n_pix - CEXT), (0, 0)))
            value_part = lax.dynamic_slice_in_dim(value_part, img % 2 * width, width, 1)
            value_sides = split_near(value_part.reshape(n_pix, each, width), "pix")
            grad_sides = split_near(grads.reshape(n_pix, slots_dev, BLK, BLK), "pix")
            value_part = join_near(*value_sides, "pix")
            gain_column, value_part, grad_sides = lax.optimization_barrier(
                (gain_column, value_part, grad_sides)
            )
        results = attend_back(
            part, results[0], scales, feats, weights, gain_column, d_cols, query_cols
        )
        score_sum = score_sum + results[1]
        gain_sum = gain_sum + results[2]
    pixel_grad = jnp.swapaxes(results[0].reshape(micro, 1, CIN, rows_dev), 2, 3)

    gain_sum = jnp.sum(gain_sum, axis=1)[None] / in_gain[None]
    late = jnp.concatenate(
        [
            score_sum[:CIN],
            jnp.pad(gain_sum, ((0, 0), (0, LAT - CIN))),
            gain_mlp.reshape(DL // LAT, LAT),
        ],
        axis=0,
    ).astype(jnp.bfloat16)
    late = jnp.pad(late, ((0, each * n_pix - CEXT), (0, 0))).reshape(n_pix, each, LAT)
    late = jnp.sum(swap(late, "pix").astype(jnp.float32), axis=0)
    value_part = sum_far(value_part, "pix").astype(jnp.bfloat16)
    grads = join_near(*grad_sides, "pix")
    late, value_part, grads = lax.optimization_barrier((late, value_part, grads))
    late = jnp.sum(everyone(late, "img"), axis=0).astype(jnp.bfloat16)
    resid_part = lax.dynamic_slice_in_dim(resid_part, img % 2 * width, width, 1)
    early = gather_far(jnp.concatenate([value_part, resid_part], axis=0), "pix")
    longest = n_pix // 4
    grad_sum = own_far(grads, "pix") + from_far(grads, "pix", (longest,))
    late, early, grad_sum = lax.optimization_barrier((late, early, grad_sum))
    late = everyone(late, "pix").reshape(n_pix * each, LAT)[:CEXT]
    late, grads = lax.optimization_barrier((late, grads))
    others = [step for step in range(1, n_pix // 2) if step != longest]
    grads = from_far_parts(grads, "pix", others)
    early = gather_near(early, "pix")
    value_part = early[:, :each].reshape(n_pix * each, width)[:CEXT]
    early = jnp.concatenate([value_part, early[:, each:].reshape(LAT, width)], axis=0)
    other = near_hop(early, "img")
    d_query, kv_grad, new_kv, latent_grad, new_latent, lat_gain_grad, new_lat_gains = finish(
        (img % 2)[None], late, w_key, query, w_query, early, other, kv_weight, latent_array, lat_gains
    )
    grad_sum, d_query = lax.optimization_barrier((grad_sum, d_query))
    for part in grads:
        grad_sum = grad_sum + part.astype(jnp.float32)
    grads = grad_sum
    in_gain_grad = late[CIN, :CIN].astype(jnp.float32)

    mine = (img * n_pix + pix) * slots_dev + jnp.arange(slots_dev, dtype=jnp.int32)
    blocks = jnp.sum(
        jnp.where(owner[None] == mine[:, None], all_blocks[None], 0), axis=1
    )
    new_left, new_right, new_master, new_copy = update_slots(
        blocks.astype(jnp.int32),
        lat_low,
        d_query,
        grads,
        left_stat,
        right_stat,
        left_root,
        right_root,
        master,
    )
    new_in_gain = in_gain - 0.2 * normalized(in_gain_grad, (0,))
    return (
        latents_out[:, None],
        pixel_grad,
        new_left,
        new_right,
        new_master,
        new_copy,
        kv_grad,
        new_kv,
        latent_grad,
        new_latent,
        in_gain_grad,
        new_in_gain,
        lat_gain_grad,
        new_lat_gains,
    )


def solution(mesh):
    pixel_spec = P(None, "img", "pix", None)
    slot_spec = P(("img", "pix"), None, None)
    in_specs = (
        (pixel_spec, P(), P()) + (slot_spec,) * 5 + (P(),) * 4 + (pixel_spec,)
    )
    out_specs = (pixel_spec, pixel_spec) + (slot_spec,) * 4 + (P(),) * 8
    return jax.shard_map(shards, mesh=mesh, in_specs=in_specs, out_specs=out_specs, check_vma=False)
```
